32 devices in a mesh: row: 4 (over y, x), col: 8 (over z, core).
Axes of the slice: x: 2, y: 2, z: 4, core: 2. Of those that a mesh axis runs over, the one named last changes fastest.
Arguments:
- features: bfloat16 [2, 4, 512, 512], P(None, 'row', 'col'), may hold values from -1 to 1, as said below
- amplitude: float32 [1], replicated, may hold values from 0.5 to 2
- noise: float32 [2, 4, 512], P(None, 'row'), may hold values from 0.1 to 1
Outputs:
- factored: float32 [2, 4, 512, 1, 8, 512], P(None, 'row', None, None, 'col')
The draws below stay inside these ranges and needn't reach their ends.
Inputs may be any that keep to these rules, and one draw needn't show every extreme that they name: `features`: coordinates of points after the length scale.
All inputs are finite; a program needn't handle non-finite values.
Results may differ from the reference program's by a relative error of at most 0.0015.
Values may be sent and summed in bfloat16 or wider, within the bound.
No kernel may reach another device: no remote copies, remote signals or barrier semaphores. Data moves between devices by JAX's collectives and lax.ppermute only.
A program may use at most 128 MiB of HBM per device.

```python
import math
import jax
import jax.numpy as jnp
from jax import lax

F = 512
BLOCK = 512
PANELS = 2
BR = 2
BC = 1
N_ROW = 4
N_COL = 8


def draw_features(key, part):
    first, second, third = jax.random.split(key, 3)
    total = BR * N_ROW * BLOCK
    latent = jax.random.normal(first, (total, 16), jnp.float32)
    mixing = 0.0625 * jax.random.uniform(second, (F,), jnp.float32, 0.7, 1.3)
    choose = jnp.arange(F, dtype=jnp.int32) % 16
    coords = latent[:, choose] * mixing[None, :] + 0.01 * jax.random.normal(third, (total, F), jnp.float32)
    coords = jnp.clip(coords, -1.0, 1.0)
    return coords.reshape(BR, N_ROW, BLOCK, F).astype(jnp.bfloat16)


def block_scale(rng, shape, cuts, low, high):
    gain = 1.0
    for axis_at, parts in cuts:
        draws = jax.random.uniform(jax.random.fold_in(jax.random.fold_in(rng, 6), axis_at), (parts,), jnp.float32, low / len(cuts), high / len(cuts))
        gain = gain * jnp.repeat(jnp.exp(draws), shape[axis_at] // parts).reshape((-1,) + (1,) * (len(shape) - 1 - axis_at))
    return gain


def setup_inputs(seed: int = 0) -> dict:
    streams_of = jax.random.split(jax.random.key(seed), 4)
    features = draw_features(jax.random.fold_in(streams_of[3], 71), 0)
    amplitude = jnp.clip(jnp.exp(jax.random.uniform(streams_of[1], (1,), jnp.float32, math.log(0.5), math.log(2.0))), 0.5, 2.0)
    noise = jnp.clip(jnp.exp(math.log(1.0) - 2.3025851 * jax.random.uniform(streams_of[2], (BR, N_ROW, BLOCK), jnp.float32) ** block_scale(streams_of[2], (BR, N_ROW, BLOCK), ((1, 4),), -0.2, 0.2)), 0.1, 1.0)
    return {"features": features, "amplitude": amplitude, "noise": noise}


def reference(features, amplitude, noise):
    total = BR * N_ROW * BLOCK
    points = features.reshape(total, F)
    sq = jnp.sum(points.astype(jnp.float32) ** 2, axis=1)
    cross = jnp.dot(points.astype(jnp.float32), points.T.astype(jnp.float32), preferred_element_type=jnp.float32)
    dist = sq[:, None] + sq[None, :] - 2.0 * cross
    kern = amplitude[0] * jnp.exp(-0.5 * dist)
    index = jnp.arange(total, dtype=jnp.int32)
    kern = kern.at[index, index].add(noise.reshape(total))
    ident = jnp.eye(BLOCK, dtype=jnp.float32)
    for step in range(PANELS):
        start = step * BLOCK
        stop = start + BLOCK
        lower = jnp.linalg.cholesky(kern[start:stop, start:stop])
        inverse = jax.scipy.linalg.solve_triangular(lower, ident, lower=True)
        below = jnp.dot(kern[stop:, start:stop], inverse.T, precision=lax.Precision.HIGHEST)
        trail = kern[stop:, stop:] - jnp.dot(below, below.T, precision=lax.Precision.HIGHEST)
        kern = kern.at[stop:, stop:].set(trail)
        kern = kern.at[start:stop, stop:].set(jnp.zeros((BLOCK, total - stop), jnp.float32))
        kern = kern.at[:start, start:stop].set(jnp.zeros((start, BLOCK), jnp.float32))
        kern = kern.at[start:, start:stop].set(jnp.concatenate([lower, below], axis=0))
    return kern.reshape(BR, N_ROW, BLOCK, BC, N_COL, BLOCK)
```

```python
import functools

import jax
import jax.numpy as jnp
from jax import lax
from jax.experimental import pallas as pl
from jax.experimental.pallas import tpu as pltpu
from jax.sharding import PartitionSpec as P

PANELS = 2
NB = 128
WB = 256
f32 = jnp.float32
bf16 = jnp.bfloat16
TRANS_B = (((1,), (1,)), ((), ()))
TRANS_A = (((0,), (0,)), ((), ()))


def split(x):
    hi = x.astype(bf16)
    return hi, (x - hi.astype(f32)).astype(bf16)


def dot_nn(ah, al, bh, bl):
    return jnp.dot(
        jnp.concatenate([ah, ah, al], 1), jnp.concatenate([bh, bl, bh], 0), preferred_element_type=f32
    )


def dot_nt(ah, al, bh, bl):
    return lax.dot_general(
        jnp.concatenate([ah, ah, al], 1), jnp.concatenate([bh, bl, bh], 1), TRANS_B, preferred_element_type=f32
    )


def dot_tn(ah, al, bh, bl):
    return lax.dot_general(
        jnp.concatenate([ah, ah, al], 0), jnp.concatenate([bh, bl, bh], 0), TRANS_A, preferred_element_type=f32
    )


def spread(x):
    return jnp.broadcast_to(x, (8, NB))


def tree_sum(xs):
    while len(xs) > 1:
        xs = [xs[i] + xs[i + 1] if i + 1 < len(xs) else xs[i] for i in range(0, len(xs), 2)]
    return xs[0]


def factor_tile(t, rows, cols, lane, sub):
    scaled, ratio, inverses, pivots = [], {}, [], None
    for j in range(8):
        pivot = spread(cols[j][j : j + 1, :])
        inv = 1.0 / pivot
        inverses.append(inv)
        pivots = pivot if j == 0 else jnp.where(sub == j, pivot, pivots)
        below = jnp.where(sub > j, cols[j], 0.0)
        for k in range(j + 1, 8):
            entry = spread(cols[k][j : j + 1, :])
            cols[k] = cols[k] - (below * entry) * inv
            ratio[j, k] = entry * inv
        row = spread(rows[j : j + 1, :]) * inv
        row = jnp.where(lane == 8 * t + j, 1.0 + inv, row)
        scaled.append(row)
        if j < 7:
            rows = rows - below * row
    return rows, lax.rsqrt(pivots), scaled, ratio, inverses


def factor_block(tiles, store_u, store_l):
    tiles = list(tiles)
    n = len(tiles)
    lane = lax.broadcasted_iota(jnp.int32, (8, NB), 1)
    sub = lax.broadcasted_iota(jnp.int32, (8, NB), 0)
    cols = [spread(tiles[0][:, k : k + 1]) for k in range(8)]
    for t in range(n):
        last = t + 1 == n
        if not last:
            near = [spread(tiles[t + 1][:, 8 * t + k : 8 * t + k + 1]) for k in range(8)]
            ahead = [spread(tiles[t + 1][:, 8 * t + 8 + k : 8 * t + 9 + k]) for k in range(8)]
        far = {i: [spread(tiles[i][:, 8 * t + k : 8 * t + k + 1]) for k in range(8)] for i in range(t + 2, n)}
        rows, root, scaled, ratio, inverses = factor_tile(t, tiles[t], cols, lane, sub)
        if not last:
            for j in range(8):
                part = near[j] * inverses[j]
                for k in range(j + 1, 8):
                    near[k] = near[k] - near[j] * ratio[j, k]
                for k in range(8):
                    ahead[k] = ahead[k] - near[j] * spread(part[k : k + 1, :])
                tiles[t + 1] = tiles[t + 1] - near[j] * scaled[j]
            cols = ahead
        back = list(scaled)
        for j in range(6, -1, -1):
            for k in range(7, j, -1):
                back[j] = back[j] - ratio[j, k] * back[k]
        for i in range(t + 2, n):
            tiles[i] = tiles[i] - tree_sum([far[i][j] * back[j] for j in range(8)])
        final = rows * root
        diff = lane - sub - 8 * t
        store_u(t, jnp.where(diff >= 0, final, 0.0))
        store_l(t, jnp.where(diff < 0, final, jnp.where(diff == 0, root, 0.0)))


def half_norm_rows(x):
    xf = x.astype(f32)
    hi, lo = split(xf * xf)
    ones = jnp.ones((8, x.shape[1]), bf16)
    total = lax.dot_general(ones, hi, TRANS_B, preferred_element_type=f32)
    total = total + lax.dot_general(ones, lo, TRANS_B, preferred_element_type=f32)
    return 0.5 * total[0:1]


def half_norm_cols(x):
    xf = x.astype(f32)
    return 0.5 * jnp.sum(xf * xf, axis=1, keepdims=True)


def diagonal(n):
    return lax.broadcasted_iota(jnp.int32, (n, n), 0) == lax.broadcasted_iota(jnp.int32, (n, n), 1)


def place(x_ref, base, piece_at, piece, value):
    at = pl.multiple_of(base + piece_at * piece, piece)
    x_ref[pl.ds(at, piece), :] = value


def chain_kernel(at_ref, amp_ref, mine_ref, other_ref, nz_ref, x_ref, uh_ref, ul_ref, inv_ref, a_ref):
    n = a_ref.shape[0]
    count = n // NB
    steps, panels, piece = mine_ref.shape[:3]
    block = n // panels
    me = at_ref[1]
    for m in range(steps):
        for s in range(panels):
            place(x_ref, s * block, me ^ (2 * m), piece, mine_ref[m, s])
            place(x_ref, s * block, me ^ (2 * m + 1), piece, other_ref[m, s])
    amp = amp_ref[0]
    sq_row = half_norm_rows(x_ref[...])
    for i in range(count):
        o = i * NB
        xi = x_ref[o : o + NB, :]
        cross = lax.dot_general(xi, x_ref[o:, :], TRANS_B, preferred_element_type=f32)
        k = amp * jnp.exp(cross - half_norm_cols(xi) - sq_row[:, o:])
        a_ref[o : o + NB, o:] = k
        shift = jnp.where(diagonal(NB), jnp.broadcast_to(nz_ref[:, o : o + NB], (NB, NB)), 0.0)
        a_ref[o : o + NB, o : o + NB] = k[:, :NB] + shift

    def panel(p, carry):
        o = pl.multiple_of(p * NB, NB)
        d = a_ref[pl.ds(o, NB), pl.ds(o, NB)]

        def store_u(t, v):
            a_ref[pl.ds(pl.multiple_of(o + 8 * t, 8), 8), pl.ds(o, NB)] = v

        def store_l(t, v):
            inv_ref[p, 8 * t : 8 * t + 8, :] = v

        factor_block([d[8 * t : 8 * t + 8] for t in range(NB // 8)], store_u, store_l)
        hi, lo = split(a_ref[pl.ds(o, NB), pl.ds(o, NB)])
        uh_ref[pl.ds(o, NB), pl.ds(o, NB)] = hi
        ul_ref[pl.ds(o, NB), pl.ds(o, NB)] = lo
        for k in range(count - 1):

            @pl.when(p == k)
            def _():
                s = k * NB
                e = s + NB
                u = dot_nn(*split(inv_ref[k]), *split(a_ref[s:e, e:]))
                hi, lo = split(u)
                uh_ref[s:e, e:] = hi
                ul_ref[s:e, e:] = lo
                for i in range(k + 1, count):
                    q = i * NB
                    w = q - e
                    a_ref[q : q + NB, q:] = a_ref[q : q + NB, q:] - dot_tn(
                        hi[:, w : w + NB], lo[:, w : w + NB], hi[:, w:], lo[:, w:]
                    )

        return carry

    lax.fori_loop(0, count, panel, 0)


def bulk_kernel(at_ref, amp_ref, *refs):
    *piece_refs, x_ref, uh_ref, ul_ref, inv_ref, nz_ref, out_ref, f_ref, ph_ref, pl_ref, wh_ref, wl_ref = refs
    n = x_ref.shape[0]
    block = n // PANELS
    piece = piece_refs[0].shape[1]
    nrows = nz_ref.shape[0]
    nblocks = f_ref.shape[0] // block
    ncols = nblocks - nrows
    row_at, me, row_n, col_n = at_ref[0], at_ref[1], at_ref[2], at_ref[3]
    amp = amp_ref[0]
    for k, ref in enumerate(piece_refs):
        for b in range(nblocks):
            place(f_ref, b * block, me ^ k, piece, ref[b])
    for q in range(n // WB):
        first, second = inv_ref[2 * q], inv_ref[2 * q + 1]
        s = q * WB
        corner = dot_tn(
            uh_ref[s : s + NB, s + NB : s + WB], ul_ref[s : s + NB, s + NB : s + WB], *split(first)
        )
        corner = -dot_nn(*split(second), *split(corner))
        zero = jnp.zeros((NB, NB), f32)
        full = jnp.concatenate(
            [jnp.concatenate([first, zero], 1), jnp.concatenate([corner, second], 1)], 0
        )
        wh_ref[q], wl_ref[q] = split(full)
    lead_sq = half_norm_rows(x_ref[...])
    chunk = 256

    def solve(step, carry):
        b = step // (block // chunk)
        number = jnp.where(b < nrows, b * row_n + row_at, (b - nrows) * col_n + me)
        o = pl.multiple_of(step * chunk, chunk)

        @pl.when(number >= PANELS)
        def _():
            xb = f_ref[pl.ds(o, chunk), :]
            sq = half_norm_cols(xb)
            for q in range(n // WB):
                s = q * WB
                cross = lax.dot_general(xb, x_ref[s : s + WB, :], TRANS_B, preferred_element_type=f32)
                acc = amp * jnp.exp(cross - sq - lead_sq[:, s : s + WB])
                if q:
                    acc = acc - dot_nn(
                        ph_ref[pl.ds(o, chunk), 0:s],
                        pl_ref[pl.ds(o, chunk), 0:s],
                        uh_ref[0:s, s : s + WB],
                        ul_ref[0:s, s : s + WB],
                    )
                hi, lo = split(dot_nt(*split(acc), wh_ref[q], wl_ref[q]))
                ph_ref[pl.ds(o, chunk), s : s + WB] = hi
                pl_ref[pl.ds(o, chunk), s : s + WB] = lo

        return carry

    lax.fori_loop(0, nblocks * (block // chunk), solve, 0)
    for b in range(ncols):
        j = b * col_n + me
        fo = (nrows + b) * block
        xc = f_ref[fo : fo + block, :]
        col_sq = half_norm_rows(xc)
        for a in range(nrows):
            i = a * row_n + row_at

            @pl.when((i >= PANELS) & (j >= PANELS))
            def _():
                for h in range(block // chunk):
                    o = a * block + h * chunk
                    xr = f_ref[o : o + chunk, :]
                    cross = lax.dot_general(xr, xc, TRANS_B, preferred_element_type=f32)
                    k = amp * jnp.exp(cross - half_norm_cols(xr) - col_sq)
                    row_id = lax.broadcasted_iota(jnp.int32, (chunk, block), 0) + h * chunk
                    col_id = lax.broadcasted_iota(jnp.int32, (chunk, block), 1)
                    on_diag = (row_id == col_id) & (i == j)
                    k = k + jnp.where(on_diag, jnp.broadcast_to(nz_ref[a : a + 1, :], (chunk, block)), 0.0)
                    out_ref[o : o + chunk, b * block : (b + 1) * block] = k - dot_nt(
                        ph_ref[o : o + chunk, :],
                        pl_ref[o : o + chunk, :],
                        ph_ref[fo : fo + block, :],
                        pl_ref[fo : fo + block, :],
                    )

            @pl.when((i >= PANELS) & (j < PANELS))
            def _():
                w = pl.multiple_of(j * block, block)
                rows = slice(a * block, (a + 1) * block)
                out_ref[rows, b * block : (b + 1) * block] = ph_ref[rows, pl.ds(w, block)].astype(f32) + pl_ref[
                    rows, pl.ds(w, block)
                ].astype(f32)

            @pl.when((i < PANELS) & (j > i))
            def _():
                out_ref[a * block : (a + 1) * block, b * block : (b + 1) * block] = jnp.zeros((block, block), f32)

            @pl.when((i < PANELS) & (j <= i))
            def _():
                v = pl.multiple_of(j * block, block)
                w = pl.multiple_of(i * block, block)
                u = uh_ref[pl.ds(v, block), pl.ds(w, block)].astype(f32)
                u = u + ul_ref[pl.ds(v, block), pl.ds(w, block)].astype(f32)
                row_id = lax.broadcasted_iota(jnp.int32, (block, block), 0)
                col_id = lax.broadcasted_iota(jnp.int32, (block, block), 1)
                keep = (row_id >= col_id) | (j < i)
                out_ref[a * block : (a + 1) * block, b * block : (b + 1) * block] = jnp.where(keep, u.T, 0.0)


SMEM = pl.BlockSpec(memory_space=pltpu.SMEM)
VMEM = pl.BlockSpec(memory_space=pltpu.VMEM)


def exchange(x, axis, k):
    return lax.ppermute(x, axis, [(i, i ^ k) for i in range(lax.axis_size(axis))])


def local(features, amplitude, noise):
    row_n = lax.axis_size("row")
    col_n = lax.axis_size("col")
    row_at = lax.axis_index("row")
    col_at = lax.axis_index("col")
    nrows, _, piece, width = features.shape
    block = piece * col_n
    ncols = nrows * row_n // col_n
    n = PANELS * block
    mine = features.reshape(nrows, piece, width)
    noise_rows = noise.reshape(nrows, block)
    lead_noise = lax.all_gather(noise_rows[0], "row")[:PANELS].reshape(1, n)
    plane = jnp.stack([mine] + [exchange(mine, "row", k) for k in range(1, row_n)])
    lead = jnp.stack(
        [lax.dynamic_index_in_dim(plane[:, 0], row_at ^ s, 0, keepdims=False) for s in range(PANELS)]
    )
    near = jnp.stack([lead] + [exchange(lead, "col", k) for k in range(2, col_n, 2)])
    other = exchange(near, "col", 1)
    near, other, plane, mine = lax.optimization_barrier((near, other, plane, mine))

    def for_col(to):
        out = [mine]
        for b in range(ncols):
            number = b * col_n + to
            out.append(
                lax.dynamic_slice(
                    plane, (row_at ^ (number % row_n), number // row_n, 0, 0), (1, 1, piece, width)
                ).reshape(1, piece, width)
            )
        return jnp.concatenate(out, 0)

    pieces = [for_col(col_at)] + [exchange(for_col(col_at ^ k), "col", k) for k in range(1, col_n)]
    at = jnp.stack([row_at, col_at, jnp.int32(row_n), jnp.int32(col_n)])
    half = jax.ShapeDtypeStruct((n, n), bf16)
    points, uh, ul, inverse = pl.pallas_call(
        chain_kernel,
        out_shape=[
            jax.ShapeDtypeStruct((n, width), bf16),
            half,
            half,
            jax.ShapeDtypeStruct((n // NB, NB, NB), f32),
        ],
        in_specs=[SMEM, SMEM, VMEM, VMEM, VMEM],
        out_specs=[VMEM] * 4,
        scratch_shapes=[pltpu.VMEM((n, n), f32)],
        compiler_params=pltpu.CompilerParams(vmem_limit_bytes=40 << 20),
        cost_estimate=pl.CostEstimate(flops=40_000_000_000, bytes_accessed=8_000_000, transcendentals=0),
        name="chain",
    )(at, amplitude, near, other, lead_noise)
    nblocks = nrows + ncols
    out = pl.pallas_call(
        bulk_kernel,
        out_shape=jax.ShapeDtypeStruct((nrows * block, ncols * block), f32),
        in_specs=[SMEM, SMEM] + [VMEM] * (len(pieces) + 5),
        out_specs=VMEM,
        scratch_shapes=[
            pltpu.VMEM((nblocks * block, width), bf16),
            pltpu.VMEM((nblocks * block, n), bf16),
            pltpu.VMEM((nblocks * block, n), bf16),
            pltpu.VMEM((n // WB, WB, WB), bf16),
            pltpu.VMEM((n // WB, WB, WB), bf16),
        ],
        compiler_params=pltpu.CompilerParams(vmem_limit_bytes=56 << 20),
        cost_estimate=pl.CostEstimate(flops=12_000_000_000, bytes_accessed=8_000_000, transcendentals=0),
        name="bulk",
    )(at, amplitude, *pieces, points, uh, ul, inverse, noise_rows)
    return out.reshape(nrows, 1, block, ncols, 1, block)


def solution(mesh):
    return jax.shard_map(
        local,
        mesh=mesh,
        in_specs=(P(None, "row", "col", None), P(), P(None, "row", None)),
        out_specs=P(None, "row", None, None, "col", None),
        check_vma=False,
    )
```

```python
import functools

import jax
import jax.numpy as jnp
from jax import lax
from jax.experimental import pallas as pl
from jax.experimental.pallas import tpu as pltpu
from jax.sharding import PartitionSpec as P

PANELS = 2
NB = 128
WB = 256
f32 = jnp.float32
bf16 = jnp.bfloat16
TRANS_B = (((1,), (1,)), ((), ()))
TRANS_A = (((0,), (0,)), ((), ()))


def split(x):
    hi = x.astype(bf16)
    return hi, (x - hi.astype(f32)).astype(bf16)


def dot_nn(ah, al, bh, bl):
    return jnp.dot(
        jnp.concatenate([ah, ah, al], 1), jnp.concatenate([bh, bl, bh], 0), preferred_element_type=f32
    )


def dot_nt(ah, al, bh, bl):
    return lax.dot_general(
        jnp.concatenate([ah, ah, al], 1), jnp.concatenate([bh, bl, bh], 1), TRANS_B, preferred_element_type=f32
    )


def dot_tn(ah, al, bh, bl):
    return lax.dot_general(
        jnp.concatenate([ah, ah, al], 0), jnp.concatenate([bh, bl, bh], 0), TRANS_A, preferred_element_type=f32
    )


def spread(x):
    return jnp.broadcast_to(x, (8, NB))


def tree_sum(xs):
    while len(xs) > 1:
        xs = [xs[i] + xs[i + 1] if i + 1 < len(xs) else xs[i] for i in range(0, len(xs), 2)]
    return xs[0]


def factor_tile(t, rows, cols, lane, sub):
    scaled, ratio, inverses, pivots = [], {}, [], None
    for j in range(8):
        pivot = spread(cols[j][j : j + 1, :])
        inv = 1.0 / pivot
        inverses.append(inv)
        pivots = pivot if j == 0 else jnp.where(sub == j, pivot, pivots)
        below = jnp.where(sub > j, cols[j], 0.0)
        for k in range(j + 1, 8):
            entry = spread(cols[k][j : j + 1, :])
            cols[k] = cols[k] - (below * entry) * inv
            ratio[j, k] = entry * inv
        row = spread(rows[j : j + 1, :]) * inv
        row = jnp.where(lane == 8 * t + j, 1.0 + inv, row)
        scaled.append(row)
        if j < 7:
            rows = rows - below * row
    return rows, lax.rsqrt(pivots), scaled, ratio, inverses


def factor_block(tiles, store_u, store_l):
    tiles = list(tiles)
    n = len(tiles)
    lane = lax.broadcasted_iota(jnp.int32, (8, NB), 1)
    sub = lax.broadcasted_iota(jnp.int32, (8, NB), 0)
    cols = [spread(tiles[0][:, k : k + 1]) for k in range(8)]
    for t in range(n):
        last = t + 1 == n
        if not last:
            near = [spread(tiles[t + 1][:, 8 * t + k : 8 * t + k + 1]) for k in range(8)]
            ahead = [spread(tiles[t + 1][:, 8 * t + 8 + k : 8 * t + 9 + k]) for k in range(8)]
        far = {i: [spread(tiles[i][:, 8 * t + k : 8 * t + k + 1]) for k in range(8)] for i in range(t + 2, n)}
        rows, root, scaled, ratio, inverses = factor_tile(t, tiles[t], cols, lane, sub)
        if not last:
            for j in range(8):
                part = near[j] * inverses[j]
                for k in range(j + 1, 8):
                    near[k] = near[k] - near[j] * ratio[j, k]
                for k in range(8):
                    ahead[k] = ahead[k] - near[j] * spread(part[k : k + 1, :])
                tiles[t + 1] = tiles[t + 1] - near[j] * scaled[j]
            cols = ahead
        back = list(scaled)
        for j in range(6, -1, -1):
            for k in range(7, j, -1):
                back[j] = back[j] - ratio[j, k] * back[k]
        for i in range(t + 2, n):
            tiles[i] = tiles[i] - tree_sum([far[i][j] * back[j] for j in range(8)])
        final = rows * root
        diff = lane - sub - 8 * t
        store_u(t, jnp.where(diff >= 0, final, 0.0))
        store_l(t, jnp.where(diff < 0, final, jnp.where(diff == 0, root, 0.0)))


def half_norm_rows(x):
    xf = x.astype(f32)
    hi, lo = split(xf * xf)
    ones = jnp.ones((8, x.shape[1]), bf16)
    total = lax.dot_general(ones, hi, TRANS_B, preferred_element_type=f32)
    total = total + lax.dot_general(ones, lo, TRANS_B, preferred_element_type=f32)
    return 0.5 * total[0:1]


def half_norm_cols(x, width):
    xf = x.astype(f32)
    hi, lo = split(xf * xf)
    ones = jnp.ones((NB, x.shape[1]), bf16)
    total = lax.dot_general(hi, ones, TRANS_B, preferred_element_type=f32)
    total = 0.5 * (total + lax.dot_general(lo, ones, TRANS_B, preferred_element_type=f32))
    return jnp.concatenate([total] * (width // NB), 1)


def diagonal(n):
    return lax.broadcasted_iota(jnp.int32, (n, n), 0) == lax.broadcasted_iota(jnp.int32, (n, n), 1)


def place(x_ref, base, piece_at, piece, value):
    at = pl.multiple_of(base + piece_at * piece, piece)
    x_ref[pl.ds(at, piece), :] = value


def factor_panels(a_ref, uh_ref, ul_ref, inv_ref, count, width):
    def panel(p, carry):
        o = pl.multiple_of(p * NB, NB)
        d = a_ref[pl.ds(o, NB), pl.ds(o, NB)]

        def store_u(t, v):
            a_ref[pl.ds(pl.multiple_of(o + 8 * t, 8), 8), pl.ds(o, NB)] = v

        def store_l(t, v):
            inv_ref[p, 8 * t : 8 * t + 8, :] = v

        factor_block([d[8 * t : 8 * t + 8] for t in range(NB // 8)], store_u, store_l)
        hi, lo = split(a_ref[pl.ds(o, NB), pl.ds(o, NB)])
        uh_ref[pl.ds(o, NB), pl.ds(o, NB)] = hi
        ul_ref[pl.ds(o, NB), pl.ds(o, NB)] = lo
        for k in range(min(count, width // NB - 1)):

            @pl.when(p == k)
            def _():
                s = k * NB
                e = s + NB
                u = dot_nn(*split(inv_ref[k]), *split(a_ref[s:e, e:]))
                hi, lo = split(u)
                uh_ref[s:e, e:] = hi
                ul_ref[s:e, e:] = lo
                for i in range(k + 1, width // NB):
                    q = i * NB
                    w = q - e
                    a_ref[q : q + NB, q:] = a_ref[q : q + NB, q:] - dot_tn(
                        hi[:, w : w + NB], lo[:, w : w + NB], hi[:, w:], lo[:, w:]
                    )

        return carry

    lax.fori_loop(0, count, panel, 0)


def first_kernel(at_ref, amp_ref, mine_ref, other_ref, nz_ref, x_ref, uh_ref, ul_ref, inv_ref, rest_ref, a_ref):
    n = a_ref.shape[0]
    steps, panels, piece = mine_ref.shape[:3]
    block = n // panels
    me = at_ref[1]
    for m in range(steps):
        for s in range(panels):
            place(x_ref, s * block, me ^ (2 * m), piece, mine_ref[m, s])
            place(x_ref, s * block, me ^ (2 * m + 1), piece, other_ref[m, s])
    amp = amp_ref[0]
    sq_row = half_norm_rows(x_ref[...])
    halves = nz_ref[...].astype(f32)
    noise = halves[:, 0] + halves[:, 1] + halves[:, 2]
    for i in range(n // NB):
        o = i * NB
        xi = x_ref[o : o + NB, :]
        cross = lax.dot_general(xi, x_ref[o:, :], TRANS_B, preferred_element_type=f32)
        k = amp * jnp.exp(cross - half_norm_cols(xi, n - o) - sq_row[:, o:])
        a_ref[o : o + NB, o:] = k
        row = noise[o // block : o // block + 1, o % block : o % block + NB]
        a_ref[o : o + NB, o : o + NB] = k[:, :NB] + jnp.where(diagonal(NB), jnp.broadcast_to(row, (NB, NB)), 0.0)
    first = inv_ref.shape[0]
    factor_panels(a_ref, uh_ref, ul_ref, inv_ref, first, n)
    rest_ref[...] = a_ref[first * NB :, first * NB :]


def second_kernel(rest_ref, uh_ref, ul_ref, inv_ref, a_ref):
    a_ref[...] = rest_ref[...]
    factor_panels(a_ref, uh_ref, ul_ref, inv_ref, inv_ref.shape[0], a_ref.shape[1])


def store_block(out_ref, a, b, row, ncols, value):
    rows, block = value.shape
    per = block // NB
    for q in range(per):
        at = ((a * block + row) * ncols + b) * per + q
        out_ref[pl.ds(at, rows, stride=ncols * per), :] = value[:, q * NB : (q + 1) * NB]


def bulk_kernel(at_ref, amp_ref, *refs):
    (rows_ref, mine_ref, other_ref, x_ref, uh0_ref, ul0_ref, inv0_ref, uh1_ref, ul1_ref, inv1_ref, nz_ref) = refs[:11]
    out_ref, c_ref, ph_ref, pl_ref, wh_ref, wl_ref = refs[11:]
    n = x_ref.shape[0]
    split_at = uh0_ref.shape[0]
    steps, _, _, piece = mine_ref.shape[:4]
    nrows, block, _ = rows_ref.shape
    ncols = c_ref.shape[0] // block
    row_at, me, row_n, col_n = at_ref[0], at_ref[1], at_ref[2], at_ref[3]
    core = me & 1
    amp = amp_ref[0]
    for m in range(steps):
        for b in range(ncols):
            place(c_ref, b * block, me ^ (2 * m), piece, mine_ref[m, core, b])
            place(c_ref, b * block, me ^ (2 * m + 1), piece, other_ref[m, b])

    def upper(r0, r1, c0, c1):
        parts = []
        if r0 < split_at:
            r = min(r1, split_at)
            parts.append((uh0_ref[r0:r, c0:c1], ul0_ref[r0:r, c0:c1]))
        if r1 > split_at:
            r = max(r0, split_at)
            d = split_at
            parts.append((uh1_ref[r - d : r1 - d, c0 - d : c1 - d], ul1_ref[r - d : r1 - d, c0 - d : c1 - d]))
        return tuple(jnp.concatenate([p[h] for p in parts], 0) if len(parts) > 1 else parts[0][h] for h in (0, 1))

    def inverse(k):
        d = split_at // NB
        return inv0_ref[k] if k < d else inv1_ref[k - d]

    for q in range(n // WB):
        top, low = inverse(2 * q), inverse(2 * q + 1)
        s = q * WB
        corner = dot_tn(*upper(s, s + NB, s + NB, s + WB), *split(top))
        corner = -dot_nn(*split(low), *split(corner))
        zero = jnp.zeros((NB, NB), f32)
        full = jnp.concatenate([jnp.concatenate([top, zero], 1), jnp.concatenate([corner, low], 1)], 0)
        wh_ref[q], wl_ref[q] = split(full)
    lead_sq = half_norm_rows(x_ref[...])
    chunk = 256

    def solve(xb, o):
        sq = half_norm_cols(xb, WB)
        for q in range(n // WB):
            s = q * WB
            cross = lax.dot_general(xb, x_ref[s : s + WB, :], TRANS_B, preferred_element_type=f32)
            acc = amp * jnp.exp(cross - sq - lead_sq[:, s : s + WB])
            if q:
                acc = acc - dot_nn(
                    ph_ref[pl.ds(o, chunk), 0:s], pl_ref[pl.ds(o, chunk), 0:s], *upper(0, s, s, s + WB)
                )
            hi, lo = split(dot_nt(*split(acc), wh_ref[q], wl_ref[q]))
            ph_ref[pl.ds(o, chunk), s : s + WB] = hi
            pl_ref[pl.ds(o, chunk), s : s + WB] = lo

    parts = block // chunk

    def solve_rows(step, carry):
        a = step // parts

        @pl.when(a * row_n + row_at >= PANELS)
        def _():
            h = pl.multiple_of((step % parts) * chunk, chunk)
            solve(rows_ref[a, pl.ds(h, chunk), :], pl.multiple_of(step * chunk, chunk))

        return carry

    def solve_cols(step, carry):
        @pl.when((step // parts) * col_n + me >= PANELS)
        def _():
            h = pl.multiple_of(step * chunk, chunk)
            solve(c_ref[pl.ds(h, chunk), :], pl.multiple_of(nrows * block + step * chunk, chunk))

        return carry

    lax.fori_loop(0, nrows * parts, solve_rows, 0)
    lax.fori_loop(0, ncols * parts, solve_cols, 0)
    for b in range(ncols):
        j = b * col_n + me
        fo = (nrows + b) * block
        xc = c_ref[b * block : (b + 1) * block, :]
        col_sq = half_norm_rows(xc)
        for a in range(nrows):
            i = a * row_n + row_at

            @pl.when((i >= PANELS) & (j >= PANELS))
            def _():
                for h in range(0, block, chunk):
                    o = a * block + h
                    xr = rows_ref[a, h : h + chunk, :]
                    cross = lax.dot_general(xr, xc, TRANS_B, preferred_element_type=f32)
                    k = amp * jnp.exp(cross - half_norm_cols(xr, block) - col_sq)
                    row_id = lax.broadcasted_iota(jnp.int32, (chunk, block), 0) + h
                    col_id = lax.broadcasted_iota(jnp.int32, (chunk, block), 1)
                    on_diag = (row_id == col_id) & (i == j)
                    k = k + jnp.where(on_diag, jnp.broadcast_to(nz_ref[a : a + 1, :], (chunk, block)), 0.0)
                    k = k - dot_nt(
                        ph_ref[o : o + chunk, :],
                        pl_ref[o : o + chunk, :],
                        ph_ref[fo : fo + block, :],
                        pl_ref[fo : fo + block, :],
                    )
                    store_block(out_ref, a, b, h, ncols, k)

            for s in range(PANELS):
                w = s * block

                @pl.when((i >= PANELS) & (j == s))
                def _():
                    rows = slice(a * block, (a + 1) * block)
                    hi, lo = ph_ref[rows, w : w + block], pl_ref[rows, w : w + block]
                    store_block(out_ref, a, b, 0, ncols, hi.astype(f32) + lo.astype(f32))

                @pl.when((i == s) & (j > s))
                def _():
                    store_block(out_ref, a, b, 0, ncols, jnp.zeros((block, block), f32))

                for v in range(s + 1):

                    @pl.when((i == s) & (j == v))
                    def _():
                        hi, lo = upper(v * block, (v + 1) * block, w, w + block)
                        u = (hi.astype(f32) + lo.astype(f32)).T
                        if v == s:
                            row_id = lax.broadcasted_iota(jnp.int32, (block, block), 0)
                            col_id = lax.broadcasted_iota(jnp.int32, (block, block), 1)
                            u = jnp.where(row_id >= col_id, u, 0.0)
                        store_block(out_ref, a, b, 0, ncols, u)


SMEM = pl.BlockSpec(memory_space=pltpu.SMEM)
VMEM = pl.BlockSpec(memory_space=pltpu.VMEM)


def exchange(x, axis, k):
    return lax.ppermute(x, axis, [(i, i ^ k) for i in range(lax.axis_size(axis))])


def choose(index, options):
    out = options[0]
    for k in range(1, len(options)):
        out = jnp.where(index == k, options[k], out)
    return out


def split3(x):
    hi, rest = x.astype(bf16), x
    rest = x - lax.reduce_precision(x, 8, 7)
    mid = rest.astype(bf16)
    low = (rest - lax.reduce_precision(rest, 8, 7)).astype(bf16)
    return jnp.stack([hi, mid, low])


def local(features, amplitude, noise):
    row_n = lax.axis_size("row")
    col_n = lax.axis_size("col")
    row_at = lax.axis_index("row")
    col_at = lax.axis_index("col")
    nrows, _, piece, width = features.shape
    block = piece * col_n
    ncols = nrows * row_n // col_n
    n = PANELS * block
    mine = features.reshape(nrows, piece, width)
    noise_rows = noise.reshape(nrows, block)
    rows = lax.all_gather(mine, "col", axis=1, tiled=True)
    extra = split3(noise_rows[0]).reshape(-1, width)
    extra = jnp.pad(extra, ((0, -extra.shape[0] % 16), (0, 0)))
    parcel = jnp.concatenate([mine.reshape(-1, width), extra], 0)
    plane = [parcel] + [exchange(parcel, "row", k) for k in range(1, row_n)]
    lead = jnp.stack([choose(row_at ^ s, [p[:piece] for p in plane]) for s in range(PANELS)])
    lead_noise = jnp.stack([choose(row_at ^ s, [p[nrows * piece :] for p in plane]) for s in range(PANELS)])
    lead_noise = lead_noise[:, : 3 * block // width].reshape(PANELS, 3, block)
    near = jnp.stack([lead] + [exchange(lead, "col", k) for k in range(2, col_n, 2)])
    other = exchange(near, "col", 1)
    near, other, everything = lax.optimization_barrier((near, other, jnp.stack(plane)))

    def for_chip(to):
        out = []
        for core in range(2):
            for b in range(ncols):
                number = b * col_n + (to & ~1) + core
                out.append(
                    lax.dynamic_slice(
                        everything, (row_at ^ (number % row_n), (number // row_n) * piece, 0), (1, piece, width)
                    )
                )
        return jnp.concatenate(out, 0).reshape(2, ncols, piece, width)

    cols_near = [for_chip(col_at)] + [exchange(for_chip(col_at ^ k), "col", k) for k in range(2, col_n, 2)]
    at = jnp.stack([row_at, col_at, jnp.int32(row_n), jnp.int32(col_n)])
    first = n // NB // 2
    n1 = n - first * NB
    points, uh0, ul0, inv0, rest = pl.pallas_call(
        first_kernel,
        out_shape=[
            jax.ShapeDtypeStruct((n, width), bf16),
            jax.ShapeDtypeStruct((first * NB, n), bf16),
            jax.ShapeDtypeStruct((first * NB, n), bf16),
            jax.ShapeDtypeStruct((first, NB, NB), f32),
            jax.ShapeDtypeStruct((n1, n1), f32),
        ],
        in_specs=[SMEM, SMEM, VMEM, VMEM, VMEM],
        out_specs=[VMEM] * 5,
        scratch_shapes=[pltpu.VMEM((n, n), f32)],
        compiler_params=pltpu.CompilerParams(vmem_limit_bytes=20 << 20),
        cost_estimate=pl.CostEstimate(flops=20_000_000_000, bytes_accessed=8_000_000, transcendentals=0),
        name="first",
    )(at, amplitude, near, other, lead_noise)
    cols_near = jnp.stack(cols_near)
    cols_near, rest = lax.optimization_barrier((cols_near, rest))
    core = col_at & 1
    cols_other = exchange(lax.dynamic_index_in_dim(cols_near, 1 - core, 1, keepdims=False), "col", 1)
    uh1, ul1, inv1 = pl.pallas_call(
        second_kernel,
        out_shape=[
            jax.ShapeDtypeStruct((n1, n1), bf16),
            jax.ShapeDtypeStruct((n1, n1), bf16),
            jax.ShapeDtypeStruct((n1 // NB, NB, NB), f32),
        ],
        in_specs=[VMEM],
        out_specs=[VMEM] * 3,
        scratch_shapes=[pltpu.VMEM((n1, n1), f32)],
        compiler_params=pltpu.CompilerParams(vmem_limit_bytes=20 << 20),
        cost_estimate=pl.CostEstimate(flops=20_000_000_000, bytes_accessed=8_000_000, transcendentals=0),
        name="second",
    )(rest)
    out = pl.pallas_call(
        bulk_kernel,
        out_shape=jax.ShapeDtypeStruct((nrows * block * ncols * (block // NB), NB), f32),
        in_specs=[SMEM, SMEM] + [VMEM] * 11,
        out_specs=VMEM,
        scratch_shapes=[
            pltpu.VMEM((ncols * block, width), bf16),
            pltpu.VMEM(((nrows + ncols) * block, n), bf16),
            pltpu.VMEM(((nrows + ncols) * block, n), bf16),
            pltpu.VMEM((n // WB, WB, WB), bf16),
            pltpu.VMEM((n // WB, WB, WB), bf16),
        ],
        compiler_params=pltpu.CompilerParams(vmem_limit_bytes=36 << 20),
        cost_estimate=pl.CostEstimate(flops=12_000_000_000, bytes_accessed=8_000_000, transcendentals=0),
        name="bulk",
    )(at, amplitude, rows, cols_near, cols_other, points, uh0, ul0, inv0, uh1, ul1, inv1, noise_rows)
    return out.reshape(nrows, 1, block, ncols, 1, block)


def solution(mesh):
    return jax.shard_map(
        local,
        mesh=mesh,
        in_specs=(P(None, "row", "col", None), P(), P(None, "row", None)),
        out_specs=P(None, "row", None, None, "col", None),
        check_vma=False,
    )
```

```python
import functools

import jax
import jax.numpy as jnp
from jax import lax
from jax.experimental import pallas as pl
from jax.experimental.pallas import tpu as pltpu
from jax.sharding import PartitionSpec as P

PANELS = 2
NB = 128
WB = 256
GRANT = 32 << 20
f32 = jnp.float32
bf16 = jnp.bfloat16
TRANS_B = (((1,), (1,)), ((), ()))
TRANS_A = (((0,), (0,)), ((), ()))


def split(x):
    hi = x.astype(bf16)
    return hi, (x - hi.astype(f32)).astype(bf16)


def dot_nn(ah, al, bh, bl):
    return jnp.dot(
        jnp.concatenate([ah, ah, al], 1), jnp.concatenate([bh, bl, bh], 0), preferred_element_type=f32
    )


def dot_nt(ah, al, bh, bl):
    return lax.dot_general(
        jnp.concatenate([ah, ah, al], 1), jnp.concatenate([bh, bl, bh], 1), TRANS_B, preferred_element_type=f32
    )


def dot_tn(ah, al, bh, bl):
    return lax.dot_general(
        jnp.concatenate([ah, ah, al], 0), jnp.concatenate([bh, bl, bh], 0), TRANS_A, preferred_element_type=f32
    )


def spread(x):
    return jnp.broadcast_to(x, (8, NB))


def tree_sum(xs):
    while len(xs) > 1:
        xs = [xs[i] + xs[i + 1] if i + 1 < len(xs) else xs[i] for i in range(0, len(xs), 2)]
    return xs[0]


def factor_tile(t, rows, cols, lane, sub):
    scaled, ratio, inverses, pivots = [], {}, [], None
    for j in range(8):
        pivot = spread(cols[j][j : j + 1, :])
        inv = 1.0 / pivot
        inverses.append(inv)
        pivots = pivot if j == 0 else jnp.where(sub == j, pivot, pivots)
        below = jnp.where(sub > j, cols[j], 0.0)
        for k in range(j + 1, 8):
            entry = spread(cols[k][j : j + 1, :])
            cols[k] = cols[k] - (below * entry) * inv
            ratio[j, k] = entry * inv
        row = spread(rows[j : j + 1, :]) * inv
        row = jnp.where(lane == 8 * t + j, 1.0 + inv, row)
        scaled.append(row)
        if j < 7:
            rows = rows - below * row
    return rows, lax.rsqrt(pivots), scaled, ratio, inverses


def factor_block(tiles, store_u, store_l):
    tiles = list(tiles)
    n = len(tiles)
    lane = lax.broadcasted_iota(jnp.int32, (8, NB), 1)
    sub = lax.broadcasted_iota(jnp.int32, (8, NB), 0)
    cols = [spread(tiles[0][:, k : k + 1]) for k in range(8)]
    for t in range(n):
        last = t + 1 == n
        if not last:
            near = [spread(tiles[t + 1][:, 8 * t + k : 8 * t + k + 1]) for k in range(8)]
            ahead = [spread(tiles[t + 1][:, 8 * t + 8 + k : 8 * t + 9 + k]) for k in range(8)]
        far = {i: [spread(tiles[i][:, 8 * t + k : 8 * t + k + 1]) for k in range(8)] for i in range(t + 2, n)}
        rows, root, scaled, ratio, inverses = factor_tile(t, tiles[t], cols, lane, sub)
        if not last:
            for j in range(8):
                part = near[j] * inverses[j]
                for k in range(j + 1, 8):
                    near[k] = near[k] - near[j] * ratio[j, k]
                for k in range(8):
                    ahead[k] = ahead[k] - near[j] * spread(part[k : k + 1, :])
                tiles[t + 1] = tiles[t + 1] - near[j] * scaled[j]
            cols = ahead
        back = list(scaled)
        for j in range(6, -1, -1):
            for k in range(7, j, -1):
                back[j] = back[j] - ratio[j, k] * back[k]
        for i in range(t + 2, n):
            tiles[i] = tiles[i] - tree_sum([far[i][j] * back[j] for j in range(8)])
        final = rows * root
        diff = lane - sub - 8 * t
        store_u(t, jnp.where(diff >= 0, final, 0.0))
        store_l(t, jnp.where(diff < 0, final, jnp.where(diff == 0, root, 0.0)))


def half_norm_rows(x):
    xf = x.astype(f32)
    hi, lo = split(xf * xf)
    ones = jnp.ones((8, x.shape[1]), bf16)
    total = lax.dot_general(ones, hi, TRANS_B, preferred_element_type=f32)
    total = total + lax.dot_general(ones, lo, TRANS_B, preferred_element_type=f32)
    return 0.5 * total[0:1]


def half_norm_cols(x, width):
    xf = x.astype(f32)
    hi, lo = split(xf * xf)
    ones = jnp.ones((NB, x.shape[1]), bf16)
    total = lax.dot_general(hi, ones, TRANS_B, preferred_element_type=f32)
    total = 0.5 * (total + lax.dot_general(lo, ones, TRANS_B, preferred_element_type=f32))
    return jnp.concatenate([total] * (width // NB), 1)


def diagonal(n):
    return lax.broadcasted_iota(jnp.int32, (n, n), 0) == lax.broadcasted_iota(jnp.int32, (n, n), 1)


def place(x_ref, base, piece_at, piece, value):
    at = pl.multiple_of(base + piece_at * piece, piece)
    x_ref[pl.ds(at, piece), :] = value


def factor_panels(a_ref, uh_ref, ul_ref, inv_ref, count, width):
    def panel(p, carry):
        o = pl.multiple_of(p * NB, NB)
        d = a_ref[pl.ds(o, NB), pl.ds(o, NB)]

        def store_u(t, v):
            a_ref[pl.ds(pl.multiple_of(o + 8 * t, 8), 8), pl.ds(o, NB)] = v

        def store_l(t, v):
            inv_ref[p, 8 * t : 8 * t + 8, :] = v

        factor_block([d[8 * t : 8 * t + 8] for t in range(NB // 8)], store_u, store_l)
        hi, lo = split(a_ref[pl.ds(o, NB), pl.ds(o, NB)])
        uh_ref[pl.ds(o, NB), pl.ds(o, NB)] = hi
        ul_ref[pl.ds(o, NB), pl.ds(o, NB)] = lo
        for k in range(min(count, width // NB - 1)):

            @pl.when(p == k)
            def _():
                s = k * NB
                e = s + NB
                u = dot_nn(*split(inv_ref[k]), *split(a_ref[s:e, e:]))
                hi, lo = split(u)
                uh_ref[s:e, e:] = hi
                ul_ref[s:e, e:] = lo
                for i in range(k + 1, width // NB):
                    q = i * NB
                    w = q - e
                    a_ref[q : q + NB, q:] = a_ref[q : q + NB, q:] - dot_tn(
                        hi[:, w : w + NB], lo[:, w : w + NB], hi[:, w:], lo[:, w:]
                    )

        return carry

    lax.fori_loop(0, count, panel, 0)


def first_kernel(at_ref, amp_ref, mine_ref, other_ref, nz_ref, x_ref, uh_ref, ul_ref, inv_ref, rest_ref, a_ref):
    n = a_ref.shape[0]
    steps, panels, piece = mine_ref.shape[:3]
    block = n // panels
    me = at_ref[1]
    for m in range(steps):
        for s in range(panels):
            place(x_ref, s * block, me ^ (2 * m), piece, mine_ref[m, s])
            place(x_ref, s * block, me ^ (2 * m + 1), piece, other_ref[m, s])
    amp = amp_ref[0]
    sq_row = half_norm_rows(x_ref[...])
    noise = nz_ref[...]
    for i in range(n // NB):
        o = i * NB
        xi = x_ref[o : o + NB, :]
        cross = lax.dot_general(xi, x_ref[o:, :], TRANS_B, preferred_element_type=f32)
        k = amp * jnp.exp(cross - half_norm_cols(xi, n - o) - sq_row[:, o:])
        a_ref[o : o + NB, o:] = k
        row = noise[o // block : o // block + 1, o % block : o % block + NB]
        a_ref[o : o + NB, o : o + NB] = k[:, :NB] + jnp.where(diagonal(NB), jnp.broadcast_to(row, (NB, NB)), 0.0)
    first = inv_ref.shape[0]
    factor_panels(a_ref, uh_ref, ul_ref, inv_ref, first, n)
    rest_ref[...] = a_ref[first * NB :, first * NB :]


def second_kernel(rest_ref, uh_ref, ul_ref, inv_ref, a_ref):
    a_ref[...] = rest_ref[...]
    factor_panels(a_ref, uh_ref, ul_ref, inv_ref, inv_ref.shape[0], a_ref.shape[1])


def store_block(out_ref, a, b, row, ncols, value):
    rows, block = value.shape
    per = block // NB
    for q in range(per):
        at = ((a * block + row) * ncols + b) * per + q
        out_ref[pl.ds(at, rows, stride=ncols * per), :] = value[:, q * NB : (q + 1) * NB]


def bulk_kernel(at_ref, amp_ref, *refs):
    lead_refs, refs = refs[:8], refs[8:]
    x_ref, uh0_ref, ul0_ref, inv0_ref, uh1_ref, ul1_ref, inv1_ref, nz_ref = lead_refs
    count = len(refs) - 10
    near_refs, other_ref, out_ref = refs[:count], refs[count], refs[count + 1]
    r_ref, c_ref, ph_ref, pl_ref, zh_ref, zl_ref, wh_ref, wl_ref = refs[count + 2 :]
    n = x_ref.shape[0]
    split_at = uh0_ref.shape[0]
    nrows, block = nz_ref.shape
    piece = other_ref.shape[2]
    ncols = c_ref.shape[0] // block
    row_at, me, row_n, col_n = at_ref[0], at_ref[1], at_ref[2], at_ref[3]
    amp = amp_ref[0]
    for m in range(count):
        for a in range(nrows):
            place(r_ref, a * block, me ^ (2 * m), piece, near_refs[m][a])
            place(r_ref, a * block, me ^ (2 * m + 1), piece, other_ref[m, a])
        for b in range(ncols):
            place(c_ref, b * block, me ^ (2 * m), piece, near_refs[m][nrows + ncols + b])
            place(c_ref, b * block, me ^ (2 * m + 1), piece, other_ref[m, nrows + b])

    def upper(r0, r1, c0, c1):
        parts = []
        if r0 < split_at:
            r = min(r1, split_at)
            parts.append((uh0_ref[r0:r, c0:c1], ul0_ref[r0:r, c0:c1]))
        if r1 > split_at:
            r = max(r0, split_at)
            d = split_at
            parts.append((uh1_ref[r - d : r1 - d, c0 - d : c1 - d], ul1_ref[r - d : r1 - d, c0 - d : c1 - d]))
        return tuple(jnp.concatenate([p[h] for p in parts], 0) if len(parts) > 1 else parts[0][h] for h in (0, 1))

    def inverse(k):
        d = split_at // NB
        return inv0_ref[k] if k < d else inv1_ref[k - d]

    steps = n // WB
    for q in range(steps):
        top, low = inverse(2 * q), inverse(2 * q + 1)
        s = q * WB
        corner = dot_tn(*upper(s, s + NB, s + NB, s + WB), *split(top))
        corner = -dot_nn(*split(low), *split(corner))
        zero = jnp.zeros((NB, NB), f32)
        full = jnp.concatenate([jnp.concatenate([top, zero], 1), jnp.concatenate([corner, low], 1)], 0)
        wh_ref[q], wl_ref[q] = split(full)
    lead_sq = half_norm_rows(x_ref[...])

    def kernel_entries(x, sq, q):
        s = q * WB
        cross = lax.dot_general(x, x_ref[s : s + WB, :], TRANS_B, preferred_element_type=f32)
        return amp * jnp.exp(cross - sq - lead_sq[:, s : s + WB])

    def forward(x, hi_ref, lo_ref, rows, last):
        sq = half_norm_cols(x, WB)
        for q in range(last):
            s = q * WB
            acc = kernel_entries(x, sq, q)
            if q:
                acc = acc - dot_nn(hi_ref[rows, 0:s], lo_ref[rows, 0:s], *upper(0, s, s, s + WB))
            hi_ref[rows, s : s + WB], lo_ref[rows, s : s + WB] = split(dot_nt(*split(acc), wh_ref[q], wl_ref[q]))

    chunk = 256
    for b in range(ncols):
        j = b * col_n + me
        cols = slice(b * block, (b + 1) * block)

        @pl.when(j >= PANELS)
        def _():
            xc = c_ref[cols, :]
            everyone = slice(0, block)
            for h in range(0, nrows * block, chunk):
                xr = r_ref[h : h + chunk, :]
                sq = half_norm_cols(xr, WB)
                for q in range(steps):
                    s = q * WB
                    ph_ref[h : h + chunk, s : s + WB], pl_ref[h : h + chunk, s : s + WB] = split(
                        kernel_entries(xr, sq, q)
                    )
            forward(xc, zh_ref, zl_ref, everyone, steps)
            for q in range(steps - 1, -1, -1):
                s = q * WB
                e = s + WB
                hi, lo = zh_ref[:, s:e], zl_ref[:, s:e]
                if q < steps - 1:
                    acc = hi.astype(f32) + lo.astype(f32)
                    acc = acc - dot_nt(zh_ref[:, e:], zl_ref[:, e:], *upper(s, e, e, n))
                    hi, lo = split(acc)
                zh_ref[:, s:e], zl_ref[:, s:e] = split(dot_nn(hi, lo, wh_ref[q], wl_ref[q]))
            col_sq = half_norm_rows(xc)
            for a in range(nrows):
                i = a * row_n + row_at

                @pl.when(i >= PANELS)
                def _():
                    for h in range(0, block, chunk):
                        o = a * block + h
                        xr = r_ref[o : o + chunk, :]
                        cross = lax.dot_general(xr, xc, TRANS_B, preferred_element_type=f32)
                        k = amp * jnp.exp(cross - half_norm_cols(xr, block) - col_sq)
                        row_id = lax.broadcasted_iota(jnp.int32, (chunk, block), 0) + h
                        col_id = lax.broadcasted_iota(jnp.int32, (chunk, block), 1)
                        on_diag = (row_id == col_id) & (i == j)
                        k = k + jnp.where(on_diag, jnp.broadcast_to(nz_ref[a : a + 1, :], (chunk, block)), 0.0)
                        k = k - dot_nt(
                            ph_ref[o : o + chunk, :], pl_ref[o : o + chunk, :], zh_ref[...], zl_ref[...]
                        )
                        store_block(out_ref, a, b, h, ncols, k)

                @pl.when(i < PANELS)
                def _():
                    store_block(out_ref, a, b, 0, ncols, jnp.zeros((block, block), f32))

        if b:
            continue
        for s in range(PANELS):
            w = s * block
            for a in range(nrows):
                i = a * row_n + row_at
                rows = slice(a * block, (a + 1) * block)

                @pl.when((j == s) & (i >= PANELS))
                def _():
                    forward(r_ref[rows, :], ph_ref, pl_ref, rows, (w + block) // WB)
                    hi, lo = ph_ref[rows, w : w + block], pl_ref[rows, w : w + block]
                    store_block(out_ref, a, b, 0, ncols, hi.astype(f32) + lo.astype(f32))

                if a:
                    continue
                for v in range(PANELS):

                    @pl.when((j == s) & (i == v))
                    def _():
                        if v < s:
                            u = jnp.zeros((block, block), f32)
                        else:
                            hi, lo = upper(w, w + block, v * block, (v + 1) * block)
                            u = (hi.astype(f32) + lo.astype(f32)).T
                        if v == s:
                            row_id = lax.broadcasted_iota(jnp.int32, (block, block), 0)
                            col_id = lax.broadcasted_iota(jnp.int32, (block, block), 1)
                            u = jnp.where(row_id >= col_id, u, 0.0)
                        store_block(out_ref, a, b, 0, ncols, u)


SMEM = pl.BlockSpec(memory_space=pltpu.SMEM)
VMEM = pl.BlockSpec(memory_space=pltpu.VMEM)


def exchange(x, axis, k):
    return lax.ppermute(x, axis, [(i, i ^ k) for i in range(lax.axis_size(axis))])


def choose(index, options):
    out = options[0]
    for k in range(1, len(options)):
        out = jnp.where(index == k, options[k], out)
    return out


def local(features, amplitude, noise):
    row_n = lax.axis_size("row")
    col_n = lax.axis_size("col")
    row_at = lax.axis_index("row")
    col_at = lax.axis_index("col")
    nrows, _, piece, width = features.shape
    block = piece * col_n
    ncols = nrows * row_n // col_n
    n = PANELS * block
    mine = features.reshape(nrows, piece, width)
    noise_rows = noise.reshape(nrows, block)
    plane = [mine] + [exchange(mine, "row", k) for k in range(1, row_n)]
    lead = jnp.stack([choose(row_at ^ s, [p[0] for p in plane]) for s in range(PANELS)])
    noise_rows, lead = lax.optimization_barrier((noise_rows, lead))
    near = [lead] + [exchange(lead, "col", k) for k in range(2, col_n, 2)]
    noises = [noise_rows] + [exchange(noise_rows, "row", k) for k in range(1, row_n)]
    lead_noise = jnp.stack([choose(row_at ^ s, [p[0] for p in noises]) for s in range(PANELS)])
    near = jnp.stack(near)
    other = exchange(near, "col", 1)
    everything, near = lax.optimization_barrier((jnp.stack(plane), near))
    core = col_at & 1

    def parcel(to):
        out = [mine]
        for to_core in (1 - core, core):
            for b in range(ncols):
                number = b * col_n + (to & ~1) + to_core
                at = (row_at ^ (number & (row_n - 1)), number // row_n, 0, 0)
                out.append(lax.dynamic_slice(everything, at, (1, 1, piece, width)).reshape(1, piece, width))
        return jnp.concatenate(out, 0)

    parcels = [parcel(col_at)] + [exchange(parcel(col_at ^ k), "col", k) for k in range(2, col_n, 2)]
    at = jnp.stack([row_at, col_at, jnp.int32(row_n), jnp.int32(col_n)])
    first = n // NB // 2
    n1 = n - first * NB
    points, uh0, ul0, inv0, rest = pl.pallas_call(
        first_kernel,
        out_shape=[
            jax.ShapeDtypeStruct((n, width), bf16),
            jax.ShapeDtypeStruct((first * NB, n), bf16),
            jax.ShapeDtypeStruct((first * NB, n), bf16),
            jax.ShapeDtypeStruct((first, NB, NB), f32),
            jax.ShapeDtypeStruct((n1, n1), f32),
        ],
        in_specs=[SMEM, SMEM, VMEM, VMEM, VMEM],
        out_specs=[VMEM] * 5,
        scratch_shapes=[pltpu.VMEM((n, n), f32)],
        compiler_params=pltpu.CompilerParams(vmem_limit_bytes=GRANT),
        cost_estimate=pl.CostEstimate(flops=20_000_000_000, bytes_accessed=8_000_000, transcendentals=0),
        name="first",
    )(at, amplitude, near, other, lead_noise)
    parcels, rest = lax.optimization_barrier((parcels, rest))
    passed = exchange(jnp.stack([p[: nrows + ncols] for p in parcels]), "col", 1)
    uh1, ul1, inv1 = pl.pallas_call(
        second_kernel,
        out_shape=[
            jax.ShapeDtypeStruct((n1, n1), bf16),
            jax.ShapeDtypeStruct((n1, n1), bf16),
            jax.ShapeDtypeStruct((n1 // NB, NB, NB), f32),
        ],
        in_specs=[VMEM],
        out_specs=[VMEM] * 3,
        scratch_shapes=[pltpu.VMEM((n1, n1), f32)],
        compiler_params=pltpu.CompilerParams(vmem_limit_bytes=GRANT),
        cost_estimate=pl.CostEstimate(flops=20_000_000_000, bytes_accessed=8_000_000, transcendentals=0),
        name="second",
    )(rest)
    half = pltpu.VMEM((block, n), bf16)
    out = pl.pallas_call(
        bulk_kernel,
        out_shape=jax.ShapeDtypeStruct((nrows * block * ncols * (block // NB), NB), f32),
        in_specs=[SMEM, SMEM] + [VMEM] * (9 + len(parcels)),
        out_specs=VMEM,
        scratch_shapes=[
            pltpu.VMEM((nrows * block, width), bf16),
            pltpu.VMEM((ncols * block, width), bf16),
            pltpu.VMEM((nrows * block, n), bf16),
            pltpu.VMEM((nrows * block, n), bf16),
            half,
            half,
            pltpu.VMEM((n // WB, WB, WB), bf16),
            pltpu.VMEM((n // WB, WB, WB), bf16),
        ],
        compiler_params=pltpu.CompilerParams(vmem_limit_bytes=GRANT),
        cost_estimate=pl.CostEstimate(flops=12_000_000_000, bytes_accessed=8_000_000, transcendentals=0),
        name="bulk",
    )(at, amplitude, points, uh0, ul0, inv0, uh1, ul1, inv1, noise_rows, *parcels, passed)
    return out.reshape(nrows, 1, block, ncols, 1, block)


def solution(mesh):
    return jax.shard_map(
        local,
        mesh=mesh,
        in_specs=(P(None, "row", "col", None), P(), P(None, "row", None)),
        out_specs=P(None, "row", None, None, "col", None),
        check_vma=False,
    )
```

```python
import functools

import jax
import jax.numpy as jnp
from jax import lax
from jax.experimental import pallas as pl
from jax.experimental.pallas import tpu as pltpu
from jax.sharding import PartitionSpec as P

PANELS = 2
NB = 128
WB = 256
GRANT = 30 << 20
UPDATE_ROWS = 256
FIRST = 5
f32 = jnp.float32
bf16 = jnp.bfloat16
TRANS_B = (((1,), (1,)), ((), ()))
TRANS_A = (((0,), (0,)), ((), ()))


def split(x):
    hi = x.astype(bf16)
    return hi, (x - hi.astype(f32)).astype(bf16)


def dot_nn(ah, al, bh, bl):
    return jnp.dot(
        jnp.concatenate([ah, ah, al], 1), jnp.concatenate([bh, bl, bh], 0), preferred_element_type=f32
    )


def dot_nt(ah, al, bh, bl):
    return lax.dot_general(
        jnp.concatenate([ah, ah, al], 1), jnp.concatenate([bh, bl, bh], 1), TRANS_B, preferred_element_type=f32
    )


def dot_tn(ah, al, bh, bl):
    return lax.dot_general(
        jnp.concatenate([ah, ah, al], 0), jnp.concatenate([bh, bl, bh], 0), TRANS_A, preferred_element_type=f32
    )


def spread(x):
    return jnp.broadcast_to(x, (8, NB))


def tree_sum(xs):
    while len(xs) > 1:
        xs = [xs[i] + xs[i + 1] if i + 1 < len(xs) else xs[i] for i in range(0, len(xs), 2)]
    return xs[0]


def factor_tile(t, rows, cols, lane, sub):
    scaled, ratio, inverses, pivots = [], {}, [], None
    for j in range(8):
        pivot = spread(cols[j][j : j + 1, :])
        inv = 1.0 / pivot
        inverses.append(inv)
        pivots = pivot if j == 0 else jnp.where(sub == j, pivot, pivots)
        below = jnp.where(sub > j, cols[j], 0.0)
        for k in range(j + 1, 8):
            entry = spread(cols[k][j : j + 1, :])
            cols[k] = cols[k] - (below * entry) * inv
            ratio[j, k] = entry * inv
        row = spread(rows[j : j + 1, :]) * inv
        row = jnp.where(lane == 8 * t + j, 1.0 + inv, row)
        scaled.append(row)
        if j < 7:
            rows = rows - below * row
    return rows, lax.rsqrt(pivots), scaled, ratio, inverses


def factor_block(tiles, store_u, store_l):
    tiles = list(tiles)
    n = len(tiles)
    lane = lax.broadcasted_iota(jnp.int32, (8, NB), 1)
    sub = lax.broadcasted_iota(jnp.int32, (8, NB), 0)
    cols = [spread(tiles[0][:, k : k + 1]) for k in range(8)]
    for t in range(n):
        last = t + 1 == n
        if not last:
            near = [spread(tiles[t + 1][:, 8 * t + k : 8 * t + k + 1]) for k in range(8)]
            ahead = [spread(tiles[t + 1][:, 8 * t + 8 + k : 8 * t + 9 + k]) for k in range(8)]
        far = {i: [spread(tiles[i][:, 8 * t + k : 8 * t + k + 1]) for k in range(8)] for i in range(t + 2, n)}
        rows, root, scaled, ratio, inverses = factor_tile(t, tiles[t], cols, lane, sub)
        if not last:
            for j in range(8):
                part = near[j] * inverses[j]
                for k in range(j + 1, 8):
                    near[k] = near[k] - near[j] * ratio[j, k]
                for k in range(8):
                    ahead[k] = ahead[k] - near[j] * spread(part[k : k + 1, :])
                tiles[t + 1] = tiles[t + 1] - near[j] * scaled[j]
            cols = ahead
        back = list(scaled)
        for j in range(6, -1, -1):
            for k in range(7, j, -1):
                back[j] = back[j] - ratio[j, k] * back[k]
        for i in range(t + 2, n):
            tiles[i] = tiles[i] - tree_sum([far[i][j] * back[j] for j in range(8)])
        final = rows * root
        diff = lane - sub - 8 * t
        store_u(t, jnp.where(diff >= 0, final, 0.0))
        store_l(t, jnp.where(diff < 0, final, jnp.where(diff == 0, root, 0.0)))


def half_norm_rows(x):
    xf = x.astype(f32)
    hi, lo = split(xf * xf)
    ones = jnp.ones((8, x.shape[1]), bf16)
    total = lax.dot_general(ones, hi, TRANS_B, preferred_element_type=f32)
    total = total + lax.dot_general(ones, lo, TRANS_B, preferred_element_type=f32)
    return 0.5 * total[0:1]


def half_norm_cols(x, width):
    xf = x.astype(f32)
    hi, lo = split(xf * xf)
    ones = jnp.ones((NB, x.shape[1]), bf16)
    total = lax.dot_general(hi, ones, TRANS_B, preferred_element_type=f32)
    total = 0.5 * (total + lax.dot_general(lo, ones, TRANS_B, preferred_element_type=f32))
    return jnp.concatenate([total] * (width // NB), 1)


def diagonal(n):
    return lax.broadcasted_iota(jnp.int32, (n, n), 0) == lax.broadcasted_iota(jnp.int32, (n, n), 1)


def place(x_ref, base, piece_at, piece, value):
    at = pl.multiple_of(base + piece_at * piece, piece)
    x_ref[pl.ds(at, piece), :] = value


def factor_panels(a_ref, u_ref, wh_ref, wl_ref, inv_ref, row0, count, block):
    n = a_ref.shape[1]

    def panel(p, carry):
        r = pl.multiple_of(p * NB, NB)
        o = pl.multiple_of(row0 + p * NB, NB)
        d = a_ref[pl.ds(r, NB), pl.ds(o, NB)]

        def store_u(t, v):
            u_ref[pl.ds(pl.multiple_of(r + 8 * t, 8), 8), pl.ds(o, NB)] = v

        def store_l(t, v):
            inv_ref[8 * t : 8 * t + 8, :] = v

        factor_block([d[8 * t : 8 * t + 8] for t in range(NB // 8)], store_u, store_l)
        for k in range(count):

            @pl.when(p == k)
            def _():
                lr = k * NB
                rows = slice(lr, lr + NB)
                s = row0 + lr
                e = s + NB
                ih, il = split(inv_ref[...])
                parts = ([a_ref[rows, :s]] if s else []) + ([a_ref[rows, e:]] if e < n else [])
                row = dot_nn(ih, il, *split(jnp.concatenate(parts, 1)))
                hi, lo = split(row)
                for w_ref, w, diag in ((wh_ref, hi, ih), (wl_ref, lo, il)):
                    if s:
                        w_ref[rows, :s] = w[:, :s]
                    w_ref[rows, s:e] = diag
                    end = (s // block + 1) * block
                    if e < end:
                        w_ref[rows, e:end] = jnp.zeros((NB, end - e), bf16)
                if e < n:
                    u_ref[rows, e:] = row[:, s:]
                    right_h = jnp.concatenate(([hi[:, :s]] if s else []) + [ih, hi[:, s:]], 1)
                    right_l = jnp.concatenate(([lo[:, :s]] if s else []) + [il, lo[:, s:]], 1)
                    for i in range(0, n - e, UPDATE_ROWS):
                        f = min(i + UPDATE_ROWS, n - e)
                        change = dot_tn(hi[:, s + i : s + f], lo[:, s + i : s + f], right_h, right_l)
                        q = slice(lr + NB + i, lr + NB + f)
                        if s:
                            a_ref[q, :s] = a_ref[q, :s] - change[:, :s]
                        a_ref[q, s:e] = -change[:, s:e]
                        a_ref[q, e:] = a_ref[q, e:] - change[:, e:]

        return carry

    lax.fori_loop(0, count, panel, 0)


def first_kernel(at_ref, amp_ref, mine_ref, other_ref, nz_ref, x_ref, u_ref, wh_ref, wl_ref, rest_ref, a_ref, inv_ref):
    n = a_ref.shape[0]
    steps, panels, piece = mine_ref.shape[:3]
    block = n // panels
    me = at_ref[1]
    for m in range(steps):
        for s in range(panels):
            place(x_ref, s * block, me ^ (2 * m), piece, mine_ref[m, s])
            place(x_ref, s * block, me ^ (2 * m + 1), piece, other_ref[m, s])
    amp = amp_ref[0]
    sq_row = half_norm_rows(x_ref[...])
    noise = nz_ref[...]
    for o in range(0, n, WB):
        xi = x_ref[o : o + WB, :]
        cross = lax.dot_general(xi, x_ref[o:, :], TRANS_B, preferred_element_type=f32)
        k = amp * jnp.exp(cross - half_norm_cols(xi, n - o) - sq_row[:, o:])
        a_ref[o : o + WB, o:] = k
        row = noise[o // block : o // block + 1, o % block : o % block + WB]
        a_ref[o : o + WB, o : o + WB] = k[:, :WB] + jnp.where(diagonal(WB), jnp.broadcast_to(row, (WB, WB)), 0.0)
    count = u_ref.shape[0] // NB
    factor_panels(a_ref, u_ref, wh_ref, wl_ref, inv_ref, 0, count, block)
    rest_ref[...] = a_ref[count * NB :, :]


def second_kernel(rest_ref, u_ref, wh_ref, wl_ref, a_ref, inv_ref):
    n1, n = rest_ref.shape
    a_ref[...] = rest_ref[...]
    factor_panels(a_ref, u_ref, wh_ref, wl_ref, inv_ref, n - n1, n1 // NB, n // PANELS)


def store_block(out_ref, a, b, row, ncols, value):
    rows, block = value.shape
    per = block // NB
    for q in range(per):
        at = ((a * block + row) * ncols + b) * per + q
        out_ref[pl.ds(at, rows, stride=ncols * per), :] = value[:, q * NB : (q + 1) * NB]


def bulk_kernel(at_ref, amp_ref, *refs):
    x_ref, u0_ref, wh0_ref, wl0_ref, u1_ref, wh1_ref, wl1_ref, nz_ref = refs[:8]
    refs = refs[8:]
    count = len(refs) - 10
    near_refs, other_ref, out_ref = refs[:count], refs[count], refs[count + 1]
    r_ref, c_ref, kh_ref, kl_ref, ph_ref, pl_ref, zh_ref, zl_ref = refs[count + 2 :]
    n = x_ref.shape[0]
    split_at = u0_ref.shape[0]
    nrows, block = nz_ref.shape
    piece = other_ref.shape[2]
    ncols = c_ref.shape[0] // block
    row_at, me, row_n, col_n = at_ref[0], at_ref[1], at_ref[2], at_ref[3]
    amp = amp_ref[0]
    for m in range(count):
        for a in range(nrows):
            place(r_ref, a * block, me ^ (2 * m), piece, near_refs[m][a])
            place(r_ref, a * block, me ^ (2 * m + 1), piece, other_ref[m, a])
        for b in range(ncols):
            place(c_ref, b * block, me ^ (2 * m), piece, near_refs[m][nrows + ncols + b])
            place(c_ref, b * block, me ^ (2 * m + 1), piece, other_ref[m, nrows + b])

    def pick(first_ref, second_ref, r0, r1, c0, c1):
        parts = []
        if r0 < split_at:
            parts.append(first_ref[r0 : min(r1, split_at), c0:c1])
        if r1 > split_at:
            parts.append(second_ref[max(r0, split_at) - split_at : r1 - split_at, c0:c1])
        return jnp.concatenate(parts, 0) if len(parts) > 1 else parts[0]

    def inverse(r0, r1, c0, c1):
        return pick(wh0_ref, wh1_ref, r0, r1, c0, c1), pick(wl0_ref, wl1_ref, r0, r1, c0, c1)

    lead_sq = half_norm_rows(x_ref[...])

    def entries(x):
        cross = lax.dot_general(x, x_ref[...], TRANS_B, preferred_element_type=f32)
        return split(amp * jnp.exp(cross - half_norm_cols(x, n) - lead_sq))

    for a in range(nrows):
        rows = slice(a * block, (a + 1) * block)
        kh_ref[rows, :], kl_ref[rows, :] = entries(r_ref[rows, :])
    for b in range(ncols):
        j = b * col_n + me
        cols = slice(b * block, (b + 1) * block)

        @pl.when(j >= PANELS)
        def _():
            xc = c_ref[cols, :]
            zh_ref[...], zl_ref[...] = entries(xc)
            for s in range(0, n, block):
                e = s + block
                panel = dot_nt(zh_ref[:, :e], zl_ref[:, :e], *inverse(s, e, 0, e))
                ph_ref[:, s:e], pl_ref[:, s:e] = split(panel)
            for s in range(0, n, block):
                e = s + block
                solved = dot_nn(ph_ref[:, s:], pl_ref[:, s:], *inverse(s, n, s, e))
                zh_ref[:, s:e], zl_ref[:, s:e] = split(solved)
            col_sq = half_norm_rows(xc)
            for a in range(nrows):
                i = a * row_n + row_at
                rows = slice(a * block, (a + 1) * block)

                @pl.when(i >= PANELS)
                def _():
                    xr = r_ref[rows, :]
                    cross = lax.dot_general(xr, xc, TRANS_B, preferred_element_type=f32)
                    k = amp * jnp.exp(cross - half_norm_cols(xr, block) - col_sq)
                    on_diag = diagonal(block) & (i == j)
                    k = k + jnp.where(on_diag, jnp.broadcast_to(nz_ref[a : a + 1, :], (block, block)), 0.0)
                    k = k - dot_nt(kh_ref[rows, :], kl_ref[rows, :], zh_ref[...], zl_ref[...])
                    store_block(out_ref, a, b, 0, ncols, k)

                @pl.when(i < PANELS)
                def _():
                    store_block(out_ref, a, b, 0, ncols, jnp.zeros((block, block), f32))

        if b:
            continue
        for s in range(PANELS):
            w = s * block
            for a in range(nrows):
                i = a * row_n + row_at
                rows = slice(a * block, (a + 1) * block)

                @pl.when((j == s) & (i >= PANELS))
                def _():
                    e = w + block
                    panel = dot_nt(kh_ref[rows, :e], kl_ref[rows, :e], *inverse(w, e, 0, e))
                    store_block(out_ref, a, b, 0, ncols, panel)

                if a:
                    continue
                for v in range(PANELS):

                    @pl.when((j == s) & (i == v))
                    def _():
                        if v < s:
                            u = jnp.zeros((block, block), f32)
                        else:
                            u = pick(u0_ref, u1_ref, w, w + block, v * block, (v + 1) * block).T
                        if v == s:
                            row_id = lax.broadcasted_iota(jnp.int32, (block, block), 0)
                            col_id = lax.broadcasted_iota(jnp.int32, (block, block), 1)
                            u = jnp.where(row_id >= col_id, u, 0.0)
                        store_block(out_ref, a, b, 0, ncols, u)


SMEM = pl.BlockSpec(memory_space=pltpu.SMEM)
VMEM = pl.BlockSpec(memory_space=pltpu.VMEM)


def exchange(x, axis, k):
    return lax.ppermute(x, axis, [(i, i ^ k) for i in range(lax.axis_size(axis))])


def choose(index, options):
    out = options[0]
    for k in range(1, len(options)):
        out = jnp.where(index == k, options[k], out)
    return out


def local(features, amplitude, noise):
    row_n = lax.axis_size("row")
    col_n = lax.axis_size("col")
    row_at = lax.axis_index("row")
    col_at = lax.axis_index("col")
    nrows, _, piece, width = features.shape
    block = piece * col_n
    ncols = nrows * row_n // col_n
    n = PANELS * block
    mine = features.reshape(nrows, piece, width)
    noise_rows = noise.reshape(nrows, block)
    plane = [mine] + [exchange(mine, "row", k) for k in range(1, row_n)]
    lead = jnp.stack([choose(row_at ^ s, [p[0] for p in plane]) for s in range(PANELS)])
    noise_rows, lead = lax.optimization_barrier((noise_rows, lead))
    near = [lead] + [exchange(lead, "col", k) for k in range(2, col_n, 2)]
    noises = [noise_rows] + [exchange(noise_rows, "row", k) for k in range(1, row_n)]
    lead_noise = jnp.stack([choose(row_at ^ s, [p[0] for p in noises]) for s in range(PANELS)])
    near = jnp.stack(near)
    other = exchange(near, "col", 1)
    everything, near = lax.optimization_barrier((jnp.stack(plane), near))
    core = col_at & 1

    def parcel(to):
        out = [mine]
        for to_core in (1 - core, core):
            for b in range(ncols):
                number = b * col_n + (to & ~1) + to_core
                at = (row_at ^ (number & (row_n - 1)), number // row_n, 0, 0)
                out.append(lax.dynamic_slice(everything, at, (1, 1, piece, width)).reshape(1, piece, width))
        return jnp.concatenate(out, 0)

    parcels = [parcel(col_at)] + [exchange(parcel(col_at ^ k), "col", k) for k in range(2, col_n, 2)]
    at = jnp.stack([row_at, col_at, jnp.int32(row_n), jnp.int32(col_n)])
    first = FIRST * n // NB // 8 * NB
    n1 = n - first
    params = pltpu.CompilerParams(vmem_limit_bytes=GRANT)
    cost = pl.CostEstimate(flops=20_000_000_000, bytes_accessed=8_000_000, transcendentals=0)
    square = pltpu.VMEM((NB, NB), f32)

    def factor_shapes(rows):
        half = jax.ShapeDtypeStruct((rows, n), bf16)
        return [jax.ShapeDtypeStruct((rows, n), f32), half, half]

    points, u0, wh0, wl0, rest = pl.pallas_call(
        first_kernel,
        out_shape=[jax.ShapeDtypeStruct((n, width), bf16)]
        + factor_shapes(first)
        + [jax.ShapeDtypeStruct((n1, n), f32)],
        in_specs=[SMEM, SMEM, VMEM, VMEM, VMEM],
        out_specs=[VMEM] * 5,
        scratch_shapes=[pltpu.VMEM((n, n), f32), square],
        compiler_params=params,
        cost_estimate=cost,
        name="first",
    )(at, amplitude, near, other, lead_noise)
    parcels, rest = lax.optimization_barrier((parcels, rest))
    passed = exchange(jnp.stack([p[: nrows + ncols] for p in parcels]), "col", 1)
    u1, wh1, wl1 = pl.pallas_call(
        second_kernel,
        out_shape=factor_shapes(n1),
        in_specs=[VMEM],
        out_specs=[VMEM] * 3,
        scratch_shapes=[pltpu.VMEM((n1, n), f32), square],
        compiler_params=params,
        cost_estimate=cost,
        name="second",
    )(rest)
    half = pltpu.VMEM((block, n), bf16)
    tall = pltpu.VMEM((nrows * block, n), bf16)
    out = pl.pallas_call(
        bulk_kernel,
        out_shape=jax.ShapeDtypeStruct((nrows * block * ncols * (block // NB), NB), f32),
        in_specs=[SMEM, SMEM] + [VMEM] * (9 + len(parcels)),
        out_specs=VMEM,
        scratch_shapes=[
            pltpu.VMEM((nrows * block, width), bf16),
            pltpu.VMEM((ncols * block, width), bf16),
            tall,
            tall,
            half,
            half,
            half,
            half,
        ],
        compiler_params=params,
        cost_estimate=cost,
        name="bulk",
    )(at, amplitude, points, u0, wh0, wl0, u1, wh1, wl1, noise_rows, *parcels, passed)
    return out.reshape(nrows, 1, block, ncols, 1, block)


def solution(mesh):
    return jax.shard_map(
        local,
        mesh=mesh,
        in_specs=(P(None, "row", "col", None), P(), P(None, "row", None)),
        out_specs=P(None, "row", None, None, "col", None),
        check_vma=False,
    )
```

```python
import functools

import jax
import jax.numpy as jnp
from jax import lax
from jax.experimental import pallas as pl
from jax.experimental.pallas import tpu as pltpu
from jax.sharding import PartitionSpec as P

PANELS = 2
NB = 128
WB = 256
GRANT = 30 << 20
UPDATE_ROWS = 256
FIRST = 5
GROUP = 4
f32 = jnp.float32
bf16 = jnp.bfloat16
TRANS_B = (((1,), (1,)), ((), ()))
TRANS_A = (((0,), (0,)), ((), ()))


def split(x):
    hi = x.astype(bf16)
    return hi, (x - hi.astype(f32)).astype(bf16)


def dot_nn(ah, al, bh, bl):
    return jnp.dot(
        jnp.concatenate([ah, ah, al], 1), jnp.concatenate([bh, bl, bh], 0), preferred_element_type=f32
    )


def dot_nt(ah, al, bh, bl):
    return lax.dot_general(
        jnp.concatenate([ah, ah, al], 1), jnp.concatenate([bh, bl, bh], 1), TRANS_B, preferred_element_type=f32
    )


def dot_tn(ah, al, bh, bl):
    return lax.dot_general(
        jnp.concatenate([ah, ah, al], 0), jnp.concatenate([bh, bl, bh], 0), TRANS_A, preferred_element_type=f32
    )


def spread(x):
    return jnp.broadcast_to(x, (8, NB))


def tree_sum(xs):
    while len(xs) > 1:
        xs = [xs[i] + xs[i + 1] if i + 1 < len(xs) else xs[i] for i in range(0, len(xs), 2)]
    return xs[0]


def factor_tile(t, rows, cols, lane, sub):
    scaled, ratio, inverses, pivots = [], {}, [], None
    for j in range(8):
        pivot = spread(cols[j][j : j + 1, :])
        inv = 1.0 / pivot
        inverses.append(inv)
        pivots = pivot if j == 0 else jnp.where(sub == j, pivot, pivots)
        for k in range(j + 1, 8):
            entry = spread(cols[k][j : j + 1, :])
            ratio[j, k] = entry * inv
            cols[k] = cols[k] - ((cols[j] * entry) * inv if k == j + 1 else cols[j] * ratio[j, k])
        row = spread(rows[j : j + 1, :]) * inv
        row = jnp.where(lane == 8 * t + j, 1.0 + inv, row)
        scaled.append(row)
        if j < 7:
            rows = rows - jnp.where(sub > j, cols[j], 0.0) * row
    return rows, lax.rsqrt(pivots), scaled, ratio, inverses


def lane_columns(tile, first):
    return [spread(tile[:, first + k : first + k + 1]) for k in range(8)]


def factor_block(tiles, store_u, store_l):
    tiles = list(tiles)
    n = len(tiles)
    lane = lax.broadcasted_iota(jnp.int32, (8, NB), 1)
    sub = lax.broadcasted_iota(jnp.int32, (8, NB), 0)
    cols = lane_columns(tiles[0], 0)
    for g in range(0, n, GROUP):
        end = g + GROUP
        window = min(n, end + 1)
        left, right = [], []
        for t in range(g, end):
            last = t + 1 == window
            if not last:
                near = lane_columns(tiles[t + 1], 8 * t)
                ahead = lane_columns(tiles[t + 1], 8 * t + 8)
            far = {i: lane_columns(tiles[i], 8 * t) for i in range(t + 2, window)}
            rows, root, scaled, ratio, inverses = factor_tile(t, tiles[t], cols, lane, sub)
            if not last:
                for j in range(8):
                    part = near[j] * inverses[j]
                    for k in range(j + 1, 8):
                        near[k] = near[k] - near[j] * ratio[j, k]
                    for k in range(8):
                        ahead[k] = ahead[k] - near[j] * spread(part[k : k + 1, :])
                    tiles[t + 1] = tiles[t + 1] - near[j] * scaled[j]
                cols = ahead
            if far:
                back = list(scaled)
                for j in range(6, -1, -1):
                    for k in range(7, j, -1):
                        back[j] = back[j] - ratio[j, k] * back[k]
                for i in far:
                    tiles[i] = tiles[i] - tree_sum([far[i][j] * back[j] for j in range(8)])
            final = rows * root
            diff = lane - sub - 8 * t
            lower = jnp.where(diff < 0, final, jnp.where(diff == 0, root, 0.0))
            store_u(t, jnp.where(diff >= 0, final, 0.0))
            store_l(t, lower)
            left.append(final)
            right.append(jnp.where(lane >= 8 * end, final, lower))
        if window < n:
            change = dot_tn(*split(jnp.concatenate(left, 0)), *split(jnp.concatenate(right, 0)))
            keep = (lane < 8 * g) | (lane >= 8 * end)
            for i in range(window, n):
                tiles[i] = jnp.where(keep, tiles[i], 0.0) - change[8 * i : 8 * i + 8]


def half_norm_rows(x):
    xf = x.astype(f32)
    hi, lo = split(xf * xf)
    ones = jnp.ones((8, x.shape[1]), bf16)
    total = lax.dot_general(ones, hi, TRANS_B, preferred_element_type=f32)
    total = total + lax.dot_general(ones, lo, TRANS_B, preferred_element_type=f32)
    return 0.5 * total[0:1]


def half_norm_cols(x, width):
    xf = x.astype(f32)
    hi, lo = split(xf * xf)
    ones = jnp.ones((NB, x.shape[1]), bf16)
    total = lax.dot_general(hi, ones, TRANS_B, preferred_element_type=f32)
    total = 0.5 * (total + lax.dot_general(lo, ones, TRANS_B, preferred_element_type=f32))
    return jnp.concatenate([total] * (width // NB), 1)


def diagonal(n):
    return lax.broadcasted_iota(jnp.int32, (n, n), 0) == lax.broadcasted_iota(jnp.int32, (n, n), 1)


def place(x_ref, base, piece_at, piece, value):
    at = pl.multiple_of(base + piece_at * piece, piece)
    x_ref[pl.ds(at, piece), :] = value


def factor_panels(a_ref, u_ref, wh_ref, wl_ref, inv_ref, row0, count, block):
    n = a_ref.shape[1]

    def panel(p, carry):
        r = pl.multiple_of(p * NB, NB)
        o = pl.multiple_of(row0 + p * NB, NB)
        d = a_ref[pl.ds(r, NB), pl.ds(o, NB)]

        def store_u(t, v):
            u_ref[pl.ds(pl.multiple_of(r + 8 * t, 8), 8), pl.ds(o, NB)] = v

        def store_l(t, v):
            inv_ref[8 * t : 8 * t + 8, :] = v

        factor_block([d[8 * t : 8 * t + 8] for t in range(NB // 8)], store_u, store_l)
        for k in range(count):

            @pl.when(p == k)
            def _():
                lr = k * NB
                rows = slice(lr, lr + NB)
                s = row0 + lr
                e = s + NB
                ih, il = split(inv_ref[...])
                parts = ([a_ref[rows, :s]] if s else []) + ([a_ref[rows, e:]] if e < n else [])
                row = dot_nn(ih, il, *split(jnp.concatenate(parts, 1)))
                hi, lo = split(row)
                for w_ref, w, diag in ((wh_ref, hi, ih), (wl_ref, lo, il)):
                    if s:
                        w_ref[rows, :s] = w[:, :s]
                    w_ref[rows, s:e] = diag
                    end = (s // block + 1) * block
                    if e < end:
                        w_ref[rows, e:end] = jnp.zeros((NB, end - e), bf16)
                if e < n:
                    u_ref[rows, e:] = row[:, s:]
                    right_h = jnp.concatenate(([hi[:, :s]] if s else []) + [ih, hi[:, s:]], 1)
                    right_l = jnp.concatenate(([lo[:, :s]] if s else []) + [il, lo[:, s:]], 1)
                    for i in range(0, n - e, UPDATE_ROWS):
                        f = min(i + UPDATE_ROWS, n - e)
                        change = dot_tn(hi[:, s + i : s + f], lo[:, s + i : s + f], right_h, right_l)
                        q = slice(lr + NB + i, lr + NB + f)
                        if s:
                            a_ref[q, :s] = a_ref[q, :s] - change[:, :s]
                        a_ref[q, s:e] = -change[:, s:e]
                        a_ref[q, e:] = a_ref[q, e:] - change[:, e:]

        return carry

    lax.fori_loop(0, count, panel, 0)


def first_kernel(at_ref, amp_ref, mine_ref, other_ref, nz_ref, x_ref, u_ref, wh_ref, wl_ref, rest_ref, a_ref, inv_ref):
    n = a_ref.shape[0]
    steps, panels, piece = mine_ref.shape[:3]
    block = n // panels
    me = at_ref[1]
    for m in range(steps):
        for s in range(panels):
            place(x_ref, s * block, me ^ (2 * m), piece, mine_ref[m, s])
            place(x_ref, s * block, me ^ (2 * m + 1), piece, other_ref[m, s])
    amp = amp_ref[0]
    sq_row = half_norm_rows(x_ref[...])
    noise = nz_ref[...]
    for o in range(0, n, WB):
        xi = x_ref[o : o + WB, :]
        cross = lax.dot_general(xi, x_ref[o:, :], TRANS_B, preferred_element_type=f32)
        k = amp * jnp.exp(cross - half_norm_cols(xi, n - o) - sq_row[:, o:])
        a_ref[o : o + WB, o:] = k
        row = noise[o // block : o // block + 1, o % block : o % block + WB]
        a_ref[o : o + WB, o : o + WB] = k[:, :WB] + jnp.where(diagonal(WB), jnp.broadcast_to(row, (WB, WB)), 0.0)
    count = u_ref.shape[0] // NB
    factor_panels(a_ref, u_ref, wh_ref, wl_ref, inv_ref, 0, count, block)
    rest_ref[...] = a_ref[count * NB :, :]


def second_kernel(rest_ref, u_ref, wh_ref, wl_ref, a_ref, inv_ref):
    n1, n = rest_ref.shape
    a_ref[...] = rest_ref[...]
    factor_panels(a_ref, u_ref, wh_ref, wl_ref, inv_ref, n - n1, n1 // NB, n // PANELS)


def store_block(out_ref, a, b, row, ncols, value):
    rows, block = value.shape
    per = block // NB
    for q in range(per):
        at = ((a * block + row) * ncols + b) * per + q
        out_ref[pl.ds(at, rows, stride=ncols * per), :] = value[:, q * NB : (q + 1) * NB]


def bulk_kernel(at_ref, amp_ref, *refs):
    x_ref, u0_ref, wh0_ref, wl0_ref, u1_ref, wh1_ref, wl1_ref, nz_ref = refs[:8]
    refs = refs[8:]
    count = len(refs) - 10
    near_refs, other_ref, out_ref = refs[:count], refs[count], refs[count + 1]
    r_ref, c_ref, kh_ref, kl_ref, ph_ref, pl_ref, zh_ref, zl_ref = refs[count + 2 :]
    n = x_ref.shape[0]
    split_at = u0_ref.shape[0]
    nrows, block = nz_ref.shape
    piece = other_ref.shape[2]
    ncols = c_ref.shape[0] // block
    row_at, me, row_n, col_n = at_ref[0], at_ref[1], at_ref[2], at_ref[3]
    amp = amp_ref[0]
    for m in range(count):
        for a in range(nrows):
            place(r_ref, a * block, me ^ (2 * m), piece, near_refs[m][a])
            place(r_ref, a * block, me ^ (2 * m + 1), piece, other_ref[m, a])
        for b in range(ncols):
            place(c_ref, b * block, me ^ (2 * m), piece, near_refs[m][nrows + ncols + b])
            place(c_ref, b * block, me ^ (2 * m + 1), piece, other_ref[m, nrows + b])

    def pick(first_ref, second_ref, r0, r1, c0, c1):
        parts = []
        if r0 < split_at:
            parts.append(first_ref[r0 : min(r1, split_at), c0:c1])
        if r1 > split_at:
            parts.append(second_ref[max(r0, split_at) - split_at : r1 - split_at, c0:c1])
        return jnp.concatenate(parts, 0) if len(parts) > 1 else parts[0]

    def inverse(r0, r1, c0, c1):
        return pick(wh0_ref, wh1_ref, r0, r1, c0, c1), pick(wl0_ref, wl1_ref, r0, r1, c0, c1)

    lead_sq = half_norm_rows(x_ref[...])

    def entries(x):
        cross = lax.dot_general(x, x_ref[...], TRANS_B, preferred_element_type=f32)
        return split(amp * jnp.exp(cross - half_norm_cols(x, n) - lead_sq))

    for a in range(nrows):
        rows = slice(a * block, (a + 1) * block)
        kh_ref[rows, :], kl_ref[rows, :] = entries(r_ref[rows, :])
    for b in range(ncols):
        j = b * col_n + me
        cols = slice(b * block, (b + 1) * block)

        @pl.when(j >= PANELS)
        def _():
            xc = c_ref[cols, :]
            zh_ref[...], zl_ref[...] = entries(xc)
            for s in range(0, n, block):
                e = s + block
                panel = dot_nt(zh_ref[:, :e], zl_ref[:, :e], *inverse(s, e, 0, e))
                ph_ref[:, s:e], pl_ref[:, s:e] = split(panel)
            for s in range(0, n, block):
                e = s + block
                solved = dot_nn(ph_ref[:, s:], pl_ref[:, s:], *inverse(s, n, s, e))
                zh_ref[:, s:e], zl_ref[:, s:e] = split(solved)
            col_sq = half_norm_rows(xc)
            for a in range(nrows):
                i = a * row_n + row_at
                rows = slice(a * block, (a + 1) * block)

                @pl.when(i >= PANELS)
                def _():
                    xr = r_ref[rows, :]
                    cross = lax.dot_general(xr, xc, TRANS_B, preferred_element_type=f32)
                    k = amp * jnp.exp(cross - half_norm_cols(xr, block) - col_sq)
                    on_diag = diagonal(block) & (i == j)
                    k = k + jnp.where(on_diag, jnp.broadcast_to(nz_ref[a : a + 1, :], (block, block)), 0.0)
                    k = k - dot_nt(kh_ref[rows, :], kl_ref[rows, :], zh_ref[...], zl_ref[...])
                    store_block(out_ref, a, b, 0, ncols, k)

                @pl.when(i < PANELS)
                def _():
                    store_block(out_ref, a, b, 0, ncols, jnp.zeros((block, block), f32))

        if b:
            continue
        for s in range(PANELS):
            w = s * block
            for a in range(nrows):
                i = a * row_n + row_at
                rows = slice(a * block, (a + 1) * block)

                @pl.when((j == s) & (i >= PANELS))
                def _():
                    e = w + block
                    panel = dot_nt(kh_ref[rows, :e], kl_ref[rows, :e], *inverse(w, e, 0, e))
                    store_block(out_ref, a, b, 0, ncols, panel)

                if a:
                    continue
                for v in range(PANELS):

                    @pl.when((j == s) & (i == v))
                    def _():
                        if v < s:
                            u = jnp.zeros((block, block), f32)
                        else:
                            u = pick(u0_ref, u1_ref, w, w + block, v * block, (v + 1) * block).T
                        if v == s:
                            row_id = lax.broadcasted_iota(jnp.int32, (block, block), 0)
                            col_id = lax.broadcasted_iota(jnp.int32, (block, block), 1)
                            u = jnp.where(row_id >= col_id, u, 0.0)
                        store_block(out_ref, a, b, 0, ncols, u)


SMEM = pl.BlockSpec(memory_space=pltpu.SMEM)
VMEM = pl.BlockSpec(memory_space=pltpu.VMEM)


def exchange(x, axis, k):
    return lax.ppermute(x, axis, [(i, i ^ k) for i in range(lax.axis_size(axis))])


def choose(index, options):
    out = options[0]
    for k in range(1, len(options)):
        out = jnp.where(index == k, options[k], out)
    return out


def local(features, amplitude, noise):
    row_n = lax.axis_size("row")
    col_n = lax.axis_size("col")
    row_at = lax.axis_index("row")
    col_at = lax.axis_index("col")
    nrows, _, piece, width = features.shape
    block = piece * col_n
    ncols = nrows * row_n // col_n
    n = PANELS * block
    mine = features.reshape(nrows, piece, width)
    noise_rows = noise.reshape(nrows, block)
    plane = [mine] + [exchange(mine, "row", k) for k in range(1, row_n)]
    lead = jnp.stack([choose(row_at ^ s, [p[0] for p in plane]) for s in range(PANELS)])
    noise_rows, lead = lax.optimization_barrier((noise_rows, lead))
    near = [lead] + [exchange(lead, "col", k) for k in range(2, col_n, 2)]
    everything, near[1] = lax.optimization_barrier((jnp.stack(plane), near[1]))
    noises = [noise_rows] + [exchange(noise_rows, "row", k) for k in range(1, row_n)]
    lead_noise = jnp.stack([choose(row_at ^ s, [p[0] for p in noises]) for s in range(PANELS)])
    core = col_at & 1

    def parcel(to):
        out = [mine]
        for to_core in (1 - core, core):
            for b in range(ncols):
                number = b * col_n + (to & ~1) + to_core
                at = (row_at ^ (number & (row_n - 1)), number // row_n, 0, 0)
                out.append(lax.dynamic_slice(everything, at, (1, 1, piece, width)).reshape(1, piece, width))
        return jnp.concatenate(out, 0)

    parcels = [parcel(col_at)] + [exchange(parcel(col_at ^ k), "col", k) for k in range(2, col_n, 2)]
    near = jnp.stack(near)
    other = exchange(near, "col", 1)
    at = jnp.stack([row_at, col_at, jnp.int32(row_n), jnp.int32(col_n)])
    first = FIRST * n // NB // 8 * NB
    n1 = n - first
    params = pltpu.CompilerParams(vmem_limit_bytes=GRANT)
    cost = pl.CostEstimate(flops=20_000_000_000, bytes_accessed=8_000_000, transcendentals=0)
    square = pltpu.VMEM((NB, NB), f32)

    def factor_shapes(rows):
        half = jax.ShapeDtypeStruct((rows, n), bf16)
        return [jax.ShapeDtypeStruct((rows, n), f32), half, half]

    points, u0, wh0, wl0, rest = pl.pallas_call(
        first_kernel,
        out_shape=[jax.ShapeDtypeStruct((n, width), bf16)]
        + factor_shapes(first)
        + [jax.ShapeDtypeStruct((n1, n), f32)],
        in_specs=[SMEM, SMEM, VMEM, VMEM, VMEM],
        out_specs=[VMEM] * 5,
        scratch_shapes=[pltpu.VMEM((n, n), f32), square],
        compiler_params=params,
        cost_estimate=pl.CostEstimate(flops=1_000_000, bytes_accessed=1_000_000, transcendentals=0),
        name="first",
    )(at, amplitude, near, other, lead_noise)
    parcels, rest = lax.optimization_barrier((parcels, rest))
    passed = exchange(jnp.stack([p[: nrows + ncols] for p in parcels]), "col", 1)
    u1, wh1, wl1 = pl.pallas_call(
        second_kernel,
        out_shape=factor_shapes(n1),
        in_specs=[VMEM],
        out_specs=[VMEM] * 3,
        scratch_shapes=[pltpu.VMEM((n1, n), f32), square],
        compiler_params=params,
        cost_estimate=cost,
        name="second",
    )(rest)
    half = pltpu.VMEM((block, n), bf16)
    tall = pltpu.VMEM((nrows * block, n), bf16)
    out = pl.pallas_call(
        bulk_kernel,
        out_shape=jax.ShapeDtypeStruct((nrows * block * ncols * (block // NB), NB), f32),
        in_specs=[SMEM, SMEM] + [VMEM] * (9 + len(parcels)),
        out_specs=VMEM,
        scratch_shapes=[
            pltpu.VMEM((nrows * block, width), bf16),
            pltpu.VMEM((ncols * block, width), bf16),
            tall,
            tall,
            half,
            half,
            half,
            half,
        ],
        compiler_params=params,
        cost_estimate=cost,
        name="bulk",
    )(at, amplitude, points, u0, wh0, wl0, u1, wh1, wl1, noise_rows, *parcels, passed)
    return out.reshape(nrows, 1, block, ncols, 1, block)


def solution(mesh):
    return jax.shard_map(
        local,
        mesh=mesh,
        in_specs=(P(None, "row", "col", None), P(), P(None, "row", None)),
        out_specs=P(None, "row", None, None, "col", None),
        check_vma=False,
    )
```

```python
import functools

import jax
import jax.numpy as jnp
from jax import lax
from jax.experimental import pallas as pl
from jax.experimental.pallas import tpu as pltpu
from jax.sharding import PartitionSpec as P

PANELS = 2
NB = 128
WB = 256
GRANT = 30 << 20
UPDATE_ROWS = 256
FIRST = 5
GROUP = 4
f32 = jnp.float32
bf16 = jnp.bfloat16
TRANS_B = (((1,), (1,)), ((), ()))
TRANS_A = (((0,), (0,)), ((), ()))


def split(x):
    hi = x.astype(bf16)
    return hi, (x - hi.astype(f32)).astype(bf16)


def dot_nn(ah, al, bh, bl):
    return jnp.dot(
        jnp.concatenate([ah, ah, al], 1), jnp.concatenate([bh, bl, bh], 0), preferred_element_type=f32
    )


def dot_nt(ah, al, bh, bl):
    return lax.dot_general(
        jnp.concatenate([ah, ah, al], 1), jnp.concatenate([bh, bl, bh], 1), TRANS_B, preferred_element_type=f32
    )


def dot_tn(ah, al, bh, bl):
    return lax.dot_general(
        jnp.concatenate([ah, ah, al], 0), jnp.concatenate([bh, bl, bh], 0), TRANS_A, preferred_element_type=f32
    )


def spread(x):
    return jnp.broadcast_to(x, (8, NB))


def tree_sum(xs):
    while len(xs) > 1:
        xs = [xs[i] + xs[i + 1] if i + 1 < len(xs) else xs[i] for i in range(0, len(xs), 2)]
    return xs[0]


def factor_tile(t, rows, cols, lane, sub):
    scaled, ratio, inverses, pivots = [], {}, [], None
    for j in range(8):
        pivot = spread(cols[j][j : j + 1, :])
        inv = 1.0 / pivot
        inverses.append(inv)
        pivots = pivot if j == 0 else jnp.where(sub == j, pivot, pivots)
        for k in range(j + 1, 8):
            entry = spread(cols[k][j : j + 1, :])
            ratio[j, k] = entry * inv
            cols[k] = cols[k] - ((cols[j] * entry) * inv if k == j + 1 else cols[j] * ratio[j, k])
        row = spread(rows[j : j + 1, :]) * inv
        row = jnp.where(lane == 8 * t + j, 1.0 + inv, row)
        scaled.append(row)
        if j < 7:
            rows = rows - jnp.where(sub > j, cols[j], 0.0) * row
    return rows, lax.rsqrt(pivots), scaled, ratio, inverses


def lane_columns(tile, first):
    return [spread(tile[:, first + k : first + k + 1]) for k in range(8)]


def factor_block(tiles, store_u, store_l):
    tiles = list(tiles)
    n = len(tiles)
    lane = lax.broadcasted_iota(jnp.int32, (8, NB), 1)
    sub = lax.broadcasted_iota(jnp.int32, (8, NB), 0)
    cols = lane_columns(tiles[0], 0)
    for g in range(0, n, GROUP):
        end = g + GROUP
        window = min(n, end + 1)
        left, right = [], []
        for t in range(g, end):
            last = t + 1 == window
            if not last:
                near = lane_columns(tiles[t + 1], 8 * t)
                ahead = lane_columns(tiles[t + 1], 8 * t + 8)
            far = {i: lane_columns(tiles[i], 8 * t) for i in range(t + 2, window)}
            rows, root, scaled, ratio, inverses = factor_tile(t, tiles[t], cols, lane, sub)
            if not last:
                for j in range(8):
                    part = near[j] * inverses[j]
                    for k in range(j + 1, 8):
                        near[k] = near[k] - near[j] * ratio[j, k]
                    for k in range(8):
                        ahead[k] = ahead[k] - near[j] * spread(part[k : k + 1, :])
                    tiles[t + 1] = tiles[t + 1] - near[j] * scaled[j]
                cols = ahead
            if far:
                back = list(scaled)
                for j in range(6, -1, -1):
                    for k in range(7, j, -1):
                        back[j] = back[j] - ratio[j, k] * back[k]
                for i in far:
                    tiles[i] = tiles[i] - tree_sum([far[i][j] * back[j] for j in range(8)])
            final = rows * root
            diff = lane - sub - 8 * t
            lower = jnp.where(diff < 0, final, jnp.where(diff == 0, root, 0.0))
            store_u(t, jnp.where(diff >= 0, final, 0.0))
            store_l(t, lower)
            left.append(final)
            right.append(jnp.where(lane >= 8 * end, final, lower))
        if window < n:
            change = dot_tn(*split(jnp.concatenate(left, 0)), *split(jnp.concatenate(right, 0)))
            keep = (lane < 8 * g) | (lane >= 8 * end)
            for i in range(window, n):
                tiles[i] = jnp.where(keep, tiles[i], 0.0) - change[8 * i : 8 * i + 8]


def half_norms(x):
    xf = x.astype(f32)
    hi, lo = split(xf * xf)
    ones = jnp.ones((NB, x.shape[1]), bf16)
    row = lax.dot_general(ones[:8], hi, TRANS_B, preferred_element_type=f32)
    row = row + lax.dot_general(ones[:8], lo, TRANS_B, preferred_element_type=f32)
    col = lax.dot_general(hi, ones, TRANS_B, preferred_element_type=f32)
    col = col + lax.dot_general(lo, ones, TRANS_B, preferred_element_type=f32)
    return 0.5 * row[0:1], 0.5 * col


def half_norm_col(x):
    xf = x.astype(f32)
    hi, lo = split(xf * xf)
    ones = jnp.ones((NB, x.shape[1]), bf16)
    col = lax.dot_general(hi, ones, TRANS_B, preferred_element_type=f32)
    return 0.5 * (col + lax.dot_general(lo, ones, TRANS_B, preferred_element_type=f32))


def widen(col, width):
    return jnp.concatenate([col] * (width // NB), 1)


def log_row(amp, width):
    return jnp.log(jnp.full((1, width), amp, f32))


def diagonal(n):
    return lax.broadcasted_iota(jnp.int32, (n, n), 0) == lax.broadcasted_iota(jnp.int32, (n, n), 1)


def place(x_ref, base, piece_at, piece, value):
    at = pl.multiple_of(base + piece_at * piece, piece)
    x_ref[pl.ds(at, piece), :] = value


def factor_panels(a_ref, u_ref, wh_ref, wl_ref, inv_ref, row0, count, block):
    n = a_ref.shape[1]

    def panel(p, carry):
        r = pl.multiple_of(p * NB, NB)
        o = pl.multiple_of(row0 + p * NB, NB)
        d = a_ref[pl.ds(r, NB), pl.ds(o, NB)]

        def store_u(t, v):
            u_ref[pl.ds(pl.multiple_of(r + 8 * t, 8), 8), pl.ds(o, NB)] = v

        def store_l(t, v):
            inv_ref[8 * t : 8 * t + 8, :] = v

        factor_block([d[8 * t : 8 * t + 8] for t in range(NB // 8)], store_u, store_l)
        for k in range(count):

            @pl.when(p == k)
            def _():
                lr = k * NB
                rows = slice(lr, lr + NB)
                s = row0 + lr
                e = s + NB
                ih, il = split(inv_ref[...])
                parts = ([a_ref[rows, :s]] if s else []) + ([a_ref[rows, e:]] if e < n else [])
                row = dot_nn(ih, il, *split(jnp.concatenate(parts, 1)))
                hi, lo = split(row)
                for w_ref, w, diag in ((wh_ref, hi, ih), (wl_ref, lo, il)):
                    if s:
                        w_ref[rows, :s] = w[:, :s]
                    w_ref[rows, s:e] = diag
                    end = (s // block + 1) * block
                    if e < end:
                        w_ref[rows, e:end] = jnp.zeros((NB, end - e), bf16)
                if e < n:
                    u_ref[rows, e:] = row[:, s:]
                    right_h = jnp.concatenate(([hi[:, :s]] if s else []) + [ih, hi[:, s:]], 1)
                    right_l = jnp.concatenate(([lo[:, :s]] if s else []) + [il, lo[:, s:]], 1)
                    for i in range(0, n - e, UPDATE_ROWS):
                        f = min(i + UPDATE_ROWS, n - e)
                        change = dot_tn(hi[:, s + i : s + f], lo[:, s + i : s + f], right_h, right_l)
                        q = slice(lr + NB + i, lr + NB + f)
                        if s:
                            a_ref[q, :s] = a_ref[q, :s] - change[:, :s]
                        a_ref[q, s:e] = -change[:, s:e]
                        a_ref[q, e:] = a_ref[q, e:] - change[:, e:]

        return carry

    lax.fori_loop(0, count, panel, 0)


def first_kernel(at_ref, amp_ref, mine_ref, other_ref, nz_ref, *refs):
    x_ref, sq_ref, u_ref, wh_ref, wl_ref, rest_ref, a_ref, inv_ref, col_ref = refs
    n = a_ref.shape[0]
    steps, panels, piece = mine_ref.shape[:3]
    block = n // panels
    me = at_ref[1]
    for m in range(steps):
        for s in range(panels):
            place(x_ref, s * block, me ^ (2 * m), piece, mine_ref[m, s])
            place(x_ref, s * block, me ^ (2 * m + 1), piece, other_ref[m, s])
    sq_row, col_ref[...] = half_norms(x_ref[...])
    sq_row = sq_row - log_row(amp_ref[0], n)
    sq_ref[...] = jnp.broadcast_to(sq_row, sq_ref.shape)
    noise = nz_ref[...]
    for o in range(0, n, WB):
        cross = lax.dot_general(x_ref[o : o + WB, :], x_ref[o:, :], TRANS_B, preferred_element_type=f32)
        k = jnp.exp(cross - widen(col_ref[o : o + WB, :], n - o) - sq_row[:, o:])
        a_ref[o : o + WB, o:] = k
        row = noise[o // block : o // block + 1, o % block : o % block + WB]
        a_ref[o : o + WB, o : o + WB] = k[:, :WB] + jnp.where(diagonal(WB), jnp.broadcast_to(row, (WB, WB)), 0.0)
    count = u_ref.shape[0] // NB
    factor_panels(a_ref, u_ref, wh_ref, wl_ref, inv_ref, 0, count, block)
    rest_ref[...] = a_ref[count * NB :, :]


def second_kernel(rest_ref, u_ref, wh_ref, wl_ref, a_ref, inv_ref):
    n1, n = rest_ref.shape
    a_ref[...] = rest_ref[...]
    factor_panels(a_ref, u_ref, wh_ref, wl_ref, inv_ref, n - n1, n1 // NB, n // PANELS)


def store_block(out_ref, a, b, row, ncols, value):
    rows, block = value.shape
    per = block // NB
    for q in range(per):
        at = ((a * block + row) * ncols + b) * per + q
        out_ref[pl.ds(at, rows, stride=ncols * per), :] = value[:, q * NB : (q + 1) * NB]


def bulk_kernel(at_ref, amp_ref, *refs):
    x_ref, sq_ref, u0_ref, wh0_ref, wl0_ref, u1_ref, wh1_ref, wl1_ref, nz_ref = refs[:9]
    refs = refs[9:]
    count = len(refs) - 11
    near_refs, other_ref, out_ref = refs[:count], refs[count], refs[count + 1]
    r_ref, c_ref, kh_ref, kl_ref, ph_ref, pl_ref, zh_ref, zl_ref, col_ref = refs[count + 2 :]
    n = x_ref.shape[0]
    split_at = u0_ref.shape[0]
    nrows, block = nz_ref.shape
    piece = other_ref.shape[2]
    ncols = c_ref.shape[0] // block
    row_at, me, row_n, col_n = at_ref[0], at_ref[1], at_ref[2], at_ref[3]
    for m in range(count):
        for a in range(nrows):
            place(r_ref, a * block, me ^ (2 * m), piece, near_refs[m][a])
            place(r_ref, a * block, me ^ (2 * m + 1), piece, other_ref[m, a])
        for b in range(ncols):
            place(c_ref, b * block, me ^ (2 * m), piece, near_refs[m][nrows + ncols + b])
            place(c_ref, b * block, me ^ (2 * m + 1), piece, other_ref[m, nrows + b])

    def pick(first_ref, second_ref, r0, r1, c0, c1):
        parts = []
        if r0 < split_at:
            parts.append(first_ref[r0 : min(r1, split_at), c0:c1])
        if r1 > split_at:
            parts.append(second_ref[max(r0, split_at) - split_at : r1 - split_at, c0:c1])
        return jnp.concatenate(parts, 0) if len(parts) > 1 else parts[0]

    def inverse(r0, r1, c0, c1):
        return pick(wh0_ref, wh1_ref, r0, r1, c0, c1), pick(wl0_ref, wl1_ref, r0, r1, c0, c1)

    lead_sq = sq_ref[0:1, :]

    def entries(x, col):
        cross = lax.dot_general(x, x_ref[...], TRANS_B, preferred_element_type=f32)
        return split(jnp.exp(cross - widen(col, n) - lead_sq))

    for a in range(nrows):
        rows = slice(a * block, (a + 1) * block)
        col_ref[rows, :] = half_norm_col(r_ref[rows, :])
        kh_ref[rows, :], kl_ref[rows, :] = entries(r_ref[rows, :], col_ref[rows, :])
    for b in range(ncols):
        j = b * col_n + me
        cols = slice(b * block, (b + 1) * block)

        @pl.when(j >= PANELS)
        def _():
            xc = c_ref[cols, :]
            col_sq, col = half_norms(xc)
            col_sq = col_sq - log_row(amp_ref[0], block)
            zh_ref[...], zl_ref[...] = entries(xc, col)
            for s in range(0, n, block):
                e = s + block
                panel = dot_nt(zh_ref[:, :e], zl_ref[:, :e], *inverse(s, e, 0, e))
                ph_ref[:, s:e], pl_ref[:, s:e] = split(panel)
            for s in range(0, n, block):
                e = s + block
                solved = dot_nn(ph_ref[:, s:], pl_ref[:, s:], *inverse(s, n, s, e))
                zh_ref[:, s:e], zl_ref[:, s:e] = split(solved)
            for a in range(nrows):
                i = a * row_n + row_at
                rows = slice(a * block, (a + 1) * block)

                @pl.when(i >= PANELS)
                def _():
                    xr = r_ref[rows, :]
                    cross = lax.dot_general(xr, xc, TRANS_B, preferred_element_type=f32)
                    k = jnp.exp(cross - widen(col_ref[rows, :], block) - col_sq)
                    on_diag = diagonal(block) & (i == j)
                    k = k + jnp.where(on_diag, jnp.broadcast_to(nz_ref[a : a + 1, :], (block, block)), 0.0)
                    k = k - dot_nt(kh_ref[rows, :], kl_ref[rows, :], zh_ref[...], zl_ref[...])
                    store_block(out_ref, a, b, 0, ncols, k)

                @pl.when(i < PANELS)
                def _():
                    store_block(out_ref, a, b, 0, ncols, jnp.zeros((block, block), f32))

        if b:
            continue
        for s in range(PANELS):
            w = s * block
            for a in range(nrows):
                i = a * row_n + row_at
                rows = slice(a * block, (a + 1) * block)

                @pl.when((j == s) & (i >= PANELS))
                def _():
                    e = w + block
                    panel = dot_nt(kh_ref[rows, :e], kl_ref[rows, :e], *inverse(w, e, 0, e))
                    store_block(out_ref, a, b, 0, ncols, panel)

                if a:
                    continue
                for v in range(PANELS):

                    @pl.when((j == s) & (i == v))
                    def _():
                        if v < s:
                            u = jnp.zeros((block, block), f32)
                        else:
                            u = pick(u0_ref, u1_ref, w, w + block, v * block, (v + 1) * block).T
                        if v == s:
                            row_id = lax.broadcasted_iota(jnp.int32, (block, block), 0)
                            col_id = lax.broadcasted_iota(jnp.int32, (block, block), 1)
                            u = jnp.where(row_id >= col_id, u, 0.0)
                        store_block(out_ref, a, b, 0, ncols, u)


SMEM = pl.BlockSpec(memory_space=pltpu.SMEM)
VMEM = pl.BlockSpec(memory_space=pltpu.VMEM)


def exchange(x, axis, k):
    return lax.ppermute(x, axis, [(i, i ^ k) for i in range(lax.axis_size(axis))])


def choose(index, options):
    out = options[0]
    for k in range(1, len(options)):
        out = jnp.where(index == k, options[k], out)
    return out


def local(features, amplitude, noise):
    row_n = lax.axis_size("row")
    col_n = lax.axis_size("col")
    row_at = lax.axis_index("row")
    col_at = lax.axis_index("col")
    nrows, _, piece, width = features.shape
    block = piece * col_n
    ncols = nrows * row_n // col_n
    n = PANELS * block
    mine = features.reshape(nrows, piece, width)
    noise_rows = noise.reshape(nrows, block)
    plane = [mine] + [exchange(mine, "row", k) for k in range(1, row_n)]
    lead = jnp.stack([choose(row_at ^ s, [p[0] for p in plane]) for s in range(PANELS)])
    noise_rows, lead = lax.optimization_barrier((noise_rows, lead))
    near = [lead] + [exchange(lead, "col", k) for k in range(2, col_n, 2)]
    everything, near[1] = lax.optimization_barrier((jnp.stack(plane), near[1]))
    noises = [noise_rows] + [exchange(noise_rows, "row", k) for k in range(1, row_n)]
    lead_noise = jnp.stack([choose(row_at ^ s, [p[0] for p in noises]) for s in range(PANELS)])
    core = col_at & 1

    def parcel(to):
        out = [mine]
        for to_core in (1 - core, core):
            for b in range(ncols):
                number = b * col_n + (to & ~1) + to_core
                at = (row_at ^ (number & (row_n - 1)), number // row_n, 0, 0)
                out.append(lax.dynamic_slice(everything, at, (1, 1, piece, width)).reshape(1, piece, width))
        return jnp.concatenate(out, 0)

    parcels = [parcel(col_at)] + [exchange(parcel(col_at ^ k), "col", k) for k in range(2, col_n, 2)]
    near = jnp.stack(near)
    other = exchange(near, "col", 1)
    at = jnp.stack([row_at, col_at, jnp.int32(row_n), jnp.int32(col_n)])
    first = FIRST * n // NB // 8 * NB
    n1 = n - first
    params = pltpu.CompilerParams(vmem_limit_bytes=GRANT)
    cost = pl.CostEstimate(flops=20_000_000_000, bytes_accessed=8_000_000, transcendentals=0)
    square = pltpu.VMEM((NB, NB), f32)

    def factor_shapes(rows):
        half = jax.ShapeDtypeStruct((rows, n), bf16)
        return [jax.ShapeDtypeStruct((rows, n), f32), half, half]

    points, lead_sq, u0, wh0, wl0, rest = pl.pallas_call(
        first_kernel,
        out_shape=[jax.ShapeDtypeStruct((n, width), bf16), jax.ShapeDtypeStruct((8, n), f32)]
        + factor_shapes(first)
        + [jax.ShapeDtypeStruct((n1, n), f32)],
        in_specs=[SMEM, SMEM, VMEM, VMEM, VMEM],
        out_specs=[VMEM] * 6,
        scratch_shapes=[pltpu.VMEM((n, n), f32), square, pltpu.VMEM((n, NB), f32)],
        compiler_params=params,
        cost_estimate=pl.CostEstimate(flops=1_000_000, bytes_accessed=1_000_000, transcendentals=0),
        name="first",
    )(at, amplitude, near, other, lead_noise)
    parcels, rest = lax.optimization_barrier((parcels, rest))
    passed = exchange(jnp.stack([p[: nrows + ncols] for p in parcels]), "col", 1)
    u1, wh1, wl1 = pl.pallas_call(
        second_kernel,
        out_shape=factor_shapes(n1),
        in_specs=[VMEM],
        out_specs=[VMEM] * 3,
        scratch_shapes=[pltpu.VMEM((n1, n), f32), square],
        compiler_params=params,
        cost_estimate=cost,
        name="second",
    )(rest)
    half = pltpu.VMEM((block, n), bf16)
    tall = pltpu.VMEM((nrows * block, n), bf16)
    out = pl.pallas_call(
        bulk_kernel,
        out_shape=jax.ShapeDtypeStruct((nrows * block * ncols * (block // NB), NB), f32),
        in_specs=[SMEM, SMEM] + [VMEM] * (10 + len(parcels)),
        out_specs=VMEM,
        scratch_shapes=[
            pltpu.VMEM((nrows * block, width), bf16),
            pltpu.VMEM((ncols * block, width), bf16),
            tall,
            tall,
            half,
            half,
            half,
            half,
            pltpu.VMEM((nrows * block, NB), f32),
        ],
        compiler_params=params,
        cost_estimate=cost,
        name="bulk",
    )(at, amplitude, points, lead_sq, u0, wh0, wl0, u1, wh1, wl1, noise_rows, *parcels, passed)
    return out.reshape(nrows, 1, block, ncols, 1, block)


def solution(mesh):
    return jax.shard_map(
        local,
        mesh=mesh,
        in_specs=(P(None, "row", "col", None), P(), P(None, "row", None)),
        out_specs=P(None, "row", None, None, "col", None),
        check_vma=False,
    )
```

```python
import functools

import jax
import jax.numpy as jnp
from jax import lax
from jax.experimental import pallas as pl
from jax.experimental.pallas import tpu as pltpu
from jax.sharding import PartitionSpec as P

PANELS = 2
NB = 128
WB = 256
GRANT = 30 << 20
UPDATE_ROWS = 256
FIRST = 6
GROUP = 4
f32 = jnp.float32
bf16 = jnp.bfloat16
TRANS_B = (((1,), (1,)), ((), ()))
TRANS_A = (((0,), (0,)), ((), ()))


def split(x):
    hi = x.astype(bf16)
    return hi, (x - hi.astype(f32)).astype(bf16)


def dot_nn(ah, al, bh, bl):
    return jnp.dot(
        jnp.concatenate([ah, ah, al], 1), jnp.concatenate([bh, bl, bh], 0), preferred_element_type=f32
    )


def dot_nt(ah, al, bh, bl):
    return lax.dot_general(
        jnp.concatenate([ah, ah, al], 1), jnp.concatenate([bh, bl, bh], 1), TRANS_B, preferred_element_type=f32
    )


def dot_tn(ah, al, bh, bl):
    return lax.dot_general(
        jnp.concatenate([ah, ah, al], 0), jnp.concatenate([bh, bl, bh], 0), TRANS_A, preferred_element_type=f32
    )


def spread(x):
    return jnp.broadcast_to(x, (8, NB))


def tree_sum(xs):
    while len(xs) > 1:
        xs = [xs[i] + xs[i + 1] if i + 1 < len(xs) else xs[i] for i in range(0, len(xs), 2)]
    return xs[0]


def factor_tile(t, rows, cols, lane, sub):
    scaled, ratio, inverses, pivots = [], {}, [], None
    for j in range(8):
        pivot = spread(cols[j][j : j + 1, :])
        inv = 1.0 / pivot
        inverses.append(inv)
        pivots = pivot if j == 0 else jnp.where(sub == j, pivot, pivots)
        for k in range(j + 1, 8):
            entry = spread(cols[k][j : j + 1, :])
            ratio[j, k] = entry * inv
            cols[k] = cols[k] - ((cols[j] * entry) * inv if k == j + 1 else cols[j] * ratio[j, k])
        row = spread(rows[j : j + 1, :]) * inv
        row = jnp.where(lane == 8 * t + j, 1.0 + inv, row)
        scaled.append(row)
        if j < 7:
            rows = rows - jnp.where(sub > j, cols[j], 0.0) * row
    return rows, lax.rsqrt(pivots), scaled, ratio, inverses


def lane_columns(tile, first):
    return [spread(tile[:, first + k : first + k + 1]) for k in range(8)]


def factor_block(tiles):
    tiles = list(tiles)
    n = len(tiles)
    lane = lax.broadcasted_iota(jnp.int32, (8, NB), 1)
    sub = lax.broadcasted_iota(jnp.int32, (8, NB), 0)
    cols = lane_columns(tiles[0], 0)
    uppers, lowers = [], []
    for g in range(0, n, GROUP):
        end = g + GROUP
        window = min(n, end + 1)
        left, right = [], []
        for t in range(g, end):
            last = t + 1 == window
            if not last:
                near = lane_columns(tiles[t + 1], 8 * t)
                ahead = lane_columns(tiles[t + 1], 8 * t + 8)
            far = {i: lane_columns(tiles[i], 8 * t) for i in range(t + 2, window)}
            rows, root, scaled, ratio, inverses = factor_tile(t, tiles[t], cols, lane, sub)
            if not last:
                for j in range(8):
                    part = near[j] * inverses[j]
                    for k in range(j + 1, 8):
                        near[k] = near[k] - near[j] * ratio[j, k]
                    for k in range(8):
                        ahead[k] = ahead[k] - near[j] * spread(part[k : k + 1, :])
                    tiles[t + 1] = tiles[t + 1] - near[j] * scaled[j]
                cols = ahead
            if far:
                back = list(scaled)
                for j in range(6, -1, -1):
                    for k in range(7, j, -1):
                        back[j] = back[j] - ratio[j, k] * back[k]
                for i in far:
                    tiles[i] = tiles[i] - tree_sum([far[i][j] * back[j] for j in range(8)])
            final = rows * root
            diff = lane - sub - 8 * t
            lower = jnp.where(diff < 0, final, jnp.where(diff == 0, root, 0.0))
            uppers.append(jnp.where(diff >= 0, final, 0.0))
            lowers.append(lower)
            left.append(final)
            right.append(jnp.where(lane >= 8 * end, final, lower))
        if window < n:
            change = dot_tn(*split(jnp.concatenate(left, 0)), *split(jnp.concatenate(right, 0)))
            keep = (lane < 8 * g) | (lane >= 8 * end)
            for i in range(window, n):
                tiles[i] = jnp.where(keep, tiles[i], 0.0) - change[8 * i : 8 * i + 8]
    return jnp.concatenate(uppers, 0), jnp.concatenate(lowers, 0)


def half_norms(x):
    xf = x.astype(f32)
    hi, lo = split(xf * xf)
    ones = jnp.ones((NB, x.shape[1]), bf16)
    row = lax.dot_general(ones[:8], hi, TRANS_B, preferred_element_type=f32)
    row = row + lax.dot_general(ones[:8], lo, TRANS_B, preferred_element_type=f32)
    col = lax.dot_general(hi, ones, TRANS_B, preferred_element_type=f32)
    col = col + lax.dot_general(lo, ones, TRANS_B, preferred_element_type=f32)
    return 0.5 * row[0:1], 0.5 * col


def half_norm_col(x):
    xf = x.astype(f32)
    hi, lo = split(xf * xf)
    ones = jnp.ones((NB, x.shape[1]), bf16)
    col = lax.dot_general(hi, ones, TRANS_B, preferred_element_type=f32)
    return 0.5 * (col + lax.dot_general(lo, ones, TRANS_B, preferred_element_type=f32))


def widen(col, width):
    return jnp.concatenate([col] * (width // NB), 1)


def log_row(amp, width):
    return jnp.log(jnp.full((1, width), amp, f32))


def diagonal(n):
    return lax.broadcasted_iota(jnp.int32, (n, n), 0) == lax.broadcasted_iota(jnp.int32, (n, n), 1)


def place(x_ref, base, piece_at, piece, value):
    at = pl.multiple_of(base + piece_at * piece, piece)
    x_ref[pl.ds(at, piece), :] = value


def factor_panels(a_ref, u_ref, wh_ref, wl_ref, row0, count, block):
    n = a_ref.shape[1]
    for p in range(count):
        rows = slice(p * NB, (p + 1) * NB)
        s = row0 + p * NB
        e = s + NB
        d = a_ref[rows, s:e]
        upper, lower = factor_block([d[8 * t : 8 * t + 8] for t in range(NB // 8)])
        u_ref[rows, s:e] = upper
        ih, il = split(lower)
        parts = ([a_ref[rows, :s]] if s else []) + ([a_ref[rows, e:]] if e < n else [])
        row = dot_nn(ih, il, *split(jnp.concatenate(parts, 1)))
        hi, lo = split(row)
        for w_ref, w, diag in ((wh_ref, hi, ih), (wl_ref, lo, il)):
            if s:
                w_ref[rows, :s] = w[:, :s]
            w_ref[rows, s:e] = diag
            end = (s // block + 1) * block
            if e < end:
                w_ref[rows, e:end] = jnp.zeros((NB, end - e), bf16)
        if e == n:
            break
        u_ref[rows, e:] = row[:, s:]
        done_h = jnp.concatenate(([hi[:, :s]] if s else []) + [ih], 1)
        done_l = jnp.concatenate(([lo[:, :s]] if s else []) + [il], 1)
        for i in range(0, n - e, UPDATE_ROWS):
            f = min(i + UPDATE_ROWS, n - e)
            change = dot_tn(
                hi[:, s + i : s + f],
                lo[:, s + i : s + f],
                jnp.concatenate([done_h, hi[:, s + i :]], 1),
                jnp.concatenate([done_l, lo[:, s + i :]], 1),
            )
            q = slice((p + 1) * NB + i, (p + 1) * NB + f)
            if s:
                a_ref[q, :s] = a_ref[q, :s] - change[:, :s]
            a_ref[q, s:e] = -change[:, s:e]
            a_ref[q, e + i :] = a_ref[q, e + i :] - change[:, e:]


def first_kernel(at_ref, amp_ref, mine_ref, other_ref, nz_ref, *refs):
    x_ref, sq_ref, u_ref, wh_ref, wl_ref, rest_ref, a_ref, col_ref = refs
    n = a_ref.shape[0]
    steps, panels, piece = mine_ref.shape[:3]
    block = n // panels
    me = at_ref[1]
    for m in range(steps):
        for s in range(panels):
            place(x_ref, s * block, me ^ (2 * m), piece, mine_ref[m, s])
            place(x_ref, s * block, me ^ (2 * m + 1), piece, other_ref[m, s])
    sq_row, col_ref[...] = half_norms(x_ref[...])
    sq_row = sq_row - log_row(amp_ref[0], n)
    sq_ref[...] = jnp.broadcast_to(sq_row, sq_ref.shape)
    noise = nz_ref[...]
    for o in range(0, n, WB):
        cross = lax.dot_general(x_ref[o : o + WB, :], x_ref[o:, :], TRANS_B, preferred_element_type=f32)
        k = jnp.exp(cross - widen(col_ref[o : o + WB, :], n - o) - sq_row[:, o:])
        a_ref[o : o + WB, o:] = k
        row = noise[o // block : o // block + 1, o % block : o % block + WB]
        a_ref[o : o + WB, o : o + WB] = k[:, :WB] + jnp.where(diagonal(WB), jnp.broadcast_to(row, (WB, WB)), 0.0)
    count = u_ref.shape[0] // NB
    factor_panels(a_ref, u_ref, wh_ref, wl_ref, 0, count, block)
    rest_ref[...] = a_ref[count * NB :, :]


def second_kernel(rest_ref, u_ref, wh_ref, wl_ref, a_ref):
    n1, n = rest_ref.shape
    a_ref[...] = rest_ref[...]
    factor_panels(a_ref, u_ref, wh_ref, wl_ref, n - n1, n1 // NB, n // PANELS)


def store_block(out_ref, a, b, row, ncols, value):
    rows, block = value.shape
    per = block // NB
    for q in range(per):
        at = ((a * block + row) * ncols + b) * per + q
        out_ref[pl.ds(at, rows, stride=ncols * per), :] = value[:, q * NB : (q + 1) * NB]


def bulk_kernel(at_ref, amp_ref, *refs):
    x_ref, sq_ref, u0_ref, wh0_ref, wl0_ref, u1_ref, wh1_ref, wl1_ref, nz_ref = refs[:9]
    refs = refs[9:]
    count = len(refs) - 11
    near_refs, other_ref, out_ref = refs[:count], refs[count], refs[count + 1]
    r_ref, c_ref, kh_ref, kl_ref, ph_ref, pl_ref, zh_ref, zl_ref, col_ref = refs[count + 2 :]
    n = x_ref.shape[0]
    split_at = u0_ref.shape[0]
    nrows, block = nz_ref.shape
    piece = other_ref.shape[2]
    ncols = c_ref.shape[0] // block
    row_at, me, row_n, col_n = at_ref[0], at_ref[1], at_ref[2], at_ref[3]
    for m in range(count):
        for a in range(nrows):
            place(r_ref, a * block, me ^ (2 * m), piece, near_refs[m][a])
            place(r_ref, a * block, me ^ (2 * m + 1), piece, other_ref[m, a])
        for b in range(ncols):
            place(c_ref, b * block, me ^ (2 * m), piece, near_refs[m][nrows + ncols + b])
            place(c_ref, b * block, me ^ (2 * m + 1), piece, other_ref[m, nrows + b])

    def pick(first_ref, second_ref, r0, r1, c0, c1):
        parts = []
        if r0 < split_at:
            parts.append(first_ref[r0 : min(r1, split_at), c0:c1])
        if r1 > split_at:
            parts.append(second_ref[max(r0, split_at) - split_at : r1 - split_at, c0:c1])
        return jnp.concatenate(parts, 0) if len(parts) > 1 else parts[0]

    def inverse(r0, r1, c0, c1):
        return pick(wh0_ref, wh1_ref, r0, r1, c0, c1), pick(wl0_ref, wl1_ref, r0, r1, c0, c1)

    lead_sq = sq_ref[0:1, :]

    def entries(x, col):
        cross = lax.dot_general(x, x_ref[...], TRANS_B, preferred_element_type=f32)
        return split(jnp.exp(cross - widen(col, n) - lead_sq))

    for a in range(nrows):
        rows = slice(a * block, (a + 1) * block)
        col_ref[rows, :] = half_norm_col(r_ref[rows, :])
        kh_ref[rows, :], kl_ref[rows, :] = entries(r_ref[rows, :], col_ref[rows, :])
    for b in range(ncols):
        j = b * col_n + me
        cols = slice(b * block, (b + 1) * block)

        @pl.when(j >= PANELS)
        def _():
            xc = c_ref[cols, :]
            col_sq, col = half_norms(xc)
            col_sq = col_sq - log_row(amp_ref[0], block)
            zh_ref[...], zl_ref[...] = entries(xc, col)
            for s in range(0, n, block):
                e = s + block
                panel = dot_nt(zh_ref[:, :e], zl_ref[:, :e], *inverse(s, e, 0, e))
                ph_ref[:, s:e], pl_ref[:, s:e] = split(panel)
            for s in range(0, n, block):
                e = s + block
                solved = dot_nn(ph_ref[:, s:], pl_ref[:, s:], *inverse(s, n, s, e))
                zh_ref[:, s:e], zl_ref[:, s:e] = split(solved)
            for a in range(nrows):
                i = a * row_n + row_at
                rows = slice(a * block, (a + 1) * block)

                @pl.when(i >= PANELS)
                def _():
                    xr = r_ref[rows, :]
                    cross = lax.dot_general(xr, xc, TRANS_B, preferred_element_type=f32)
                    k = jnp.exp(cross - widen(col_ref[rows, :], block) - col_sq)
                    on_diag = diagonal(block) & (i == j)
                    k = k + jnp.where(on_diag, jnp.broadcast_to(nz_ref[a : a + 1, :], (block, block)), 0.0)
                    k = k - dot_nt(kh_ref[rows, :], kl_ref[rows, :], zh_ref[...], zl_ref[...])
                    store_block(out_ref, a, b, 0, ncols, k)

                @pl.when(i < PANELS)
                def _():
                    store_block(out_ref, a, b, 0, ncols, jnp.zeros((block, block), f32))

        if b:
            continue
        for s in range(PANELS):
            w = s * block
            for a in range(nrows):
                i = a * row_n + row_at
                rows = slice(a * block, (a + 1) * block)

                @pl.when((j == s) & (i >= PANELS))
                def _():
                    e = w + block
                    panel = dot_nt(kh_ref[rows, :e], kl_ref[rows, :e], *inverse(w, e, 0, e))
                    store_block(out_ref, a, b, 0, ncols, panel)

                if a:
                    continue
                for v in range(PANELS):

                    @pl.when((j == s) & (i == v))
                    def _():
                        if v < s:
                            u = jnp.zeros((block, block), f32)
                        else:
                            u = pick(u0_ref, u1_ref, w, w + block, v * block, (v + 1) * block).T
                        if v == s:
                            row_id = lax.broadcasted_iota(jnp.int32, (block, block), 0)
                            col_id = lax.broadcasted_iota(jnp.int32, (block, block), 1)
                            u = jnp.where(row_id >= col_id, u, 0.0)
                        store_block(out_ref, a, b, 0, ncols, u)


SMEM = pl.BlockSpec(memory_space=pltpu.SMEM)
VMEM = pl.BlockSpec(memory_space=pltpu.VMEM)


def exchange(x, axis, k):
    return lax.ppermute(x, axis, [(i, i ^ k) for i in range(lax.axis_size(axis))])


def choose(index, options):
    out = options[0]
    for k in range(1, len(options)):
        out = jnp.where(index == k, options[k], out)
    return out


def local(features, amplitude, noise):
    row_n = lax.axis_size("row")
    col_n = lax.axis_size("col")
    row_at = lax.axis_index("row")
    col_at = lax.axis_index("col")
    nrows, _, piece, width = features.shape
    block = piece * col_n
    ncols = nrows * row_n // col_n
    n = PANELS * block
    mine = features.reshape(nrows, piece, width)
    noise_rows = noise.reshape(nrows, block)
    plane = [mine] + [exchange(mine, "row", k) for k in range(1, row_n)]
    lead = jnp.stack([choose(row_at ^ s, [p[0] for p in plane]) for s in range(PANELS)])
    noise_rows, lead = lax.optimization_barrier((noise_rows, lead))
    near = [lead] + [exchange(lead, "col", k) for k in range(2, col_n, 2)]
    everything, near[1] = lax.optimization_barrier((jnp.stack(plane), near[1]))
    noises = [noise_rows] + [exchange(noise_rows, "row", k) for k in range(1, row_n)]
    lead_noise = jnp.stack([choose(row_at ^ s, [p[0] for p in noises]) for s in range(PANELS)])
    core = col_at & 1

    def parcel(to):
        out = [mine]
        for to_core in (1 - core, core):
            for b in range(ncols):
                number = b * col_n + (to & ~1) + to_core
                at = (row_at ^ (number & (row_n - 1)), number // row_n, 0, 0)
                out.append(lax.dynamic_slice(everything, at, (1, 1, piece, width)).reshape(1, piece, width))
        return jnp.concatenate(out, 0)

    parcels = [parcel(col_at)] + [exchange(parcel(col_at ^ k), "col", k) for k in range(2, col_n, 2)]
    near = jnp.stack(near)
    other = exchange(near, "col", 1)
    at = jnp.stack([row_at, col_at, jnp.int32(row_n), jnp.int32(col_n)])
    first = FIRST * n // NB // 8 * NB
    n1 = n - first
    params = pltpu.CompilerParams(vmem_limit_bytes=GRANT)
    cost = pl.CostEstimate(flops=20_000_000_000, bytes_accessed=8_000_000, transcendentals=0)

    def factor_shapes(rows):
        half = jax.ShapeDtypeStruct((rows, n), bf16)
        return [jax.ShapeDtypeStruct((rows, n), f32), half, half]

    points, lead_sq, u0, wh0, wl0, rest = pl.pallas_call(
        first_kernel,
        out_shape=[jax.ShapeDtypeStruct((n, width), bf16), jax.ShapeDtypeStruct((8, n), f32)]
        + factor_shapes(first)
        + [jax.ShapeDtypeStruct((n1, n), f32)],
        in_specs=[SMEM, SMEM, VMEM, VMEM, VMEM],
        out_specs=[VMEM] * 6,
        scratch_shapes=[pltpu.VMEM((n, n), f32), pltpu.VMEM((n, NB), f32)],
        compiler_params=params,
        cost_estimate=pl.CostEstimate(flops=1_000_000, bytes_accessed=1_000_000, transcendentals=0),
        name="first",
    )(at, amplitude, near, other, lead_noise)
    parcels, rest = lax.optimization_barrier((parcels, rest))
    passed = exchange(jnp.stack([p[: nrows + ncols] for p in parcels]), "col", 1)
    u1, wh1, wl1 = pl.pallas_call(
        second_kernel,
        out_shape=factor_shapes(n1),
        in_specs=[VMEM],
        out_specs=[VMEM] * 3,
        scratch_shapes=[pltpu.VMEM((n1, n), f32)],
        compiler_params=params,
        cost_estimate=cost,
        name="second",
    )(rest)
    half = pltpu.VMEM((block, n), bf16)
    tall = pltpu.VMEM((nrows * block, n), bf16)
    out = pl.pallas_call(
        bulk_kernel,
        out_shape=jax.ShapeDtypeStruct((nrows * block * ncols * (block // NB), NB), f32),
        in_specs=[SMEM, SMEM] + [VMEM] * (10 + len(parcels)),
        out_specs=VMEM,
        scratch_shapes=[
            pltpu.VMEM((nrows * block, width), bf16),
            pltpu.VMEM((ncols * block, width), bf16),
            tall,
            tall,
            half,
            half,
            half,
            half,
            pltpu.VMEM((nrows * block, NB), f32),
        ],
        compiler_params=params,
        cost_estimate=cost,
        name="bulk",
    )(at, amplitude, points, lead_sq, u0, wh0, wl0, u1, wh1, wl1, noise_rows, *parcels, passed)
    return out.reshape(nrows, 1, block, ncols, 1, block)


def solution(mesh):
    return jax.shard_map(
        local,
        mesh=mesh,
        in_specs=(P(None, "row", "col", None), P(), P(None, "row", None)),
        out_specs=P(None, "row", None, None, "col", None),
        check_vma=False,
    )
```

```python
import functools

import jax
import jax.numpy as jnp
from jax import lax
from jax.experimental import pallas as pl
from jax.experimental.pallas import tpu as pltpu
from jax.sharding import PartitionSpec as P

PANELS = 2
NB = 128
WB = 256
GRANT = 30 << 20
UPDATE_ROWS = 256
FIRST = 6
GROUP = 4
f32 = jnp.float32
bf16 = jnp.bfloat16
TRANS_B = (((1,), (1,)), ((), ()))
TRANS_A = (((0,), (0,)), ((), ()))


def split(x):
    hi = x.astype(bf16)
    return hi, (x - hi.astype(f32)).astype(bf16)


def dot_nn(ah, al, bh, bl):
    return jnp.dot(
        jnp.concatenate([ah, ah, al], 1), jnp.concatenate([bh, bl, bh], 0), preferred_element_type=f32
    )


def dot_nt(ah, al, bh, bl):
    return lax.dot_general(
        jnp.concatenate([ah, ah, al], 1), jnp.concatenate([bh, bl, bh], 1), TRANS_B, preferred_element_type=f32
    )


def dot_tn(ah, al, bh, bl):
    return lax.dot_general(
        jnp.concatenate([ah, ah, al], 0), jnp.concatenate([bh, bl, bh], 0), TRANS_A, preferred_element_type=f32
    )


def spread(x):
    return jnp.broadcast_to(x, (8, NB))


def tree_sum(xs):
    while len(xs) > 1:
        xs = [xs[i] + xs[i + 1] if i + 1 < len(xs) else xs[i] for i in range(0, len(xs), 2)]
    return xs[0]


def factor_tile(t, rows, cols, lane, sub):
    scaled, ratio, inverses, pivots = [], {}, [], None
    for j in range(8):
        pivot = spread(cols[j][j : j + 1, :])
        inv = 1.0 / pivot
        inverses.append(inv)
        pivots = pivot if j == 0 else jnp.where(sub == j, pivot, pivots)
        for k in range(j + 1, 8):
            entry = spread(cols[k][j : j + 1, :])
            ratio[j, k] = entry * inv
            cols[k] = cols[k] - ((cols[j] * entry) * inv if k == j + 1 else cols[j] * ratio[j, k])
        row = spread(rows[j : j + 1, :]) * inv
        row = jnp.where(lane == 8 * t + j, 1.0 + inv, row)
        scaled.append(row)
        if j < 7:
            rows = rows - jnp.where(sub > j, cols[j], 0.0) * row
    return rows, lax.rsqrt(pivots), scaled, ratio, inverses


def lane_columns(tile, first):
    return [spread(tile[:, first + k : first + k + 1]) for k in range(8)]


def factor_block(tiles):
    tiles = list(tiles)
    n = len(tiles)
    lane = lax.broadcasted_iota(jnp.int32, (8, NB), 1)
    sub = lax.broadcasted_iota(jnp.int32, (8, NB), 0)
    cols = lane_columns(tiles[0], 0)
    uppers, lowers = [], []
    for g in range(0, n, GROUP):
        end = g + GROUP
        window = min(n, end + 1)
        left, right = [], []
        for t in range(g, end):
            last = t + 1 == window
            if not last:
                near = lane_columns(tiles[t + 1], 8 * t)
                ahead = lane_columns(tiles[t + 1], 8 * t + 8)
            far = {i: lane_columns(tiles[i], 8 * t) for i in range(t + 2, window)}
            rows, root, scaled, ratio, inverses = factor_tile(t, tiles[t], cols, lane, sub)
            if not last:
                for j in range(8):
                    part = near[j] * inverses[j]
                    for k in range(j + 1, 8):
                        near[k] = near[k] - near[j] * ratio[j, k]
                    for k in range(8):
                        ahead[k] = ahead[k] - near[j] * spread(part[k : k + 1, :])
                    tiles[t + 1] = tiles[t + 1] - near[j] * scaled[j]
                cols = ahead
            if far:
                back = list(scaled)
                for j in range(6, -1, -1):
                    for k in range(7, j, -1):
                        back[j] = back[j] - ratio[j, k] * back[k]
                for i in far:
                    tiles[i] = tiles[i] - tree_sum([far[i][j] * back[j] for j in range(8)])
            final = rows * root
            diff = lane - sub - 8 * t
            lower = jnp.where(diff < 0, final, jnp.where(diff == 0, root, 0.0))
            uppers.append(jnp.where(diff >= 0, final, 0.0))
            lowers.append(lower)
            left.append(final)
            right.append(jnp.where(lane >= 8 * end, final, lower))
        if window < n:
            change = dot_tn(*split(jnp.concatenate(left, 0)), *split(jnp.concatenate(right, 0)))
            keep = (lane < 8 * g) | (lane >= 8 * end)
            for i in range(window, n):
                tiles[i] = jnp.where(keep, tiles[i], 0.0) - change[8 * i : 8 * i + 8]
    return jnp.concatenate(uppers, 0), jnp.concatenate(lowers, 0)


def half_norms(x):
    xf = x.astype(f32)
    hi, lo = split(xf * xf)
    ones = jnp.ones((NB, x.shape[1]), bf16)
    row = lax.dot_general(ones[:8], hi, TRANS_B, preferred_element_type=f32)
    row = row + lax.dot_general(ones[:8], lo, TRANS_B, preferred_element_type=f32)
    col = lax.dot_general(hi, ones, TRANS_B, preferred_element_type=f32)
    col = col + lax.dot_general(lo, ones, TRANS_B, preferred_element_type=f32)
    return 0.5 * row[0:1], 0.5 * col


def half_norm_col(x):
    xf = x.astype(f32)
    hi, lo = split(xf * xf)
    ones = jnp.ones((NB, x.shape[1]), bf16)
    col = lax.dot_general(hi, ones, TRANS_B, preferred_element_type=f32)
    return 0.5 * (col + lax.dot_general(lo, ones, TRANS_B, preferred_element_type=f32))


def widen(col, width):
    return jnp.concatenate([col] * (width // NB), 1)


def log_row(amp, width):
    return jnp.log(jnp.full((1, width), amp, f32))


def diagonal(n):
    return lax.broadcasted_iota(jnp.int32, (n, n), 0) == lax.broadcasted_iota(jnp.int32, (n, n), 1)


def place(x_ref, base, piece_at, piece, value):
    at = pl.multiple_of(base + piece_at * piece, piece)
    x_ref[pl.ds(at, piece), :] = value


def factor_panels(a_ref, u_ref, wh_ref, wl_ref, row0, count, block):
    n = a_ref.shape[1]
    for p in range(count):
        rows = slice(p * NB, (p + 1) * NB)
        s = row0 + p * NB
        e = s + NB
        d = a_ref[rows, s:e]
        upper, lower = factor_block([d[8 * t : 8 * t + 8] for t in range(NB // 8)])
        u_ref[rows, s:e] = upper
        ih, il = split(lower)
        parts = ([a_ref[rows, :s]] if s else []) + ([a_ref[rows, e:]] if e < n else [])
        row = dot_nn(ih, il, *split(jnp.concatenate(parts, 1)))
        hi, lo = split(row)
        for w_ref, w, diag in ((wh_ref, hi, ih), (wl_ref, lo, il)):
            if s:
                w_ref[rows, :s] = w[:, :s]
            w_ref[rows, s:e] = diag
            end = (s // block + 1) * block
            if e < end:
                w_ref[rows, e:end] = jnp.zeros((NB, end - e), bf16)
        if e == n:
            break
        u_ref[rows, e:] = row[:, s:]
        done_h = jnp.concatenate(([hi[:, :s]] if s else []) + [ih], 1)
        done_l = jnp.concatenate(([lo[:, :s]] if s else []) + [il], 1)
        for i in range(0, n - e, UPDATE_ROWS):
            f = min(i + UPDATE_ROWS, n - e)
            change = dot_tn(
                hi[:, s + i : s + f],
                lo[:, s + i : s + f],
                jnp.concatenate([done_h, hi[:, s + i :]], 1),
                jnp.concatenate([done_l, lo[:, s + i :]], 1),
            )
            q = slice((p + 1) * NB + i, (p + 1) * NB + f)
            if s:
                a_ref[q, :s] = a_ref[q, :s] - change[:, :s]
            a_ref[q, s:e] = -change[:, s:e]
            a_ref[q, e + i :] = a_ref[q, e + i :] - change[:, e:]


def first_kernel(at_ref, amp_ref, mine_ref, other_ref, nz_ref, *refs):
    x_ref, sq_ref, u_ref, wh_ref, wl_ref, rest_ref, a_ref, col_ref = refs
    n = a_ref.shape[0]
    steps, panels, piece = mine_ref.shape[:3]
    block = n // panels
    me = at_ref[1]
    for m in range(steps):
        for s in range(panels):
            place(x_ref, s * block, me ^ (2 * m), piece, mine_ref[m, s])
            place(x_ref, s * block, me ^ (2 * m + 1), piece, other_ref[m, s])
    sq_row, col_ref[...] = half_norms(x_ref[...])
    sq_row = sq_row - log_row(amp_ref[0], n)
    sq_ref[...] = jnp.broadcast_to(sq_row, sq_ref.shape)
    noise = nz_ref[...]
    for o in range(0, n, WB):
        cross = lax.dot_general(x_ref[o : o + WB, :], x_ref[o:, :], TRANS_B, preferred_element_type=f32)
        k = jnp.exp(cross - widen(col_ref[o : o + WB, :], n - o) - sq_row[:, o:])
        a_ref[o : o + WB, o:] = k
        row = noise[o // block : o // block + 1, o % block : o % block + WB]
        a_ref[o : o + WB, o : o + WB] = k[:, :WB] + jnp.where(diagonal(WB), jnp.broadcast_to(row, (WB, WB)), 0.0)
    count = u_ref.shape[0] // NB
    factor_panels(a_ref, u_ref, wh_ref, wl_ref, 0, count, block)
    rest_ref[...] = a_ref[count * NB :, :]


def second_kernel(rest_ref, u_ref, wh_ref, wl_ref, a_ref):
    n1, n = rest_ref.shape
    a_ref[...] = rest_ref[...]
    factor_panels(a_ref, u_ref, wh_ref, wl_ref, n - n1, n1 // NB, n // PANELS)


def store_block(out_ref, a, b, row, ncols, value):
    rows, block = value.shape
    per = block // NB
    for q in range(per):
        at = ((a * block + row) * ncols + b) * per + q
        out_ref[pl.ds(at, rows, stride=ncols * per), :] = value[:, q * NB : (q + 1) * NB]


def bulk_kernel(at_ref, amp_ref, *refs):
    x_ref, sq_ref, u0_ref, wh0_ref, wl0_ref, u1_ref, wh1_ref, wl1_ref, nz_ref = refs[:9]
    refs = refs[9:]
    count = len(refs) - 11
    near_refs, other_ref, out_ref = refs[:count], refs[count], refs[count + 1]
    r_ref, c_ref, kh_ref, kl_ref, ph_ref, pl_ref, zh_ref, zl_ref, col_ref = refs[count + 2 :]
    n = x_ref.shape[0]
    split_at = u0_ref.shape[0]
    nrows, block = nz_ref.shape
    piece = other_ref.shape[2]
    ncols = c_ref.shape[0] // block
    row_at, me, row_n, col_n = at_ref[0], at_ref[1], at_ref[2], at_ref[3]
    for m in range(count):
        for a in range(nrows):
            place(r_ref, a * block, me ^ (2 * m), piece, near_refs[m][a])
            place(r_ref, a * block, me ^ (2 * m + 1), piece, other_ref[m, a])
        for b in range(ncols):
            place(c_ref, b * block, me ^ (2 * m), piece, near_refs[m][nrows + ncols + b])
            place(c_ref, b * block, me ^ (2 * m + 1), piece, other_ref[m, nrows + b])

    def pick(first_ref, second_ref, r0, r1, c0, c1):
        parts = []
        if r0 < split_at:
            parts.append(first_ref[r0 : min(r1, split_at), c0:c1])
        if r1 > split_at:
            parts.append(second_ref[max(r0, split_at) - split_at : r1 - split_at, c0:c1])
        return jnp.concatenate(parts, 0) if len(parts) > 1 else parts[0]

    def inverse(r0, r1, c0, c1):
        return pick(wh0_ref, wh1_ref, r0, r1, c0, c1), pick(wl0_ref, wl1_ref, r0, r1, c0, c1)

    lead_sq = sq_ref[0:1, :]

    def entries(x, col):
        cross = lax.dot_general(x, x_ref[...], TRANS_B, preferred_element_type=f32)
        return split(jnp.exp(cross - widen(col, n) - lead_sq))

    def row_entries():
        for a in range(nrows):
            rows = slice(a * block, (a + 1) * block)
            col_ref[rows, :] = half_norm_col(r_ref[rows, :])
            kh_ref[rows, :], kl_ref[rows, :] = entries(r_ref[rows, :], col_ref[rows, :])

    for b in range(ncols):
        j = b * col_n + me
        cols = slice(b * block, (b + 1) * block)

        @pl.when(j >= PANELS)
        def _():
            xc = c_ref[cols, :]
            col_sq, col = half_norms(xc)
            col_sq = col_sq - log_row(amp_ref[0], block)
            zh_ref[...], zl_ref[...] = entries(xc, col)
            row_entries()
            for s in range(0, n, block):
                e = s + block
                panel = dot_nt(zh_ref[:, :e], zl_ref[:, :e], *inverse(s, e, 0, e))
                ph_ref[:, s:e], pl_ref[:, s:e] = split(panel)
            for s in range(0, n, block):
                e = s + block
                solved = dot_nn(ph_ref[:, s:], pl_ref[:, s:], *inverse(s, n, s, e))
                zh_ref[:, s:e], zl_ref[:, s:e] = split(solved)
            for a in range(nrows):
                i = a * row_n + row_at
                rows = slice(a * block, (a + 1) * block)
                cross = lax.dot_general(r_ref[rows, :], xc, TRANS_B, preferred_element_type=f32)
                k = jnp.exp(cross - widen(col_ref[rows, :], block) - col_sq)
                on_diag = diagonal(block) & (i == j)
                k = k + jnp.where(on_diag, jnp.broadcast_to(nz_ref[a : a + 1, :], (block, block)), 0.0)
                k = k - dot_nt(kh_ref[rows, :], kl_ref[rows, :], zh_ref[...], zl_ref[...])
                store_block(out_ref, a, b, 0, ncols, jnp.where(i >= PANELS, k, 0.0))

        if b:
            continue

        @pl.when(j < PANELS)
        def _():
            def some_entries(step, carry):
                o = pl.multiple_of(step * WB, WB)
                x = r_ref[pl.ds(o, WB), :]
                kh_ref[pl.ds(o, WB), :], kl_ref[pl.ds(o, WB), :] = entries(x, half_norm_col(x))
                return carry

            lax.fori_loop(0, nrows * block // WB, some_entries, 0)

        for s in range(PANELS):
            w = s * block
            e = w + block

            @pl.when(j == s)
            def _():
                def some_rows(step, carry):
                    o = pl.multiple_of(step * WB, WB)
                    rows = pl.ds(o, WB)
                    panel = dot_nt(kh_ref[rows, :e], kl_ref[rows, :e], *inverse(w, e, 0, e))
                    store_block(out_ref, 0, b, o, ncols, panel)
                    return carry

                lax.fori_loop(0, nrows * block // WB, some_rows, 0)

            for v in range(PANELS):

                @pl.when((j == s) & (row_at == v))
                def _():
                    if v < s:
                        u = jnp.zeros((block, block), f32)
                    else:
                        u = pick(u0_ref, u1_ref, w, e, v * block, (v + 1) * block).T
                    if v == s:
                        row_id = lax.broadcasted_iota(jnp.int32, (block, block), 0)
                        col_id = lax.broadcasted_iota(jnp.int32, (block, block), 1)
                        u = jnp.where(row_id >= col_id, u, 0.0)
                    store_block(out_ref, 0, b, 0, ncols, u)


SMEM = pl.BlockSpec(memory_space=pltpu.SMEM)
VMEM = pl.BlockSpec(memory_space=pltpu.VMEM)


def exchange(x, axis, k):
    return lax.ppermute(x, axis, [(i, i ^ k) for i in range(lax.axis_size(axis))])


def choose(index, options):
    out = options[0]
    for k in range(1, len(options)):
        out = jnp.where(index == k, options[k], out)
    return out


def local(features, amplitude, noise):
    row_n = lax.axis_size("row")
    col_n = lax.axis_size("col")
    row_at = lax.axis_index("row")
    col_at = lax.axis_index("col")
    nrows, _, piece, width = features.shape
    block = piece * col_n
    ncols = nrows * row_n // col_n
    n = PANELS * block
    mine = features.reshape(nrows, piece, width)
    noise_rows = noise.reshape(nrows, block)
    plane = [mine] + [exchange(mine, "row", k) for k in range(1, row_n)]
    lead = jnp.stack([choose(row_at ^ s, [p[0] for p in plane]) for s in range(PANELS)])
    noise_rows, lead = lax.optimization_barrier((noise_rows, lead))
    near = [lead] + [exchange(lead, "col", k) for k in range(2, col_n, 2)]
    everything, near[1] = lax.optimization_barrier((jnp.stack(plane), near[1]))
    noises = [noise_rows] + [exchange(noise_rows, "row", k) for k in range(1, row_n)]
    lead_noise = jnp.stack([choose(row_at ^ s, [p[0] for p in noises]) for s in range(PANELS)])
    core = col_at & 1

    def parcel(to):
        out = [mine]
        for to_core in (1 - core, core):
            for b in range(ncols):
                number = b * col_n + (to & ~1) + to_core
                at = (row_at ^ (number & (row_n - 1)), number // row_n, 0, 0)
                out.append(lax.dynamic_slice(everything, at, (1, 1, piece, width)).reshape(1, piece, width))
        return jnp.concatenate(out, 0)

    parcels = [parcel(col_at)] + [exchange(parcel(col_at ^ k), "col", k) for k in range(2, col_n, 2)]
    near = jnp.stack(near)
    other = exchange(near, "col", 1)
    at = jnp.stack([row_at, col_at, jnp.int32(row_n), jnp.int32(col_n)])
    first = FIRST * n // NB // 8 * NB
    n1 = n - first
    params = pltpu.CompilerParams(vmem_limit_bytes=GRANT)
    cost = pl.CostEstimate(flops=20_000_000_000, bytes_accessed=8_000_000, transcendentals=0)

    def factor_shapes(rows):
        half = jax.ShapeDtypeStruct((rows, n), bf16)
        return [jax.ShapeDtypeStruct((rows, n), f32), half, half]

    points, lead_sq, u0, wh0, wl0, rest = pl.pallas_call(
        first_kernel,
        out_shape=[jax.ShapeDtypeStruct((n, width), bf16), jax.ShapeDtypeStruct((8, n), f32)]
        + factor_shapes(first)
        + [jax.ShapeDtypeStruct((n1, n), f32)],
        in_specs=[SMEM, SMEM, VMEM, VMEM, VMEM],
        out_specs=[VMEM] * 6,
        scratch_shapes=[pltpu.VMEM((n, n), f32), pltpu.VMEM((n, NB), f32)],
        compiler_params=params,
        cost_estimate=pl.CostEstimate(flops=1_000_000, bytes_accessed=1_000_000, transcendentals=0),
        name="first",
    )(at, amplitude, near, other, lead_noise)
    parcels, rest = lax.optimization_barrier((parcels, rest))
    passed = exchange(jnp.stack([p[: nrows + ncols] for p in parcels]), "col", 1)
    u1, wh1, wl1 = pl.pallas_call(
        second_kernel,
        out_shape=factor_shapes(n1),
        in_specs=[VMEM],
        out_specs=[VMEM] * 3,
        scratch_shapes=[pltpu.VMEM((n1, n), f32)],
        compiler_params=params,
        cost_estimate=cost,
        name="second",
    )(rest)
    half = pltpu.VMEM((block, n), bf16)
    tall = pltpu.VMEM((nrows * block, n), bf16)
    out = pl.pallas_call(
        bulk_kernel,
        out_shape=jax.ShapeDtypeStruct((nrows * block * ncols * (block // NB), NB), f32),
        in_specs=[SMEM, SMEM] + [VMEM] * (10 + len(parcels)),
        out_specs=VMEM,
        scratch_shapes=[
            pltpu.VMEM((nrows * block, width), bf16),
            pltpu.VMEM((ncols * block, width), bf16),
            tall,
            tall,
            half,
            half,
            half,
            half,
            pltpu.VMEM((nrows * block, NB), f32),
        ],
        compiler_params=params,
        cost_estimate=cost,
        name="bulk",
    )(at, amplitude, points, lead_sq, u0, wh0, wl0, u1, wh1, wl1, noise_rows, *parcels, passed)
    return out.reshape(nrows, 1, block, ncols, 1, block)


def solution(mesh):
    return jax.shard_map(
        local,
        mesh=mesh,
        in_specs=(P(None, "row", "col", None), P(), P(None, "row", None)),
        out_specs=P(None, "row", None, None, "col", None),
        check_vma=False,
    )
```

```python
import functools

import jax
import jax.numpy as jnp
from jax import lax
from jax.experimental import pallas as pl
from jax.experimental.pallas import tpu as pltpu
from jax.sharding import PartitionSpec as P

PANELS = 2
NB = 128
WB = 256
GRANT = 30 << 20
UPDATE_ROWS = 256
FIRST = 6
GROUP = 4
f32 = jnp.float32
bf16 = jnp.bfloat16
TRANS_B = (((1,), (1,)), ((), ()))
TRANS_A = (((0,), (0,)), ((), ()))


def split(x):
    hi = x.astype(bf16)
    return hi, (x - hi.astype(f32)).astype(bf16)


def dot_nn(ah, al, bh, bl):
    return jnp.dot(
        jnp.concatenate([ah, ah, al], 1), jnp.concatenate([bh, bl, bh], 0), preferred_element_type=f32
    )


def dot_nt(ah, al, bh, bl):
    return lax.dot_general(
        jnp.concatenate([ah, ah, al], 1), jnp.concatenate([bh, bl, bh], 1), TRANS_B, preferred_element_type=f32
    )


def dot_tn(ah, al, bh, bl):
    return lax.dot_general(
        jnp.concatenate([ah, ah, al], 0), jnp.concatenate([bh, bl, bh], 0), TRANS_A, preferred_element_type=f32
    )


def spread(x):
    return jnp.broadcast_to(x, (8, NB))


def tree_sum(xs):
    while len(xs) > 1:
        xs = [xs[i] + xs[i + 1] if i + 1 < len(xs) else xs[i] for i in range(0, len(xs), 2)]
    return xs[0]


def factor_tile(t, rows, cols, lane, sub):
    scaled, ratio, inverses, pivots = [], {}, [], None
    for j in range(8):
        pivot = spread(cols[j][j : j + 1, :])
        inv = 1.0 / pivot
        inverses.append(inv)
        pivots = pivot if j == 0 else jnp.where(sub == j, pivot, pivots)
        for k in range(j + 1, 8):
            entry = spread(cols[k][j : j + 1, :])
            ratio[j, k] = entry * inv
            cols[k] = cols[k] - ((cols[j] * entry) * inv if k == j + 1 else cols[j] * ratio[j, k])
        row = spread(rows[j : j + 1, :]) * inv
        row = jnp.where(lane == 8 * t + j, 1.0 + inv, row)
        scaled.append(row)
        if j < 7:
            rows = rows - jnp.where(sub > j, cols[j], 0.0) * row
    return rows, lax.rsqrt(pivots), scaled, ratio, inverses


def lane_columns(tile, first):
    return [spread(tile[:, first + k : first + k + 1]) for k in range(8)]


def factor_block(tiles):
    tiles = list(tiles)
    n = len(tiles)
    lane = lax.broadcasted_iota(jnp.int32, (8, NB), 1)
    sub = lax.broadcasted_iota(jnp.int32, (8, NB), 0)
    cols = lane_columns(tiles[0], 0)
    uppers, lowers = [], []
    for g in range(0, n, GROUP):
        end = g + GROUP
        window = min(n, end + 1)
        left, right = [], []
        for t in range(g, end):
            last = t + 1 == window
            if not last:
                near = lane_columns(tiles[t + 1], 8 * t)
                ahead = lane_columns(tiles[t + 1], 8 * t + 8)
            far = {i: lane_columns(tiles[i], 8 * t) for i in range(t + 2, window)}
            rows, root, scaled, ratio, inverses = factor_tile(t, tiles[t], cols, lane, sub)
            if not last:
                for j in range(8):
                    part = near[j] * inverses[j]
                    for k in range(j + 1, 8):
                        near[k] = near[k] - near[j] * ratio[j, k]
                    for k in range(8):
                        ahead[k] = ahead[k] - near[j] * spread(part[k : k + 1, :])
                    tiles[t + 1] = tiles[t + 1] - near[j] * scaled[j]
                cols = ahead
            if far:
                back = list(scaled)
                for j in range(6, -1, -1):
                    for k in range(7, j, -1):
                        back[j] = back[j] - ratio[j, k] * back[k]
                for i in far:
                    tiles[i] = tiles[i] - tree_sum([far[i][j] * back[j] for j in range(8)])
            final = rows * root
            diff = lane - sub - 8 * t
            lower = jnp.where(diff < 0, final, jnp.where(diff == 0, root, 0.0))
            uppers.append(jnp.where(diff >= 0, final, 0.0))
            lowers.append(lower)
            left.append(final)
            right.append(jnp.where(lane >= 8 * end, final, lower))
        if window < n:
            change = dot_tn(*split(jnp.concatenate(left, 0)), *split(jnp.concatenate(right, 0)))
            keep = (lane < 8 * g) | (lane >= 8 * end)
            for i in range(window, n):
                tiles[i] = jnp.where(keep, tiles[i], 0.0) - change[8 * i : 8 * i + 8]
    return jnp.concatenate(uppers, 0), jnp.concatenate(lowers, 0)


def half_norms(x):
    xf = x.astype(f32)
    hi, lo = split(xf * xf)
    ones = jnp.ones((NB, x.shape[1]), bf16)
    row = lax.dot_general(ones[:8], hi, TRANS_B, preferred_element_type=f32)
    row = row + lax.dot_general(ones[:8], lo, TRANS_B, preferred_element_type=f32)
    col = lax.dot_general(hi, ones, TRANS_B, preferred_element_type=f32)
    col = col + lax.dot_general(lo, ones, TRANS_B, preferred_element_type=f32)
    return 0.5 * row[0:1], 0.5 * col


def half_norm_col(x):
    xf = x.astype(f32)
    hi, lo = split(xf * xf)
    ones = jnp.ones((NB, x.shape[1]), bf16)
    col = lax.dot_general(hi, ones, TRANS_B, preferred_element_type=f32)
    return 0.5 * (col + lax.dot_general(lo, ones, TRANS_B, preferred_element_type=f32))


def widen(col, width):
    return jnp.concatenate([col] * (width // NB), 1)


def log_row(amp, width):
    return jnp.log(jnp.full((1, width), amp, f32))


def diagonal(n):
    return lax.broadcasted_iota(jnp.int32, (n, n), 0) == lax.broadcasted_iota(jnp.int32, (n, n), 1)


def place(x_ref, base, piece_at, piece, value):
    at = pl.multiple_of(base + piece_at * piece, piece)
    x_ref[pl.ds(at, piece), :] = value


def factor_panels(a_ref, u_ref, wh_ref, wl_ref, row0, count, block):
    n = a_ref.shape[1]
    for p in range(count):
        rows = slice(p * NB, (p + 1) * NB)
        s = row0 + p * NB
        e = s + NB
        d = a_ref[rows, s:e]
        upper, lower = factor_block([d[8 * t : 8 * t + 8] for t in range(NB // 8)])
        u_ref[rows, s:e] = upper
        ih, il = split(lower)
        parts = ([a_ref[rows, :s]] if s else []) + ([a_ref[rows, e:]] if e < n else [])
        row = dot_nn(ih, il, *split(jnp.concatenate(parts, 1)))
        hi, lo = split(row)
        for w_ref, w, diag in ((wh_ref, hi, ih), (wl_ref, lo, il)):
            if s:
                w_ref[rows, :s] = w[:, :s]
            w_ref[rows, s:e] = diag
            end = (s // block + 1) * block
            if e < end:
                w_ref[rows, e:end] = jnp.zeros((NB, end - e), bf16)
        if e == n:
            break
        u_ref[rows, e:] = row[:, s:]
        done_h = jnp.concatenate(([hi[:, :s]] if s else []) + [ih], 1)
        done_l = jnp.concatenate(([lo[:, :s]] if s else []) + [il], 1)
        for i in range(0, n - e, UPDATE_ROWS):
            f = min(i + UPDATE_ROWS, n - e)
            change = dot_tn(
                hi[:, s + i : s + f],
                lo[:, s + i : s + f],
                jnp.concatenate([done_h, hi[:, s + i :]], 1),
                jnp.concatenate([done_l, lo[:, s + i :]], 1),
            )
            q = slice((p + 1) * NB + i, (p + 1) * NB + f)
            if s:
                a_ref[q, :s] = a_ref[q, :s] - change[:, :s]
            a_ref[q, s:e] = -change[:, s:e]
            a_ref[q, e + i :] = a_ref[q, e + i :] - change[:, e:]


def first_kernel(at_ref, amp_ref, mine_ref, other_ref, nz_ref, *refs):
    x_ref, sq_ref, u_ref, wh_ref, wl_ref, rest_ref, a_ref, col_ref = refs
    n = a_ref.shape[0]
    steps, panels, piece = mine_ref.shape[:3]
    block = n // panels
    me = at_ref[1]
    for m in range(steps):
        for s in range(panels):
            place(x_ref, s * block, me ^ (2 * m), piece, mine_ref[m, s])
            place(x_ref, s * block, me ^ (2 * m + 1), piece, other_ref[m, s])
    sq_row, col_ref[...] = half_norms(x_ref[...])
    sq_row = sq_row - log_row(amp_ref[0], n)
    sq_ref[...] = jnp.broadcast_to(sq_row, sq_ref.shape)
    noise = nz_ref[...]
    for o in range(0, n, WB):
        cross = lax.dot_general(x_ref[o : o + WB, :], x_ref[o:, :], TRANS_B, preferred_element_type=f32)
        k = jnp.exp(cross - widen(col_ref[o : o + WB, :], n - o) - sq_row[:, o:])
        a_ref[o : o + WB, o:] = k
        row = noise[o // block : o // block + 1, o % block : o % block + WB]
        a_ref[o : o + WB, o : o + WB] = k[:, :WB] + jnp.where(diagonal(WB), jnp.broadcast_to(row, (WB, WB)), 0.0)
    count = u_ref.shape[0] // NB
    factor_panels(a_ref, u_ref, wh_ref, wl_ref, 0, count, block)
    rest_ref[...] = a_ref[count * NB :, :]


def second_kernel(rest_ref, u_ref, wh_ref, wl_ref, a_ref):
    n1, n = rest_ref.shape
    a_ref[...] = rest_ref[...]
    factor_panels(a_ref, u_ref, wh_ref, wl_ref, n - n1, n1 // NB, n // PANELS)


def store_block(out_ref, a, b, row, ncols, value):
    rows, block = value.shape
    per = block // NB
    for q in range(per):
        at = ((a * block + row) * ncols + b) * per + q
        out_ref[pl.ds(at, rows, stride=ncols * per), :] = value[:, q * NB : (q + 1) * NB]


def bulk_kernel(at_ref, amp_ref, *refs):
    x_ref, sq_ref, u0_ref, wh0_ref, wl0_ref, u1_ref, wh1_ref, wl1_ref, nz_ref = refs[:9]
    refs = refs[9:]
    count = len(refs) - 11
    near_refs, other_ref, out_ref = refs[:count], refs[count], refs[count + 1]
    r_ref, c_ref, kh_ref, kl_ref, ph_ref, pl_ref, zh_ref, zl_ref, col_ref = refs[count + 2 :]
    n = x_ref.shape[0]
    split_at = u0_ref.shape[0]
    nrows, block = nz_ref.shape
    piece = other_ref.shape[2]
    ncols = c_ref.shape[0] // block
    row_at, me, row_n, col_n = at_ref[0], at_ref[1], at_ref[2], at_ref[3]
    for m in range(count):
        for a in range(nrows):
            place(r_ref, a * block, me ^ (2 * m), piece, near_refs[m][a])
            place(r_ref, a * block, me ^ (2 * m + 1), piece, other_ref[m, a])
        for b in range(ncols):
            place(c_ref, b * block, me ^ (2 * m), piece, near_refs[m][nrows + ncols + b])
            place(c_ref, b * block, me ^ (2 * m + 1), piece, other_ref[m, nrows + b])

    def pick(first_ref, second_ref, r0, r1, c0, c1):
        parts = []
        if r0 < split_at:
            parts.append(first_ref[r0 : min(r1, split_at), c0:c1])
        if r1 > split_at:
            parts.append(second_ref[max(r0, split_at) - split_at : r1 - split_at, c0:c1])
        return jnp.concatenate(parts, 0) if len(parts) > 1 else parts[0]

    def inverse(r0, r1, c0, c1):
        return pick(wh0_ref, wh1_ref, r0, r1, c0, c1), pick(wl0_ref, wl1_ref, r0, r1, c0, c1)

    lead_sq = sq_ref[0:1, :]

    def entries(x, col):
        cross = lax.dot_general(x, x_ref[...], TRANS_B, preferred_element_type=f32)
        return split(jnp.exp(cross - widen(col, n) - lead_sq))

    for a in range(nrows):
        rows = slice(a * block, (a + 1) * block)

        @pl.when(a * row_n + row_at >= PANELS)
        def _():
            col_ref[rows, :] = half_norm_col(r_ref[rows, :])
            kh_ref[rows, :], kl_ref[rows, :] = entries(r_ref[rows, :], col_ref[rows, :])

    for b in range(ncols):
        j = b * col_n + me
        cols = slice(b * block, (b + 1) * block)

        @pl.when(j >= PANELS)
        def _():
            xc = c_ref[cols, :]
            col_sq, col = half_norms(xc)
            col_sq = col_sq - log_row(amp_ref[0], block)
            zh_ref[...], zl_ref[...] = entries(xc, col)
            for s in range(0, n, block):
                e = s + block
                panel = dot_nt(zh_ref[:, :e], zl_ref[:, :e], *inverse(s, e, 0, e))
                ph_ref[:, s:e], pl_ref[:, s:e] = split(panel)
            for s in range(0, n, block):
                e = s + block
                solved = dot_nn(ph_ref[:, s:], pl_ref[:, s:], *inverse(s, n, s, e))
                zh_ref[:, s:e], zl_ref[:, s:e] = split(solved)
            for a in range(nrows):
                i = a * row_n + row_at
                rows = slice(a * block, (a + 1) * block)

                @pl.when(i >= PANELS)
                def _():
                    xr = r_ref[rows, :]
                    cross = lax.dot_general(xr, xc, TRANS_B, preferred_element_type=f32)
                    k = jnp.exp(cross - widen(col_ref[rows, :], block) - col_sq)
                    on_diag = diagonal(block) & (i == j)
                    k = k + jnp.where(on_diag, jnp.broadcast_to(nz_ref[a : a + 1, :], (block, block)), 0.0)
                    k = k - dot_nt(kh_ref[rows, :], kl_ref[rows, :], zh_ref[...], zl_ref[...])
                    store_block(out_ref, a, b, 0, ncols, k)

                @pl.when(i < PANELS)
                def _():
                    store_block(out_ref, a, b, 0, ncols, jnp.zeros((block, block), f32))

        if b:
            continue
        for s in range(PANELS):
            w = s * block
            for a in range(nrows):
                i = a * row_n + row_at
                rows = slice(a * block, (a + 1) * block)

                @pl.when((j == s) & (i >= PANELS))
                def _():
                    e = w + block
                    panel = dot_nt(kh_ref[rows, :e], kl_ref[rows, :e], *inverse(w, e, 0, e))
                    store_block(out_ref, a, b, 0, ncols, panel)

                if a:
                    continue
                for v in range(PANELS):

                    @pl.when((j == s) & (i == v))
                    def _():
                        if v < s:
                            u = jnp.zeros((block, block), f32)
                        else:
                            u = pick(u0_ref, u1_ref, w, w + block, v * block, (v + 1) * block).T
                        if v == s:
                            row_id = lax.broadcasted_iota(jnp.int32, (block, block), 0)
                            col_id = lax.broadcasted_iota(jnp.int32, (block, block), 1)
                            u = jnp.where(row_id >= col_id, u, 0.0)
                        store_block(out_ref, a, b, 0, ncols, u)


SMEM = pl.BlockSpec(memory_space=pltpu.SMEM)
VMEM = pl.BlockSpec(memory_space=pltpu.VMEM)


def exchange(x, axis, k):
    return lax.ppermute(x, axis, [(i, i ^ k) for i in range(lax.axis_size(axis))])


def choose(index, options):
    out = options[0]
    for k in range(1, len(options)):
        out = jnp.where(index == k, options[k], out)
    return out


def local(features, amplitude, noise):
    row_n = lax.axis_size("row")
    col_n = lax.axis_size("col")
    row_at = lax.axis_index("row")
    col_at = lax.axis_index("col")
    nrows, _, piece, width = features.shape
    block = piece * col_n
    ncols = nrows * row_n // col_n
    n = PANELS * block
    mine = features.reshape(nrows, piece, width)
    noise_rows = noise.reshape(nrows, block)
    plane = [mine] + [exchange(mine, "row", k) for k in range(1, row_n)]
    lead = jnp.stack([choose(row_at ^ s, [p[0] for p in plane]) for s in range(PANELS)])
    noise_rows, lead = lax.optimization_barrier((noise_rows, lead))
    near = [lead] + [exchange(lead, "col", k) for k in range(2, col_n, 2)]
    everything, near[1] = lax.optimization_barrier((jnp.stack(plane), near[1]))
    noises = [noise_rows] + [exchange(noise_rows, "row", k) for k in range(1, row_n)]
    lead_noise = jnp.stack([choose(row_at ^ s, [p[0] for p in noises]) for s in range(PANELS)])
    core = col_at & 1

    def parcel(to):
        out = [mine]
        for to_core in (1 - core, core):
            for b in range(ncols):
                number = b * col_n + (to & ~1) + to_core
                at = (row_at ^ (number & (row_n - 1)), number // row_n, 0, 0)
                out.append(lax.dynamic_slice(everything, at, (1, 1, piece, width)).reshape(1, piece, width))
        return jnp.concatenate(out, 0)

    parcels = [parcel(col_at)] + [exchange(parcel(col_at ^ k), "col", k) for k in range(2, col_n, 2)]
    near = jnp.stack(near)
    other = exchange(near, "col", 1)
    at = jnp.stack([row_at, col_at, jnp.int32(row_n), jnp.int32(col_n)])
    first = FIRST * n // NB // 8 * NB
    n1 = n - first
    params = pltpu.CompilerParams(vmem_limit_bytes=GRANT)
    cost = pl.CostEstimate(flops=20_000_000_000, bytes_accessed=8_000_000, transcendentals=0)

    def factor_shapes(rows):
        half = jax.ShapeDtypeStruct((rows, n), bf16)
        return [jax.ShapeDtypeStruct((rows, n), f32), half, half]

    points, lead_sq, u0, wh0, wl0, rest = pl.pallas_call(
        first_kernel,
        out_shape=[jax.ShapeDtypeStruct((n, width), bf16), jax.ShapeDtypeStruct((8, n), f32)]
        + factor_shapes(first)
        + [jax.ShapeDtypeStruct((n1, n), f32)],
        in_specs=[SMEM, SMEM, VMEM, VMEM, VMEM],
        out_specs=[VMEM] * 6,
        scratch_shapes=[pltpu.VMEM((n, n), f32), pltpu.VMEM((n, NB), f32)],
        compiler_params=params,
        cost_estimate=pl.CostEstimate(flops=1_000_000, bytes_accessed=1_000_000, transcendentals=0),
        name="first",
    )(at, amplitude, near, other, lead_noise)
    parcels, rest = lax.optimization_barrier((parcels, rest))
    passed = exchange(jnp.stack([p[: nrows + ncols] for p in parcels]), "col", 1)
    u1, wh1, wl1 = pl.pallas_call(
        second_kernel,
        out_shape=factor_shapes(n1),
        in_specs=[VMEM],
        out_specs=[VMEM] * 3,
        scratch_shapes=[pltpu.VMEM((n1, n), f32)],
        compiler_params=params,
        cost_estimate=cost,
        name="second",
    )(rest)
    half = pltpu.VMEM((block, n), bf16)
    tall = pltpu.VMEM((nrows * block, n), bf16)
    out = pl.pallas_call(
        bulk_kernel,
        out_shape=jax.ShapeDtypeStruct((nrows * block * ncols * (block // NB), NB), f32),
        in_specs=[SMEM, SMEM] + [VMEM] * (10 + len(parcels)),
        out_specs=VMEM,
        scratch_shapes=[
            pltpu.VMEM((nrows * block, width), bf16),
            pltpu.VMEM((ncols * block, width), bf16),
            tall,
            tall,
            half,
            half,
            half,
            half,
            pltpu.VMEM((nrows * block, NB), f32),
        ],
        compiler_params=params,
        cost_estimate=cost,
        name="bulk",
    )(at, amplitude, points, lead_sq, u0, wh0, wl0, u1, wh1, wl1, noise_rows, *parcels, passed)
    return out.reshape(nrows, 1, block, ncols, 1, block)


def solution(mesh):
    return jax.shard_map(
        local,
        mesh=mesh,
        in_specs=(P(None, "row", "col", None), P(), P(None, "row", None)),
        out_specs=P(None, "row", None, None, "col", None),
        check_vma=False,
    )
```

```python
import functools

import jax
import jax.numpy as jnp
from jax import lax
from jax.experimental import pallas as pl
from jax.experimental.pallas import tpu as pltpu
from jax.sharding import PartitionSpec as P

PANELS = 2
NB = 128
WB = 256
GRANT = 30 << 20
UPDATE_ROWS = 256
FIRST = 6
GROUP = 4
f32 = jnp.float32
bf16 = jnp.bfloat16
TRANS_B = (((1,), (1,)), ((), ()))
TRANS_A = (((0,), (0,)), ((), ()))


def split(x):
    hi = x.astype(bf16)
    return hi, (x - hi.astype(f32)).astype(bf16)


def dot_nn(ah, al, bh, bl):
    return jnp.dot(
        jnp.concatenate([ah, ah, al], 1), jnp.concatenate([bh, bl, bh], 0), preferred_element_type=f32
    )


def dot_nt(ah, al, bh, bl):
    return lax.dot_general(
        jnp.concatenate([ah, ah, al], 1), jnp.concatenate([bh, bl, bh], 1), TRANS_B, preferred_element_type=f32
    )


def dot_tn(ah, al, bh, bl):
    return lax.dot_general(
        jnp.concatenate([ah, ah, al], 0), jnp.concatenate([bh, bl, bh], 0), TRANS_A, preferred_element_type=f32
    )


def spread(x):
    return jnp.broadcast_to(x, (8, NB))


def tree_sum(xs):
    while len(xs) > 1:
        xs = [xs[i] + xs[i + 1] if i + 1 < len(xs) else xs[i] for i in range(0, len(xs), 2)]
    return xs[0]


def factor_tile(t, rows, cols, lane, sub):
    scaled, ratio, inverses, pivots = [], {}, [], None
    for j in range(8):
        pivot = spread(cols[j][j : j + 1, :])
        inv = 1.0 / pivot
        inverses.append(inv)
        pivots = pivot if j == 0 else jnp.where(sub == j, pivot, pivots)
        for k in range(j + 1, 8):
            entry = spread(cols[k][j : j + 1, :])
            ratio[j, k] = entry * inv
            cols[k] = cols[k] - ((cols[j] * entry) * inv if k == j + 1 else cols[j] * ratio[j, k])
        row = spread(rows[j : j + 1, :]) * inv
        row = jnp.where(lane == 8 * t + j, 1.0 + inv, row)
        scaled.append(row)
        if j < 7:
            rows = rows - jnp.where(sub > j, cols[j], 0.0) * row
    return rows, lax.rsqrt(pivots), scaled, ratio, inverses


def lane_columns(tile, first):
    return [spread(tile[:, first + k : first + k + 1]) for k in range(8)]


def factor_block(tiles):
    tiles = list(tiles)
    n = len(tiles)
    lane = lax.broadcasted_iota(jnp.int32, (8, NB), 1)
    sub = lax.broadcasted_iota(jnp.int32, (8, NB), 0)
    cols = lane_columns(tiles[0], 0)
    uppers, lowers = [], []
    for g in range(0, n, GROUP):
        end = g + GROUP
        window = min(n, end + 1)
        left, right = [], []
        for t in range(g, end):
            last = t + 1 == window
            if not last:
                near = lane_columns(tiles[t + 1], 8 * t)
                ahead = lane_columns(tiles[t + 1], 8 * t + 8)
            far = {i: lane_columns(tiles[i], 8 * t) for i in range(t + 2, window)}
            rows, root, scaled, ratio, inverses = factor_tile(t, tiles[t], cols, lane, sub)
            if not last:
                for j in range(8):
                    part = near[j] * inverses[j]
                    for k in range(j + 1, 8):
                        near[k] = near[k] - near[j] * ratio[j, k]
                    for k in range(8):
                        ahead[k] = ahead[k] - near[j] * spread(part[k : k + 1, :])
                    tiles[t + 1] = tiles[t + 1] - near[j] * scaled[j]
                cols = ahead
            if far:
                back = list(scaled)
                for j in range(6, -1, -1):
                    for k in range(7, j, -1):
                        back[j] = back[j] - ratio[j, k] * back[k]
                for i in far:
                    tiles[i] = tiles[i] - tree_sum([far[i][j] * back[j] for j in range(8)])
            final = rows * root
            diff = lane - sub - 8 * t
            lower = jnp.where(diff < 0, final, jnp.where(diff == 0, root, 0.0))
            uppers.append(jnp.where(diff >= 0, final, 0.0))
            lowers.append(lower)
            left.append(final)
            right.append(jnp.where(lane >= 8 * end, final, lower))
        if window < n:
            change = dot_tn(*split(jnp.concatenate(left, 0)), *split(jnp.concatenate(right, 0)))
            keep = (lane < 8 * g) | (lane >= 8 * end)
            for i in range(window, n):
                tiles[i] = jnp.where(keep, tiles[i], 0.0) - change[8 * i : 8 * i + 8]
    return jnp.concatenate(uppers, 0), jnp.concatenate(lowers, 0)


def half_norms(x):
    xf = x.astype(f32)
    hi, lo = split(xf * xf)
    ones = jnp.ones((NB, x.shape[1]), bf16)
    row = lax.dot_general(ones[:8], hi, TRANS_B, preferred_element_type=f32)
    row = row + lax.dot_general(ones[:8], lo, TRANS_B, preferred_element_type=f32)
    col = lax.dot_general(hi, ones, TRANS_B, preferred_element_type=f32)
    col = col + lax.dot_general(lo, ones, TRANS_B, preferred_element_type=f32)
    return 0.5 * row[0:1], 0.5 * col


def half_norm_col(x):
    xf = x.astype(f32)
    hi, lo = split(xf * xf)
    ones = jnp.ones((NB, x.shape[1]), bf16)
    col = lax.dot_general(hi, ones, TRANS_B, preferred_element_type=f32)
    return 0.5 * (col + lax.dot_general(lo, ones, TRANS_B, preferred_element_type=f32))


def widen(col, width):
    return jnp.concatenate([col] * (width // NB), 1)


def log_row(amp, width):
    return jnp.log(jnp.full((1, width), amp, f32))


def diagonal(n):
    return lax.broadcasted_iota(jnp.int32, (n, n), 0) == lax.broadcasted_iota(jnp.int32, (n, n), 1)


def place(x_ref, base, piece_at, piece, value):
    at = pl.multiple_of(base + piece_at * piece, piece)
    x_ref[pl.ds(at, piece), :] = value


def factor_panels(a_ref, u_ref, wh_ref, wl_ref, row0, count, block):
    n = a_ref.shape[1]
    for p in range(count):
        rows = slice(p * NB, (p + 1) * NB)
        s = row0 + p * NB
        e = s + NB
        d = a_ref[rows, s:e]
        upper, lower = factor_block([d[8 * t : 8 * t + 8] for t in range(NB // 8)])
        u_ref[rows, s:e] = upper
        ih, il = split(lower)
        parts = ([a_ref[rows, :s]] if s else []) + ([a_ref[rows, e:]] if e < n else [])
        row = dot_nn(ih, il, *split(jnp.concatenate(parts, 1)))
        hi, lo = split(row)
        for w_ref, w, diag in ((wh_ref, hi, ih), (wl_ref, lo, il)):
            if s:
                w_ref[rows, :s] = w[:, :s]
            w_ref[rows, s:e] = diag
            end = (s // block + 1) * block
            if e < end:
                w_ref[rows, e:end] = jnp.zeros((NB, end - e), bf16)
        if e == n:
            break
        u_ref[rows, e:] = row[:, s:]
        done_h = jnp.concatenate(([hi[:, :s]] if s else []) + [ih], 1)
        done_l = jnp.concatenate(([lo[:, :s]] if s else []) + [il], 1)
        for i in range(0, n - e, UPDATE_ROWS):
            f = min(i + UPDATE_ROWS, n - e)
            change = dot_tn(
                hi[:, s + i : s + f],
                lo[:, s + i : s + f],
                jnp.concatenate([done_h, hi[:, s + i :]], 1),
                jnp.concatenate([done_l, lo[:, s + i :]], 1),
            )
            q = slice((p + 1) * NB + i, (p + 1) * NB + f)
            if s:
                a_ref[q, :s] = a_ref[q, :s] - change[:, :s]
            a_ref[q, s:e] = -change[:, s:e]
            a_ref[q, e + i :] = a_ref[q, e + i :] - change[:, e:]


def first_kernel(at_ref, amp_ref, mine_ref, other_ref, nz_ref, *refs):
    x_ref, sq_ref, u_ref, wh_ref, wl_ref, rest_ref, a_ref, col_ref = refs
    n = a_ref.shape[0]
    steps, panels, piece = mine_ref.shape[:3]
    block = n // panels
    me = at_ref[1]
    for m in range(steps):
        for s in range(panels):
            place(x_ref, s * block, me ^ (2 * m), piece, mine_ref[m, s])
            place(x_ref, s * block, me ^ (2 * m + 1), piece, other_ref[m, s])
    sq_row, col_ref[...] = half_norms(x_ref[...])
    sq_row = sq_row - log_row(amp_ref[0], n)
    sq_ref[...] = jnp.broadcast_to(sq_row, sq_ref.shape)
    noise = nz_ref[...]
    for o in range(0, n, WB):
        cross = lax.dot_general(x_ref[o : o + WB, :], x_ref[o:, :], TRANS_B, preferred_element_type=f32)
        k = jnp.exp(cross - widen(col_ref[o : o + WB, :], n - o) - sq_row[:, o:])
        a_ref[o : o + WB, o:] = k
        row = noise[o // block : o // block + 1, o % block : o % block + WB]
        a_ref[o : o + WB, o : o + WB] = k[:, :WB] + jnp.where(diagonal(WB), jnp.broadcast_to(row, (WB, WB)), 0.0)
    count = u_ref.shape[0] // NB
    factor_panels(a_ref, u_ref, wh_ref, wl_ref, 0, count, block)
    rest_ref[...] = a_ref[count * NB :, :]


def second_kernel(rest_ref, u_ref, wh_ref, wl_ref, a_ref):
    n1, n = rest_ref.shape
    a_ref[...] = rest_ref[...]
    factor_panels(a_ref, u_ref, wh_ref, wl_ref, n - n1, n1 // NB, n // PANELS)


def store_block(out_ref, a, b, row, ncols, value):
    rows, block = value.shape
    per = block // NB
    for q in range(per):
        at = ((a * block + row) * ncols + b) * per + q
        out_ref[pl.ds(at, rows, stride=ncols * per), :] = value[:, q * NB : (q + 1) * NB]


def bulk_kernel(at_ref, amp_ref, *refs):
    x_ref, sq_ref, u0_ref, wh0_ref, wl0_ref, u1_ref, wh1_ref, wl1_ref, nz_ref = refs[:9]
    refs = refs[9:]
    count = len(refs) - 11
    near_refs, other_ref, out_ref = refs[:count], refs[count], refs[count + 1]
    r_ref, c_ref, kh_ref, kl_ref, ph_ref, pl_ref, zh_ref, zl_ref, col_ref = refs[count + 2 :]
    n = x_ref.shape[0]
    split_at = u0_ref.shape[0]
    nrows, block = nz_ref.shape
    piece = other_ref.shape[2]
    ncols = c_ref.shape[0] // block
    row_at, me, row_n, col_n = at_ref[0], at_ref[1], at_ref[2], at_ref[3]
    for m in range(count):
        for a in range(nrows):
            place(r_ref, a * block, me ^ (2 * m), piece, near_refs[m][a])
            place(r_ref, a * block, me ^ (2 * m + 1), piece, other_ref[m, a])
        for b in range(ncols):
            place(c_ref, b * block, me ^ (2 * m), piece, near_refs[m][nrows + ncols + b])
            place(c_ref, b * block, me ^ (2 * m + 1), piece, other_ref[m, nrows + b])

    def pick(first_ref, second_ref, r0, r1, c0, c1):
        parts = []
        if r0 < split_at:
            parts.append(first_ref[r0 : min(r1, split_at), c0:c1])
        if r1 > split_at:
            parts.append(second_ref[max(r0, split_at) - split_at : r1 - split_at, c0:c1])
        return jnp.concatenate(parts, 0) if len(parts) > 1 else parts[0]

    def inverse(r0, r1, c0, c1):
        return pick(wh0_ref, wh1_ref, r0, r1, c0, c1), pick(wl0_ref, wl1_ref, r0, r1, c0, c1)

    lead_sq = sq_ref[0:1, :]

    def entries(x, col):
        cross = lax.dot_general(x, x_ref[...], TRANS_B, preferred_element_type=f32)
        return split(jnp.exp(cross - widen(col, n) - lead_sq))

    for a in range(nrows):
        rows = slice(a * block, (a + 1) * block)

        @pl.when(a * row_n + row_at >= PANELS)
        def _():
            col_ref[rows, :] = half_norm_col(r_ref[rows, :])
            kh_ref[rows, :], kl_ref[rows, :] = entries(r_ref[rows, :], col_ref[rows, :])

    for b in range(ncols):
        j = b * col_n + me
        cols = slice(b * block, (b + 1) * block)

        @pl.when(j >= PANELS)
        def _():
            xc = c_ref[cols, :]
            col_sq, col = half_norms(xc)
            col_sq = col_sq - log_row(amp_ref[0], block)
            zh_ref[...], zl_ref[...] = entries(xc, col)
            for s in range(0, n, block):
                e = s + block
                panel = dot_nt(zh_ref[:, :e], zl_ref[:, :e], *inverse(s, e, 0, e))
                ph_ref[:, s:e], pl_ref[:, s:e] = split(panel)
            for s in range(0, n, block):
                e = s + block
                solved = dot_nn(ph_ref[:, s:], pl_ref[:, s:], *inverse(s, n, s, e))
                zh_ref[:, s:e], zl_ref[:, s:e] = split(solved)
            for a in range(nrows):
                i = a * row_n + row_at
                rows = slice(a * block, (a + 1) * block)

                @pl.when(i >= PANELS)
                def _():
                    xr = r_ref[rows, :]
                    cross = lax.dot_general(xr, xc, TRANS_B, preferred_element_type=f32)
                    k = jnp.exp(cross - widen(col_ref[rows, :], block) - col_sq)
                    on_diag = diagonal(block) & (i == j)
                    k = k + jnp.where(on_diag, jnp.broadcast_to(nz_ref[a : a + 1, :], (block, block)), 0.0)
                    k = k - dot_nt(kh_ref[rows, :], kl_ref[rows, :], zh_ref[...], zl_ref[...])
                    store_block(out_ref, a, b, 0, ncols, k)

                @pl.when(i < PANELS)
                def _():
                    store_block(out_ref, a, b, 0, ncols, jnp.zeros((block, block), f32))

        if b:
            continue
        for s in range(PANELS):
            w = s * block
            e = w + block

            @pl.when(j == s)
            def _():
                def some_rows(step, carry):
                    o = pl.multiple_of(step * WB, WB)
                    rows = pl.ds(o, WB)
                    panel = dot_nt(kh_ref[rows, :e], kl_ref[rows, :e], *inverse(w, e, 0, e))
                    store_block(out_ref, 0, b, o, ncols, panel)
                    return carry

                start = jnp.where(row_at < PANELS, block // WB, 0)
                lax.fori_loop(start, nrows * block // WB, some_rows, 0)

            for v in range(PANELS):

                @pl.when((j == s) & (row_at == v))
                def _():
                    if v < s:
                        u = jnp.zeros((block, block), f32)
                    else:
                        u = pick(u0_ref, u1_ref, w, e, v * block, (v + 1) * block).T
                    if v == s:
                        row_id = lax.broadcasted_iota(jnp.int32, (block, block), 0)
                        col_id = lax.broadcasted_iota(jnp.int32, (block, block), 1)
                        u = jnp.where(row_id >= col_id, u, 0.0)
                    store_block(out_ref, 0, b, 0, ncols, u)


SMEM = pl.BlockSpec(memory_space=pltpu.SMEM)
VMEM = pl.BlockSpec(memory_space=pltpu.VMEM)


def exchange(x, axis, k):
    return lax.ppermute(x, axis, [(i, i ^ k) for i in range(lax.axis_size(axis))])


def choose(index, options):
    out = options[0]
    for k in range(1, len(options)):
        out = jnp.where(index == k, options[k], out)
    return out


def local(features, amplitude, noise):
    row_n = lax.axis_size("row")
    col_n = lax.axis_size("col")
    row_at = lax.axis_index("row")
    col_at = lax.axis_index("col")
    nrows, _, piece, width = features.shape
    block = piece * col_n
    ncols = nrows * row_n // col_n
    n = PANELS * block
    mine = features.reshape(nrows, piece, width)
    noise_rows = noise.reshape(nrows, block)
    plane = [mine] + [exchange(mine, "row", k) for k in range(1, row_n)]
    lead = jnp.stack([choose(row_at ^ s, [p[0] for p in plane]) for s in range(PANELS)])
    noise_rows, lead = lax.optimization_barrier((noise_rows, lead))
    near = [lead] + [exchange(lead, "col", k) for k in range(2, col_n, 2)]
    everything, near[1] = lax.optimization_barrier((jnp.stack(plane), near[1]))
    noises = [noise_rows] + [exchange(noise_rows, "row", k) for k in range(1, row_n)]
    lead_noise = jnp.stack([choose(row_at ^ s, [p[0] for p in noises]) for s in range(PANELS)])
    core = col_at & 1

    def parcel(to):
        out = [mine]
        for to_core in (1 - core, core):
            for b in range(ncols):
                number = b * col_n + (to & ~1) + to_core
                at = (row_at ^ (number & (row_n - 1)), number // row_n, 0, 0)
                out.append(lax.dynamic_slice(everything, at, (1, 1, piece, width)).reshape(1, piece, width))
        return jnp.concatenate(out, 0)

    parcels = [parcel(col_at)] + [exchange(parcel(col_at ^ k), "col", k) for k in range(2, col_n, 2)]
    near = jnp.stack(near)
    other = exchange(near, "col", 1)
    at = jnp.stack([row_at, col_at, jnp.int32(row_n), jnp.int32(col_n)])
    first = FIRST * n // NB // 8 * NB
    n1 = n - first
    params = pltpu.CompilerParams(vmem_limit_bytes=GRANT)
    cost = pl.CostEstimate(flops=20_000_000_000, bytes_accessed=8_000_000, transcendentals=0)

    def factor_shapes(rows):
        half = jax.ShapeDtypeStruct((rows, n), bf16)
        return [jax.ShapeDtypeStruct((rows, n), f32), half, half]

    points, lead_sq, u0, wh0, wl0, rest = pl.pallas_call(
        first_kernel,
        out_shape=[jax.ShapeDtypeStruct((n, width), bf16), jax.ShapeDtypeStruct((8, n), f32)]
        + factor_shapes(first)
        + [jax.ShapeDtypeStruct((n1, n), f32)],
        in_specs=[SMEM, SMEM, VMEM, VMEM, VMEM],
        out_specs=[VMEM] * 6,
        scratch_shapes=[pltpu.VMEM((n, n), f32), pltpu.VMEM((n, NB), f32)],
        compiler_params=params,
        cost_estimate=pl.CostEstimate(flops=1_000_000, bytes_accessed=1_000_000, transcendentals=0),
        name="first",
    )(at, amplitude, near, other, lead_noise)
    parcels, rest = lax.optimization_barrier((parcels, rest))
    passed = exchange(jnp.stack([p[: nrows + ncols] for p in parcels]), "col", 1)
    u1, wh1, wl1 = pl.pallas_call(
        second_kernel,
        out_shape=factor_shapes(n1),
        in_specs=[VMEM],
        out_specs=[VMEM] * 3,
        scratch_shapes=[pltpu.VMEM((n1, n), f32)],
        compiler_params=params,
        cost_estimate=cost,
        name="second",
    )(rest)
    half = pltpu.VMEM((block, n), bf16)
    tall = pltpu.VMEM((nrows * block, n), bf16)
    out = pl.pallas_call(
        bulk_kernel,
        out_shape=jax.ShapeDtypeStruct((nrows * block * ncols * (block // NB), NB), f32),
        in_specs=[SMEM, SMEM] + [VMEM] * (10 + len(parcels)),
        out_specs=VMEM,
        scratch_shapes=[
            pltpu.VMEM((nrows * block, width), bf16),
            pltpu.VMEM((ncols * block, width), bf16),
            tall,
            tall,
            half,
            half,
            half,
            half,
            pltpu.VMEM((nrows * block, NB), f32),
        ],
        compiler_params=params,
        cost_estimate=cost,
        name="bulk",
    )(at, amplitude, points, lead_sq, u0, wh0, wl0, u1, wh1, wl1, noise_rows, *parcels, passed)
    return out.reshape(nrows, 1, block, ncols, 1, block)


def solution(mesh):
    return jax.shard_map(
        local,
        mesh=mesh,
        in_specs=(P(None, "row", "col", None), P(), P(None, "row", None)),
        out_specs=P(None, "row", None, None, "col", None),
        check_vma=False,
    )
```
